32 devices in a mesh: batch: 8 (over z, core), seq: 4 (over y, x).
Axes of the slice: x: 2, y: 2, z: 4, core: 2. Of those that a mesh axis runs over, the one named last changes fastest.
Arguments:
- tokens: bfloat16 [8, 1024, 1024], P('batch', 'seq'), may hold values from -6 to 6
- teacher: bfloat16 [8, 1024, 1024], P('batch', 'seq'), may hold values from -6 to 6
- piece_starts: int32 [8, 1024], P('batch', 'seq'), may hold values from 0 to 1, as said below
- valid_rows: int32 [8, 1024], P('batch', 'seq'), may hold values 0 or 1
- norm_gain: bfloat16 [1024], P(('batch', 'seq')), may hold values from 0.5 to 1.5
- in_weight: bfloat16 [1024, 4096], P(('batch', 'seq')), may hold values from -0.1875 to 0.1875
- conv_weight: bfloat16 [4, 2048], P(None, ('batch', 'seq')), may hold values from -3 to 3
- conv_bias: bfloat16 [2048], P(('batch', 'seq')), may hold values from -3 to 3
- xproj_weight: bfloat16 [2048, 96], P(('batch', 'seq')), may hold values from -0.125 to 0.125
- dtproj_weight: bfloat16 [64, 2048], P(None, ('batch', 'seq')), may hold values from -0.75 to 0.75
- dt_bias: bfloat16 [2048], P(('batch', 'seq')), may hold values from -7 to -1
- a_log: bfloat16 [2048, 16], P(('batch', 'seq')), may hold values from -3 to 1.5
- skip_weight: bfloat16 [2048], P(('batch', 'seq')), may hold values from 0.5 to 1.5
- out_weight: bfloat16 [2048, 1024], P(('batch', 'seq')), may hold values from -0.25 to 0.25
Outputs:
- output: bfloat16 [8, 1024, 1024], P('batch', 'seq')
- loss: float32 [], replicated
- input_grad: float32 [8, 1024, 1024], P('batch', 'seq')
- norm_gain_grad: float32 [1024], P(('batch', 'seq'))
- in_weight_grad: float32 [1024, 4096], P(('batch', 'seq'))
- conv_weight_grad: float32 [4, 2048], P(None, ('batch', 'seq'))
- conv_bias_grad: float32 [2048], P(('batch', 'seq'))
- xproj_weight_grad: float32 [2048, 96], P(('batch', 'seq'))
- dtproj_weight_grad: float32 [64, 2048], P(None, ('batch', 'seq'))
- dt_bias_grad: float32 [2048], P(('batch', 'seq'))
- a_log_grad: float32 [2048, 16], P(('batch', 'seq'))
- skip_weight_grad: float32 [2048], P(('batch', 'seq'))
- out_weight_grad: float32 [2048, 1024], P(('batch', 'seq'))
The draws below stay inside these ranges and needn't reach their ends.
Inputs may be any that keep to these rules, and one draw needn't show every extreme that they name: `piece_starts`: each 1 starts a piece of 256 positions that ends within its sequence; pieces of one sequence do not intersect.
All inputs are finite; a program needn't handle non-finite values. No bound on the sum of `valid_rows` on one device may be relied on, other than what follows from the above.
Results may differ from the reference program's by a relative error of at most 0.0075.
Values may be sent and summed in bfloat16 or wider, within the bound.
No kernel may reach another device: no remote copies, remote signals or barrier semaphores. Data moves between devices by JAX's collectives and lax.ppermute only.
A program may use at most 192 MiB of HBM per device.

```python
import jax
import jax.numpy as jnp
from jax import lax

D = 1024
E = 2048
R = 64
N = 16
K = 4
PIECE = 256
LENGTH = 1024
SEQUENCES = 8
TOKENS = 8192


def draw_piece_starts(key, part):
    slot_len = 2 * PIECE
    slot_count = LENGTH // slot_len
    offsets = jax.random.randint(key, (SEQUENCES, slot_count), 1, PIECE + 1).astype(jnp.int32)
    moved = (jnp.arange(SEQUENCES, dtype=jnp.int32) % 2 * PIECE).astype(jnp.int32)
    places = jnp.arange(LENGTH, dtype=jnp.int32)
    shifted = places[None, :] - moved[:, None]
    slot_index = jnp.clip(shifted // slot_len, 0, slot_count - 1).astype(jnp.int32)
    within = shifted - slot_index * slot_len
    chosen = jnp.take_along_axis(offsets, slot_index, axis=1)
    usable = slot_count - (moved > 0).astype(jnp.int32)
    marked = (shifted >= 0) & (within == chosen) & (slot_index < usable[:, None])
    return marked.astype(jnp.int32)


def with_ends(entries, rng, least, top_value):
    place = [jax.random.randint(jax.random.fold_in(rng, axis), (), 0, length) for axis, length in enumerate(entries.shape)]
    main_axis = entries.shape.index(max(entries.shape))
    next_to = place[:main_axis] + [(place[main_axis] + 1) % entries.shape[main_axis]] + place[main_axis + 1:]
    return entries.at[tuple(place)].set(least).at[tuple(next_to)].set(top_value)


def level_of(key, extent, shards, low, top_value):
    gain = 1.0
    for position, blocks in shards:
        draws = jax.random.uniform(jax.random.fold_in(jax.random.fold_in(key, 6), position), (blocks,), jnp.float32, low / len(shards), top_value / len(shards))
        gain = gain * jnp.repeat(jnp.exp(draws), extent[position] // blocks).reshape((-1,) + (1,) * (len(extent) - 1 - position))
    return gain


def noise(key, dims, spread, bound, cuts=(), kind=jnp.bfloat16):
    factor_of = level_of(key, dims, cuts, -0.22, 0.18) if cuts else 1.0
    result = jax.random.normal(key, dims, jnp.float32) * spread * factor_of
    return jnp.minimum(jnp.maximum(result, -bound), bound).astype(kind)


def setup_inputs(seed: int = 0) -> dict:
    splits = jax.random.split(jax.random.key(seed), 15)
    return {
        "tokens": noise(splits[0], (SEQUENCES, LENGTH, D), 1.0, 6.0, ((0, 8), (1, 4))),
        "teacher": noise(splits[1], (SEQUENCES, LENGTH, D), 1.0, 6.0, ((0, 8), (1, 4))),
        "piece_starts": draw_piece_starts(jax.random.fold_in(splits[14], 71), 0),
        "valid_rows": with_ends((jax.random.randint(splits[3], (SEQUENCES, LENGTH), 0, 8) < 7).astype(jnp.int32), jax.random.fold_in(splits[3], 1), 0, 1),
        "norm_gain": jnp.clip(1.0 + 0.1 * jax.random.normal(splits[4], (D,), jnp.float32), 0.5, 1.5).astype(jnp.bfloat16),
        "in_weight": noise(splits[5], (D, 2 * E), D ** -0.5, 0.1875, ((0, 32),)),
        "conv_weight": noise(splits[6], (K, E), K ** -0.5, 3.0, ((1, 32),)),
        "conv_bias": noise(splits[7], (E,), 0.5, 3.0, ((0, 32),)),
        "xproj_weight": noise(splits[8], (E, R + 2 * N), E ** -0.5, 0.125, ((0, 32),)),
        "dtproj_weight": noise(splits[9], (R, E), R ** -0.5, 0.75, ((1, 32),)),
        "dt_bias": jnp.clip(-7.0 + 6.0 * jax.random.uniform(splits[10], (E,), jnp.float32) ** level_of(splits[10], (E,), ((0, 32),), -0.2, 0.2), -7.0, -1.0).astype(jnp.bfloat16),
        "a_log": jnp.clip(-3.0 + 4.5 * jax.random.uniform(splits[11], (E, N), jnp.float32) ** level_of(splits[11], (E, N), ((0, 32),), -0.2, 0.2), -3.0, 1.5).astype(jnp.bfloat16),
        "skip_weight": jnp.clip(0.5 + 1.0 * jax.random.uniform(splits[12], (E,), jnp.float32) ** level_of(splits[12], (E,), ((0, 32),), -0.2, 0.2), 0.5, 1.5).astype(jnp.bfloat16),
        "out_weight": noise(splits[13], (E, D), (E // 4) ** -0.5, 0.25, ((0, 32),)),
    }


@jax.custom_vjp
def low(v):
    return lax.optimization_barrier(v.astype(jnp.bfloat16)).astype(jnp.float32)

@jax.custom_vjp
def low_back(v):
    return v

def low_keep(v):
    return (low(v), None)

def low_pass(kept, grad):
    return (grad,)

def back_keep(v):
    return (v, None)

def back_low(kept, grad):
    return (low(grad),)
low.defvjp(low_keep, low_pass)
low_back.defvjp(back_keep, back_low)

def matmul(left, right):
    return jnp.dot(left, right, precision=lax.Precision.HIGHEST, preferred_element_type=jnp.float32)

def swish_fn(values):
    return values * jax.nn.sigmoid(values)

def one_sequence(params, tokens_f, starts, valid_f, teacher_f):
    norm_gain, in_weight, conv_weight, conv_bias, xproj_weight, dtproj_weight, dt_bias, a_log, skip_weight, out_weight = params
    mean_sq = lax.optimization_barrier(jnp.mean(tokens_f * tokens_f, axis=-1, keepdims=True))
    unit_rows = tokens_f * lax.rsqrt(mean_sq + 1e-05)
    normed = low(unit_rows * norm_gain)
    joint_proj = low_back(matmul(normed, in_weight))
    stream = low(joint_proj[:, :E])
    gate_pre = joint_proj[:, E:]
    widened = jnp.pad(stream, ((K - 1, 0), (0, 0)))
    conv_pre = conv_bias + jnp.zeros((LENGTH, E), jnp.float32)
    for kernel_tap in range(K):
        conv_pre = conv_pre + conv_weight[kernel_tap] * widened[kernel_tap:kernel_tap + LENGTH]
    activated = low(swish_fn(conv_pre))
    projected = low_back(matmul(activated, xproj_weight))
    low_rank = low(projected[:, :R])
    into_state = projected[:, R:R + N]
    read_state = projected[:, R + N:]
    step_size = jax.nn.softplus(low_back(matmul(low_rank, dtproj_weight)) + dt_bias)
    decay_rates = -jnp.exp(a_log)
    start_flags = starts.astype(jnp.float32)
    cumulative = jnp.cumsum(starts).astype(jnp.int32)
    lagged = jnp.concatenate([jnp.zeros((PIECE,), jnp.int32), cumulative[:LENGTH - PIECE]])
    inside = (cumulative - lagged > 0).astype(jnp.float32)
    carry_on = inside * (1.0 - start_flags)
    step_next = jnp.concatenate([step_size[1:], jnp.zeros((1, E), jnp.float32)], axis=0)
    carry_next = jnp.concatenate([carry_on[1:], jnp.zeros((1,), jnp.float32)])
    zero_state = jnp.zeros((E, N), jnp.float32)

    def ahead_step(current, row_data):
        step_t, act_t, into_t, read_t = row_data
        current = jnp.exp(step_t[:, None] * decay_rates) * current + (step_t * act_t)[:, None] * into_t[None, :]
        return (current, lax.optimization_barrier(jnp.sum(current * read_t[None, :], axis=1)))
    _, ahead_out = lax.scan(ahead_step, zero_state, (step_size, activated, into_state, read_state))

    def behind_step(current, row_data):
        step_t, act_t, into_t, read_t, next_t, flag_t = row_data
        fresh_in = (step_t * act_t)[:, None] * into_t[None, :]
        current = fresh_in + flag_t * jnp.exp(next_t[:, None] * decay_rates) * current
        return (current, lax.optimization_barrier(jnp.sum((current - fresh_in) * read_t[None, :], axis=1)))
    _, behind_out = lax.scan(behind_step, zero_state, (step_size, activated, into_state, read_state, step_next, carry_next), reverse=True)
    mixed = ahead_out + inside[:, None] * behind_out + skip_weight * activated
    gated = low(mixed * swish_fn(gate_pre))
    branch = low_back(matmul(gated, out_weight))
    result_f = tokens_f + branch
    misfit = result_f - teacher_f
    square_sum = jnp.sum(valid_f[:, None] * misfit * misfit)
    return (result_f, square_sum)

def reference(tokens, teacher, piece_starts, valid_rows, norm_gain, in_weight, conv_weight, conv_bias, xproj_weight, dtproj_weight, dt_bias, a_log, skip_weight, out_weight):
    tokens_f = tokens.astype(jnp.float32)
    teacher_f = teacher.astype(jnp.float32)
    valid_f = valid_rows.astype(jnp.float32)
    params = tuple((weight.astype(jnp.float32) for weight in (norm_gain, in_weight, conv_weight, conv_bias, xproj_weight, dtproj_weight, dt_bias, a_log, skip_weight, out_weight)))
    counted = jnp.sum(valid_f)
    checked = jax.checkpoint(one_sequence)

    def whole_block(inputs, weights):

        def per_sequence(total_sq, seq_item):
            tok_seq, start_seq, valid_seq, teach_seq = seq_item
            result_f, square_sum = checked(weights, tok_seq, start_seq, valid_seq, teach_seq)
            return (total_sq + square_sum, result_f)
        total_sq, results = lax.scan(per_sequence, jnp.zeros((), jnp.float32), (inputs, piece_starts, valid_f, teacher_f))
        return ((results, total_sq * (TOKENS / counted)), total_sq)
    (results, scaled), pullback, total_sq = jax.vjp(whole_block, tokens_f, params, has_aux=True)
    cotangent = (jnp.zeros_like(results), jnp.ones_like(scaled))
    input_grad, weight_grads = pullback(cotangent)
    gain_grad, input_projection_gradient, conv_grad, convb_grad, xproj_grad, dtproj_grad, dtbias_grad, alog_grad, skip_grad, output_projection_gradient = weight_grads
    loss = total_sq / (counted * D)
    return (results.astype(jnp.bfloat16), loss, input_grad, gain_grad, input_projection_gradient, conv_grad, convb_grad, xproj_grad, dtproj_grad, dtbias_grad, alog_grad, skip_grad, output_projection_gradient)
```

```python
import jax
import jax.numpy as jnp
from jax import lax
from jax.experimental import pallas as pl
from jax.experimental.pallas import tpu as pltpu
from jax.sharding import PartitionSpec as P

PIECE = 256
BLOCK = 16
ROWS = 128
LOG2E = 1.4426950408889634
LN2 = 0.6931471805599453
NEVER = 1e9
f32 = jnp.float32
bf16 = jnp.bfloat16


def _row(ref, t, n):
    return jnp.broadcast_to(ref[pl.ds(t, 1), :], (n, ref.shape[1]))

def _col(blk, tt, c):
    return jnp.broadcast_to(blk[:, tt:tt+1], (blk.shape[0], c))

def _nt(a, b):
    return lax.dot_general(a, b, (((1,), (1,)), ((), ())), preferred_element_type=f32)

def piece_back_kernel(stepm_ref, u_ref, b3_ref, r2_ref, g_ref, carry_ref):
    rows, c = u_ref.shape
    n = r2_ref.shape[0]
    @pl.when(pl.program_id(0) == 0)
    def _(): carry_ref[...] = jnp.zeros_like(carry_ref)
    r2 = r2_ref[...]
    def block(i, carry):
        j = rows // BLOCK - 1 - i
        bblk = b3_ref[j]
        for tt in reversed(range(BLOCK)):
            t = j * BLOCK + tt
            g = _row(u_ref, t, n) * _col(bblk, tt, c) + carry
            g_ref[pl.ds(pl.multiple_of(t * n, n), n), :] = g.astype(bf16)
            carry = jnp.exp2(_row(stepm_ref, t, n) * r2) * g
        return carry
    carry_ref[...] = lax.fori_loop(0, rows // BLOCK, block, carry_ref[...])

def ahead_kernel(step_ref, u_ref, b3_ref, cblk_ref, r2_ref, g_ref, y_ref, hp_ref, carry_ref, s_ref):
    rows, c = u_ref.shape
    n = r2_ref.shape[0]
    @pl.when(pl.program_id(0) == 0)
    def _(): carry_ref[...] = jnp.zeros_like(carry_ref)
    r2 = r2_ref[...]
    def block(j, h):
        bblk = b3_ref[j]
        for tt in range(BLOCK):
            t = j * BLOCK + tt
            at = pl.ds(pl.multiple_of(t * n, n), n)
            hp = jnp.exp2(_row(step_ref, t, n) * r2) * h
            h = hp + _row(u_ref, t, n) * _col(bblk, tt, c)
            hpb = hp.astype(bf16)
            hp_ref[at, :] = hpb
            s_ref[tt * n:(tt + 1) * n, :] = (hp + g_ref[at, :].astype(f32)).astype(bf16)
        rows16 = pl.ds(pl.multiple_of(j * BLOCK, BLOCK), BLOCK)
        y_ref[rows16, :] = jnp.dot(cblk_ref[rows16, :], s_ref[...], preferred_element_type=f32)
        return h
    carry_ref[...] = lax.fori_loop(0, rows // BLOCK, block, carry_ref[...])

def piece_grad_kernel(stepm_ref, dm_ref, c3_ref, r2_ref, q_ref, carry_ref):
    rows, c = dm_ref.shape
    n = r2_ref.shape[0]
    @pl.when(pl.program_id(0) == 0)
    def _(): carry_ref[...] = jnp.zeros_like(carry_ref)
    r2 = r2_ref[...]
    def block(j, w):
        cblk = c3_ref[j]
        for tt in range(BLOCK):
            t = j * BLOCK + tt
            q = jnp.exp2(_row(stepm_ref, t, n) * r2) * w
            q_ref[pl.ds(pl.multiple_of(t * n, n), n), :] = q.astype(bf16)
            w = q + _row(dm_ref, t, n) * _col(cblk, tt, c)
        return w
    carry_ref[...] = lax.fori_loop(0, rows // BLOCK, block, carry_ref[...])

def state_grad_kernel(step_ref, u_ref, dm_ref, c3_ref, bblk_ref, oblk_ref, nblk_ref, r2_ref, g_ref, hp_ref, q_ref,
               x_ref, y_ref, db_ref, dc_ref, al_ref, carry_ref, ig_ref, rr_ref, rs_ref, s_ref, sb_ref):
    rows, c = u_ref.shape
    n = r2_ref.shape[0]
    @pl.when(pl.program_id(0) == 0)
    def _():
        carry_ref[...] = jnp.zeros_like(carry_ref)
        al_ref[...] = jnp.zeros_like(al_ref)
    r2 = r2_ref[...]
    sb_ref[...] = step_ref[...]
    def block(i, m):
        j = rows // BLOCK - 1 - i
        cblk = c3_ref[j]
        for tt in reversed(range(BLOCK)):
            t = j * BLOCK + tt
            at = pl.ds(pl.multiple_of(t * n, n), n)
            loc = slice(tt * n, (tt + 1) * n)
            mu = m + _row(dm_ref, t, n) * _col(cblk, tt, c)
            srow = _row(step_ref, t, n)
            m = jnp.exp2(srow * r2) * mu
            mub = mu.astype(bf16)
            q = q_ref[at, :]
            g = g_ref[at, :]
            hp = hp_ref[at, :]
            rg = mub * hp + q * g
            ig_ref[loc, :] = mub + q
            rr_ref[loc, :] = (rg.astype(f32) * r2).astype(bf16)
            rs_ref[loc, :] = rg * srow.astype(bf16)
            s_ref[loc, :] = hp + g
        r16 = pl.ds(pl.multiple_of(j * BLOCK, BLOCK), BLOCK)
        ig = ig_ref[...]
        x_ref[r16, :] = jnp.dot(bblk_ref[r16, :], ig, preferred_element_type=f32)
        y_ref[r16, :] = jnp.dot(oblk_ref[...], rr_ref[...], preferred_element_type=f32)
        al_ref[...] += jnp.dot(nblk_ref[...], rs_ref[...], preferred_element_type=f32)
        db_ref[r16, :] = _nt(u_ref[r16, :].astype(bf16), ig)
        dc_ref[r16, :] = _nt(dm_ref[r16, :].astype(bf16), s_ref[...])
        return m
    carry_ref[...] = lax.fori_loop(0, rows // BLOCK, block, carry_ref[...])

def blocks_of(v):
    t, n = v.shape
    return v.reshape(t // BLOCK, BLOCK, n).transpose(0, 2, 1)

def block_diag(v):
    t, n = v.shape
    wide = jnp.tile(v, (1, BLOCK))
    keep = (jnp.arange(t)[:, None] % BLOCK) == (jnp.arange(BLOCK * n)[None, :] // n)
    return jnp.where(keep, wide, 0.0).astype(bf16)

def call(kernel, rows, total, reverse, ins, in_kinds, outs, out_kinds, scratch):
    steps = total // rows
    where = (lambda i: steps - 1 - i) if reverse else (lambda i: i)
    def spec(shape, kind):
        if kind == "full":
            return pl.BlockSpec(shape, lambda i: (0,) * len(shape))
        per = shape[0] // steps
        return pl.BlockSpec((per,) + shape[1:], lambda i: (where(i),) + (0,) * (len(shape) - 1))
    return pl.pallas_call(kernel,
        out_shape=[jax.ShapeDtypeStruct(s, d) for s, d in outs],
        grid=(steps,),
        in_specs=[spec(a.shape, k) for a, k in zip(ins, in_kinds)],
        out_specs=[spec(s, k) for (s, d), k in zip(outs, out_kinds)],
        scratch_shapes=scratch,
        compiler_params=pltpu.CompilerParams(dimension_semantics=("arbitrary",), vmem_limit_bytes=60<<20),
    )(*ins)

def run_g(stepm,u,b3,r2):
    t,c=u.shape; n=r2.shape[0]
    return call(piece_back_kernel, ROWS, t, True, [stepm,u,b3,r2], ["t","t","t","full"], [((t*n,c),bf16)], ["t"], [pltpu.VMEM((n,c),f32)])[0]
def run_h(step,u,b3,cblk,r2,g):
    t,c=u.shape; n=r2.shape[0]
    return call(ahead_kernel, ROWS, t, False, [step,u,b3,cblk,r2,g], ["t","t","t","t","full","t"], [((t,c),f32),((t*n,c),bf16)], ["t","t"], [pltpu.VMEM((n,c),f32),pltpu.VMEM((BLOCK*n,c),bf16)])
def run_q(stepm,dm,c3,r2):
    t,c=dm.shape; n=r2.shape[0]
    return call(piece_grad_kernel, ROWS, t, False, [stepm,dm,c3,r2], ["t","t","t","full"], [((t*n,c),bf16)], ["t"], [pltpu.VMEM((n,c),f32)])[0]
def run_m(step,u,dm,c3,bblk,oblk,nblk,r2,g,hp,q):
    t,c=u.shape; n=r2.shape[0]
    return call(state_grad_kernel, ROWS, t, True, [step,u,dm,c3,bblk,oblk,nblk,r2,g,hp,q], ["t"]*5+["full"]*3+["t"]*3,
      [((t,c),f32),((t,c),f32),((t,BLOCK*n),f32),((t,BLOCK*n),f32),((n,c),f32)], ["t","t","t","t","full"],
      [pltpu.VMEM((n,c),f32)]+[pltpu.VMEM((BLOCK*n,c),bf16)]*4+[pltpu.VMEM((ROWS,c),f32)])


def partner(value, axis, k):
    return lax.ppermute(value, axis, [(i, i ^ k) for i in range(lax.axis_size(axis))])


def gather_parts(value, axis):
    n = lax.axis_size(axis)
    if n > 4:
        return lax.all_gather(value, axis)
    me = lax.axis_index(axis)
    parts = [value] + [partner(value, axis, k) for k in range(1, n)]
    whole = jnp.zeros((n,) + value.shape, value.dtype)
    for k, part in enumerate(parts):
        whole = lax.dynamic_update_index_in_dim(whole, part, me ^ k, 0)
    return whole


def sum_parts(value, axis):
    n = lax.axis_size(axis)
    if n > 4:
        return lax.psum(value, axis)
    low = value.astype(bf16)
    total = low.astype(f32)
    for k in range(1, n):
        total = total + partner(low, axis, k).astype(f32)
    return total


def scatter_sum(value, axis):
    n = lax.axis_size(axis)
    if n > 4:
        return lax.psum_scatter(value, axis, scatter_dimension=0)
    me = lax.axis_index(axis)
    low = value.astype(bf16)
    total = lax.dynamic_index_in_dim(value, me, 0, False)
    for k in range(1, n):
        total = total + partner(lax.dynamic_index_in_dim(low, me ^ k, 0, False), axis, k).astype(f32)
    return total


def sum_everywhere(value, axes):
    for axis in axes:
        k = 1
        while k < lax.axis_size(axis):
            value = value + partner(value, axis, k)
            k *= 2
    return value


def swish_fn(v):
    return v * jax.nn.sigmoid(v)


def swish_slope(v):
    s = jax.nn.sigmoid(v)
    return s * (1.0 + v * (1.0 - s))


def dot(a, b):
    return jnp.dot(a, b, preferred_element_type=f32)


def dot_t(a, b):
    return lax.dot_general(a, b, (((1,), (1,)), ((), ())), preferred_element_type=f32)


def t_dot(a, b):
    return lax.dot_general(a, b, (((0,), (0,)), ((), ())), preferred_element_type=f32)


def body(
    tokens,
    teacher,
    piece_starts,
    valid_rows,
    norm_gain,
    in_weight,
    conv_weight,
    conv_bias,
    xproj_weight,
    dtproj_weight,
    dt_bias,
    a_log,
    skip_weight,
    out_weight,
):
    seqs = lax.axis_size("seq")
    batches = lax.axis_size("batch")
    _, rows, width = tokens.shape
    total = rows * seqs
    taps, own = conv_weight.shape
    chans = own * batches
    depth = in_weight.shape[0]
    rank = dtproj_weight.shape[0]
    states = a_log.shape[1]
    me = lax.axis_index("seq")

    tok = tokens.reshape(rows, width)
    valid_f = valid_rows.reshape(rows, 1).astype(f32)
    counted = jnp.sum(valid_rows)
    extra = jnp.concatenate(
        [
            norm_gain[:, None],
            jnp.full((depth, 1), counted // 128).astype(bf16),
            jnp.full((depth, 1), counted % 128).astype(bf16),
            jnp.zeros((depth, 125), bf16),
        ],
        axis=1,
    )
    split = in_weight.reshape(depth, 2, batches, seqs, own).transpose(3, 0, 1, 2, 4).reshape(seqs, depth, 2 * chans)
    split = jnp.concatenate([split, jnp.broadcast_to(extra[None], (seqs, depth, 128))], axis=2)
    split = lax.all_to_all(split, "seq", 0, 0).reshape(seqs * depth, 2 * chans + 128)
    gathered = lax.all_gather(split, "batch", axis=0, tiled=True)
    in_w = gathered[:, : 2 * chans]
    gain = gathered[:, 2 * chans].astype(f32)
    total_valid = (
        jnp.sum(gathered[:, 2 * chans + 1].astype(f32)) * 128.0 + jnp.sum(gathered[:, 2 * chans + 2].astype(f32))
    ) / depth
    small = jnp.concatenate(
        [
            out_weight,
            xproj_weight,
            dtproj_weight.T,
            a_log,
            conv_weight.T,
            conv_bias[:, None],
            dt_bias[:, None],
            skip_weight[:, None],
        ],
        axis=1,
    )
    used = small.shape[1]
    small = jnp.pad(small, ((0, 0), (0, -used % 128)))
    small = lax.all_gather(small, "batch", axis=0, tiled=True)
    cuts = [0]
    for size in (width, rank + 2 * states, rank, states, taps, 1, 1, 1):
        cuts.append(cuts[-1] + size)
    out_w, xproj_w, dt_w, alog_w, conv_w, convb_w, dtb_w, skip_w = [
        small[:, a:b] for a, b in zip(cuts[:-1], cuts[1:])
    ]
    r2 = -jnp.exp(alog_w.astype(f32).T) * LOG2E
    conv_f = conv_w.astype(f32).T
    convb_f = convb_w.astype(f32).T
    dtb_f = dtb_w.astype(f32).T
    skip_f = skip_w.astype(f32).T

    flags = jnp.pad(piece_starts.astype(bf16), ((0, 15), (0, width - rows)))
    everything = gather_parts(jnp.concatenate([tok, flags], axis=0), "seq")
    x_all = everything[:, :rows].reshape(total, width).astype(f32)
    starts = everything[:, rows, :rows].reshape(total).astype(f32)
    mean_sq = jnp.mean(x_all * x_all, axis=-1, keepdims=True)
    unit = x_all * lax.rsqrt(mean_sq + 1e-05)
    normed = (unit * gain[None]).astype(bf16)
    joint = dot(normed, in_w)
    stream = joint[:, :chans].astype(bf16)
    gate = joint[:, chans:]
    wide = jnp.pad(stream, ((taps - 1, 0), (0, 0))).astype(f32)
    conv_pre = convb_f
    for tap in range(taps):
        conv_pre = conv_pre + conv_f[tap] * wide[tap : tap + total]
    act = swish_fn(conv_pre).astype(bf16)
    act_f = act.astype(f32)
    proj = sum_parts(dot(act, xproj_w), "seq")
    low = proj[:, :rank].astype(bf16)
    b_in = proj[:, rank : rank + states]
    c_out = proj[:, rank + states :]
    dt_pre = dot_t(low, dt_w) + dtb_f
    step = jax.nn.softplus(dt_pre)
    running = jnp.cumsum(starts)
    lagged = jnp.concatenate([jnp.zeros((PIECE,), f32), running[: total - PIECE]])
    inside = (running - lagged > 0.5).astype(f32)
    carry_on = inside * (1.0 - starts)
    stepm = jnp.where(carry_on[:, None] > 0.5, step, NEVER)
    u = step * act_f
    b3, c3 = blocks_of(b_in), blocks_of(c_out)
    bblk, cblk = block_diag(b_in), block_diag(c_out)
    oblk = block_diag(jnp.ones((BLOCK, states), f32))
    nblk = jnp.tile(jnp.eye(states, dtype=bf16), (1, BLOCK))
    g = run_g(stepm, u, b3, r2)
    y, hp = run_h(step, u, b3, cblk, r2, g)
    mixed = y + skip_f * act_f
    gate_act = swish_fn(gate)
    gated = (mixed * gate_act).astype(bf16)
    branch = scatter_sum(dot(gated, out_w).reshape(seqs, rows, width), "seq")
    tok_f = tok.astype(f32)
    result = tok_f + branch
    output = result.astype(bf16)
    misfit = result - teacher.reshape(rows, width).astype(f32)
    square_sum = sum_everywhere(jnp.sum(valid_f * misfit * misfit).reshape(1, 1), ("batch", "seq"))
    loss = square_sum[0, 0] / (total_valid * width)
    d_result = 2.0 * (total * batches) / total_valid * valid_f * misfit

    d_branch = gather_parts(d_result.astype(bf16), "seq").reshape(total, width)
    d_gated = dot_t(d_branch, out_w)
    out_grad = lax.psum_scatter(t_dot(gated, d_branch), "batch", scatter_dimension=0, tiled=True)
    d_mixed = d_gated * gate_act
    d_gate = (d_gated * mixed * swish_slope(gate)).astype(bf16)
    q = run_q(stepm, d_mixed, c3, r2)
    xs, ys, dbs, dcs, als = run_m(step, u, d_mixed, c3, bblk, oblk, nblk, r2, g, hp, q)
    d_step = ys * LN2 + act_f * xs
    d_act = step * xs + skip_f * d_mixed
    keep = (jnp.arange(total)[:, None] % BLOCK) == (jnp.arange(BLOCK * states)[None, :] // states)
    d_b = jnp.where(keep, dbs, 0.0).reshape(total, BLOCK, states).sum(1)
    d_c = jnp.where(keep, dcs, 0.0).reshape(total, BLOCK, states).sum(1)
    alog_grad = (als * (r2 * LN2)).T
    skip_grad = jnp.sum(d_mixed * act_f, axis=0)
    d_pre = d_step * jax.nn.sigmoid(dt_pre)
    dtb_grad = jnp.sum(d_pre, axis=0)
    d_pre_low = d_pre.astype(bf16)
    dt_grad = t_dot(d_pre_low, low)
    d_low = dot(d_pre_low, dt_w)
    d_proj = sum_parts(jnp.concatenate([d_low, d_b, d_c], axis=1), "seq").astype(bf16)
    xproj_grad = t_dot(act, d_proj)
    d_act_all = d_act + dot_t(d_proj, xproj_w)
    d_conv = d_act_all * swish_slope(conv_pre)
    convb_grad = jnp.sum(d_conv, axis=0)
    longer = jnp.pad(d_conv, ((0, taps - 1), (0, 0)))
    d_stream = jnp.zeros_like(d_conv)
    conv_grads = []
    for tap in range(taps):
        conv_grads.append(jnp.sum(d_conv * wide[tap : tap + total], axis=0))
        back = taps - 1 - tap
        d_stream = d_stream + conv_f[tap] * longer[back : back + total]
    d_joint = jnp.concatenate([d_stream.astype(bf16), d_gate], axis=1)
    in_grad = t_dot(normed, d_joint)
    d_normed = scatter_sum(dot_t(d_joint, in_w).reshape(seqs, rows, width), "seq")
    small_grads = jnp.concatenate(
        [xproj_grad, dt_grad, alog_grad, jnp.stack(conv_grads + [convb_grad, dtb_grad, skip_grad], axis=1)], axis=1
    )
    kept = small_grads.shape[1]
    small_grads = jnp.pad(small_grads, ((0, 0), (0, -kept % 256))).reshape(batches, -1, 2 * chans)
    lines = seqs * depth
    both = jnp.concatenate([in_grad.reshape(batches, lines, 2 * chans), small_grads], axis=1)
    both = lax.psum_scatter(both, "batch", scatter_dimension=0)
    small_out = both[lines:].reshape(own, -1)
    in_out = lax.all_to_all(both[:lines].reshape(seqs, depth, 2 * chans), "seq", 0, 0)
    in_out = in_out.reshape(seqs, depth, 2, batches, own).transpose(1, 2, 3, 0, 4).reshape(depth, -1)
    cuts = [0]
    for size in (rank + 2 * states, rank, states, taps, 1, 1, 1):
        cuts.append(cuts[-1] + size)
    xproj_out, dt_out, alog_out, conv_out, convb_out, dtb_out, skip_out = [
        small_out[:, a:b] for a, b in zip(cuts[:-1], cuts[1:])
    ]
    gain_f = norm_gain.astype(f32)
    gain_out = jnp.sum(in_out * in_weight.astype(f32), axis=1) / gain_f
    own_sq = jnp.mean(tok_f * tok_f, axis=-1, keepdims=True)
    root_inv = lax.rsqrt(own_sq + 1e-05)
    own_unit = tok_f * root_inv
    scaled = d_normed * gain[None]
    input_grad = d_result + root_inv * (scaled - own_unit * jnp.mean(scaled * own_unit, axis=-1, keepdims=True))
    return (
        output[None],
        loss,
        input_grad[None],
        gain_out,
        in_out,
        conv_out.T,
        convb_out[:, 0],
        xproj_out,
        dt_out.T,
        dtb_out[:, 0],
        alog_out,
        skip_out[:, 0],
        out_grad,
    )


def solution(mesh):
    return jax.shard_map(
        body,
        mesh=mesh,
        in_specs=(
            P("batch", "seq", None),
            P("batch", "seq", None),
            P("batch", "seq"),
            P("batch", "seq"),
            P(("batch", "seq")),
            P(("batch", "seq"), None),
            P(None, ("batch", "seq")),
            P(("batch", "seq")),
            P(("batch", "seq"), None),
            P(None, ("batch", "seq")),
            P(("batch", "seq")),
            P(("batch", "seq"), None),
            P(("batch", "seq")),
            P(("batch", "seq"), None),
        ),
        out_specs=(
            P("batch", "seq", None),
            P(),
            P("batch", "seq", None),
            P(("batch", "seq")),
            P(("batch", "seq"), None),
            P(None, ("batch", "seq")),
            P(("batch", "seq")),
            P(("batch", "seq"), None),
            P(None, ("batch", "seq")),
            P(("batch", "seq")),
            P(("batch", "seq"), None),
            P(("batch", "seq")),
            P(("batch", "seq"), None),
        ),
        check_vma=False,
    )
```

```python
import jax
import jax.numpy as jnp
from jax import lax
from jax.experimental import pallas as pl
from jax.experimental.pallas import tpu as pltpu
from jax.sharding import PartitionSpec as P

PIECE = 256
BLOCK = 16
ROWS = 128
LOG2E = 1.4426950408889634
LN2 = 0.6931471805599453
NEVER = 1e9
LANES = 128
f32 = jnp.float32
bf16 = jnp.bfloat16

ALOG, CONV, CONVB, DTB, SKIP = 64, 80, 84, 85, 86
INTO, OUT, CARRY = 64, 80, 96


def dot(a, b):
    return jnp.dot(a, b, preferred_element_type=f32)


def dot_t(a, b):
    return lax.dot_general(a, b, (((1,), (1,)), ((), ())), preferred_element_type=f32)


def t_dot(a, b):
    return lax.dot_general(a, b, (((0,), (0,)), ((), ())), preferred_element_type=f32)


def sigmoid(v):
    return 1.0 / (1.0 + jnp.exp(-v))


def row_of(ref, t, n):
    return jnp.broadcast_to(ref[pl.ds(t, 1), :], (n, ref.shape[1]))


def col_of(block, tt, c):
    return jnp.broadcast_to(block[:, tt : tt + 1], (block.shape[0], c))


def rates_of(vec_ref, n):
    return -jnp.exp(vec_ref[ALOG : ALOG + n, :]) * LOG2E


def dt_of(proj, vec_ref, rank):
    low = proj[:, :rank].astype(bf16)
    return low, dot(low, vec_ref[:rank, :].astype(bf16)) + vec_ref[DTB : DTB + 1, :]


def softplus(v):
    return jnp.maximum(v, 0.0) + jnp.log1p(jnp.exp(-jnp.abs(v)))


def columns(proj_t, first, n, into_ref):
    for j in range(into_ref.shape[0]):
        into_ref[j] = proj_t[first : first + n, j * BLOCK : (j + 1) * BLOCK]


def block_diag(values, n):
    rows, wide = values.shape[0], BLOCK * n
    spread = (
        lax.broadcasted_iota(jnp.int32, (n, wide), 1) % n == lax.broadcasted_iota(jnp.int32, (n, wide), 0)
    ).astype(f32).astype(bf16)
    keep = lax.broadcasted_iota(jnp.int32, (rows, wide), 1) // n == lax.broadcasted_iota(
        jnp.int32, (rows, wide), 0
    ) % BLOCK
    return jnp.where(keep, dot(values, spread), 0.0).astype(bf16)


def unit_of(x):
    return x * lax.rsqrt(jnp.mean(x * x, axis=-1, keepdims=True) + 1e-05)


def start_kernel(
    me_ref, x_ref, *refs,
):
    parts = refs[:-13]
    (
        normed_ref, stream_ref, pre_ref, act_ref, proj_ref, w_ref, vec_ref, xproj_ref, gain_ref, marks_ref,
        wide_ref, ext_ref, cols_ref,
    ) = refs[-13:]
    rows, chans = stream_ref.shape
    taps = CONVB - CONV

    @pl.when(pl.program_id(0) == 0)
    def _():
        wide_ref[:8, :] = jnp.zeros((8, chans), f32)
        place = 1
        for part in parts:
            count, lines, _ = part.shape
            own = chans * lines // w_ref.shape[0]
            for k in range(count):
                block = me_ref[place]
                place += 1
                at = pl.ds(pl.multiple_of(block * lines, lines), lines)
                w_ref[at, :] = part[k, :, :chans]
                ext = part[k, :, chans:].astype(f32)
                ext_ref[at, :] = ext
                at = pl.ds(pl.multiple_of(block * own, own), own)
                cols_ref[at, :] = ext[:own]
                used = lax.broadcasted_iota(jnp.int32, (own, LANES), 1) < CARRY
                xproj_ref[at, :] = jnp.where(used, ext[own : 2 * own], 0.0).astype(bf16)
        for k in range(w_ref.shape[0] // LANES):
            at = slice(k * LANES, (k + 1) * LANES)
            gain_ref[:, at] = ext_ref[at, :].T[LANES - 3 : LANES - 2]
        for k in range(chans // LANES):
            at = slice(k * LANES, (k + 1) * LANES)
            vec_ref[:, at] = cols_ref[at, :].T
        marks_ref[...] = jnp.sum(ext_ref[...], axis=0, keepdims=True)

    normed = (unit_of(x_ref[...].astype(f32)) * gain_ref[...]).astype(bf16)
    normed_ref[...] = normed
    stream = dot(normed, w_ref[...]).astype(bf16)
    stream_ref[...] = stream
    wide_ref[8:, :] = stream.astype(f32)
    pre = jnp.broadcast_to(vec_ref[CONVB : CONVB + 1, :], (rows, chans))
    for tap in range(taps):
        first = 8 - taps + 1 + tap
        pre = pre + vec_ref[CONV + tap : CONV + tap + 1, :] * wide_ref[first : first + rows, :]
    wide_ref[:8, :] = wide_ref[rows:, :]
    pre_ref[...] = pre
    act = (pre * sigmoid(pre)).astype(bf16)
    act_ref[...] = act
    proj_ref[...] = dot(act, xproj_ref[...]).astype(bf16)


def piece_kernel(me_ref, proj_ref, act_ref, vec_ref, g_ref, carry_ref, u_ref, stepm_ref, col_ref):
    rows, c = act_ref.shape
    n = carry_ref.shape[0]

    @pl.when(pl.program_id(0) == 0)
    def _():
        carry_ref[...] = jnp.zeros_like(carry_ref)

    proj = proj_ref[...]
    _, pre = dt_of(proj, vec_ref, INTO)
    step = softplus(pre)
    u_ref[...] = step * act_ref[...].astype(f32)
    stepm_ref[...] = jnp.where(proj[:, CARRY : CARRY + 1] > 0.5, step, NEVER)
    columns(proj.T, INTO, n, col_ref)
    r2 = rates_of(vec_ref, n)

    def block(i, carry):
        j = rows // BLOCK - 1 - i
        into = col_ref[j]
        for tt in reversed(range(BLOCK)):
            t = j * BLOCK + tt
            g = row_of(u_ref, t, n) * col_of(into, tt, c) + carry
            g_ref[pl.ds(pl.multiple_of(t * n, n), n), :] = g.astype(bf16)
            carry = jnp.exp2(row_of(stepm_ref, t, n) * r2) * g
        return carry

    carry_ref[...] = lax.fori_loop(0, rows // BLOCK, block, carry_ref[...])


def ahead_kernel(
    me_ref, proj_ref, act_ref, normed_ref, g_ref, vec_ref, second_ref,
    hp_ref, mixed_ref, gate_ref, gated_ref, branch_ref, wgate_ref, outw_ref,
    carry_ref, u_ref, step_ref, col_ref, diag_ref, s_ref, y_ref,
):
    rows, c = act_ref.shape
    n = carry_ref.shape[0]

    @pl.when(pl.program_id(0) == 0)
    def _():
        carry_ref[...] = jnp.zeros_like(carry_ref)
        blocks = second_ref.shape[0]
        lines, own = wgate_ref.shape[0] // blocks, outw_ref.shape[0] // blocks
        for b in range(blocks):
            wgate_ref[b * lines : (b + 1) * lines, :] = second_ref[b, :lines, :]
            for k in range(outw_ref.shape[1] // c):
                outw_ref[b * own : (b + 1) * own, k * c : (k + 1) * c] = second_ref[
                    b, lines + k * own : lines + (k + 1) * own, :
                ]

    proj = proj_ref[...]
    act = act_ref[...].astype(f32)
    _, pre = dt_of(proj, vec_ref, INTO)
    step = softplus(pre)
    step_ref[...] = step
    u_ref[...] = step * act
    columns(proj.T, INTO, n, col_ref)
    read = proj[:, OUT : OUT + n]
    high = read.astype(bf16)
    diag_ref[0, BLOCK:] = block_diag(high, n)
    diag_ref[1, BLOCK:] = block_diag((read - high.astype(f32)).astype(bf16), n)
    r2 = rates_of(vec_ref, n)

    def read_out(j):
        r16 = pl.ds(pl.multiple_of(j * BLOCK, BLOCK), BLOCK)
        both = dot(jnp.concatenate([diag_ref[0, r16, :], diag_ref[1, r16, :]], axis=0), s_ref[...])
        y_ref[r16, :] = both[:BLOCK] + both[BLOCK:]

    def block(j, h):
        read_out(j)
        into = col_ref[j]
        for tt in range(BLOCK):
            t = j * BLOCK + tt
            at = pl.ds(pl.multiple_of(t * n, n), n)
            hp = jnp.exp2(row_of(step_ref, t, n) * r2) * h
            h = hp + row_of(u_ref, t, n) * col_of(into, tt, c)
            hp_ref[at, :] = hp.astype(bf16)
            s_ref[tt * n : (tt + 1) * n, :] = (hp + g_ref[at, :].astype(f32)).astype(bf16)
        return h

    carry_ref[...] = lax.fori_loop(0, rows // BLOCK, block, carry_ref[...])
    read_out(rows // BLOCK)
    mixed = y_ref[BLOCK:] + vec_ref[SKIP : SKIP + 1, :] * act
    mixed_ref[...] = mixed
    gate = dot(normed_ref[...], wgate_ref[...])
    gate_ref[...] = gate
    gated = (mixed * (gate * sigmoid(gate))).astype(bf16)
    gated_ref[...] = gated
    branch_ref[...] = dot(gated, outw_ref[...]).astype(bf16)


def piece_grad_kernel(
    me_ref, proj_ref, act_ref, mixed_ref, gate_ref, db_ref, vec_ref, outw_ref,
    q_ref, dm_ref, dg_ref, sgrad_ref,
    carry_ref, stepm_ref, col_ref,
):
    rows, c = act_ref.shape
    n = carry_ref.shape[0]

    @pl.when(pl.program_id(0) == 0)
    def _():
        carry_ref[...] = jnp.zeros_like(carry_ref)
        sgrad_ref[...] = jnp.zeros_like(sgrad_ref)

    proj = proj_ref[...]
    _, pre = dt_of(proj, vec_ref, INTO)
    stepm_ref[...] = jnp.where(proj[:, CARRY : CARRY + 1] > 0.5, softplus(pre), NEVER)
    columns(proj.T, OUT, n, col_ref)
    db = db_ref[...]
    dgated = dot_t(db, outw_ref[...])
    gate = gate_ref[...]
    s = sigmoid(gate)
    dm = dgated * (gate * s)
    dm_ref[...] = dm
    dg = (dgated * mixed_ref[...] * (s * (1.0 + gate * (1.0 - s)))).astype(bf16)
    dg_ref[...] = dg
    sgrad_ref[...] += jnp.sum(dm * act_ref[...].astype(f32), axis=0, keepdims=True)
    r2 = rates_of(vec_ref, n)

    def block(j, w):
        read = col_ref[j]
        for tt in range(BLOCK):
            t = j * BLOCK + tt
            q = jnp.exp2(row_of(stepm_ref, t, n) * r2) * w
            q_ref[pl.ds(pl.multiple_of(t * n, n), n), :] = q.astype(bf16)
            w = q + row_of(dm_ref, t, n) * col_of(read, tt, c)
        return w

    carry_ref[...] = lax.fori_loop(0, rows // BLOCK, block, carry_ref[...])


def state_grad_kernel(
    me_ref, proj_ref, act_ref, dm_ref, g_ref, hp_ref, q_ref, vec_ref, sgrad_ref,
    dact_ref, dproj_ref, table_ref,
    carry_ref, u_ref, step_ref, col_ref, diag_ref, ig_ref, rr_ref, rs_ref, pair_ref, own_ref, x_ref, y_ref, dp_ref,
):
    rows, c = act_ref.shape
    n = carry_ref.shape[0]
    wide = BLOCK * n

    @pl.when(pl.program_id(0) == 0)
    def _():
        carry_ref[...] = jnp.zeros_like(carry_ref)
        table_ref[...] = jnp.zeros_like(table_ref)
        table_ref[SKIP : SKIP + 1, :] = sgrad_ref[...]
        rs_ref[...] = jnp.zeros_like(rs_ref)

    proj = proj_ref[...]
    act = act_ref[...].astype(f32)
    low, pre = dt_of(proj, vec_ref, INTO)
    step = softplus(pre)
    step_ref[...] = step
    u_ref[...] = step * act
    columns(proj.T, OUT, n, col_ref)
    diag_ref[:rows] = block_diag(proj[:, INTO : INTO + n].astype(bf16), n)
    r2 = rates_of(vec_ref, n)
    iota = lambda shape, axis: lax.broadcasted_iota(jnp.int32, shape, axis)
    mask = lambda v: v.astype(f32).astype(bf16)
    by_row = mask(iota((BLOCK, wide), 1) // n == iota((BLOCK, wide), 0))
    by_state = mask(iota((n, wide), 1) % n == iota((n, wide), 0))
    part = min(c, 2 * LANES)
    which = mask(iota((2 * part, LANES), 0) // part == iota((2 * part, LANES), 1) // n % 2)
    own_lane = iota((wide, LANES), 1) % n == iota((wide, LANES), 0) % n

    def sums(j):
        r16 = pl.ds(pl.multiple_of(j * BLOCK, BLOCK), BLOCK)
        x_ref[r16, :] = dot(diag_ref[r16, :], ig_ref[...])
        y_ref[r16, :] = dot(by_row, rr_ref[...])
        table_ref[ALOG : ALOG + n, :] += dot(by_state, rs_ref[...])
        dp_ref[pl.ds(pl.multiple_of((j + 1) * BLOCK, BLOCK), BLOCK), :] = dot(by_row, own_ref[...])
        own_ref[...] = jnp.where(own_lane, dot(pair_ref[...], which), 0.0).astype(bf16)

    def block(i, m):
        j = rows // BLOCK - 1 - i
        sums(j + 1)
        read = col_ref[j]
        for tt in reversed(range(BLOCK)):
            t = j * BLOCK + tt
            at = pl.ds(pl.multiple_of(t * n, n), n)
            loc = slice(tt * n, (tt + 1) * n)
            drow = row_of(dm_ref, t, n)
            mu = m + drow * col_of(read, tt, c)
            srow = row_of(step_ref, t, n)
            m = jnp.exp2(srow * r2) * mu
            low_mu = mu.astype(bf16)
            q = q_ref[at, :]
            g = g_ref[at, :]
            hp = hp_ref[at, :]
            rg = low_mu * hp + q * g
            ig = low_mu + q
            ig_ref[loc, :] = ig
            rr_ref[loc, :] = (rg.astype(f32) * r2).astype(bf16)
            rs_ref[loc, :] = rg * srow.astype(bf16)
            pb = ig * row_of(u_ref, t, n).astype(bf16)
            pc = (hp + g) * drow.astype(bf16)
            sb, sc = pb[:, :part], pc[:, :part]
            for k in range(1, c // part):
                sb = sb + pb[:, k * part : (k + 1) * part]
                sc = sc + pc[:, k * part : (k + 1) * part]
            pair_ref[loc, :part] = sb
            pair_ref[loc, part:] = sc
        return m

    carry_ref[...] = lax.fori_loop(0, rows // BLOCK, block, carry_ref[...])
    sums(0)
    dp_ref[:BLOCK, :] = dot(by_row, own_ref[...])
    rs_ref[...] = jnp.zeros_like(rs_ref)
    xs = x_ref[:rows]
    dact_ref[...] = step_ref[...] * xs + vec_ref[SKIP : SKIP + 1, :] * dm_ref[...]
    dpre = (y_ref[:rows] * LN2 + act * xs) * sigmoid(pre)
    table_ref[DTB : DTB + 1, :] += jnp.sum(dpre, axis=0, keepdims=True)
    dpre_low = dpre.astype(bf16)
    table_ref[:INTO, :] += t_dot(low, dpre_low)
    dproj_ref[...] = dp_ref[:rows].astype(bf16)
    dproj_ref[:, :INTO] = dot_t(dpre_low, vec_ref[:INTO, :].astype(bf16)).astype(bf16)

    @pl.when(pl.program_id(0) == pl.num_programs(0) - 1)
    def _():
        table_ref[ALOG : ALOG + n, :] *= -jnp.exp(vec_ref[ALOG : ALOG + n, :])


def end_kernel(own, me_ref, *refs):
    parts = refs[:-17]
    (
        dact_ref, pre_ref, stream_ref, act_ref, dg_ref, vec_ref, xproj_ref, ws_ref, wg_ref, table_ref,
        dn_ref, ds_ref, small_ref,
        wide_ref, xgrad_ref, cgrad_ref, turned_ref,
    ) = refs[-17:]
    rows, c = act_ref.shape
    taps = CONVB - CONV

    @pl.when(pl.program_id(0) == 0)
    def _():
        wide_ref[rows:, :] = jnp.zeros((8, c), f32)
        xgrad_ref[...] = jnp.zeros_like(xgrad_ref)
        cgrad_ref[...] = table_ref[...]

    dproj = parts[0][...].astype(f32)
    for part in parts[1:]:
        dproj = dproj + part[...].astype(f32)
    used = lax.broadcasted_iota(jnp.int32, dproj.shape, 1) < CARRY
    dproj = jnp.where(used, dproj, 0.0).astype(bf16)
    pre = pre_ref[...]
    s = sigmoid(pre)
    dconv = (dact_ref[...] + dot_t(dproj, xproj_ref[...])) * (s * (1.0 + pre * (1.0 - s)))
    wide_ref[:rows, :] = dconv
    xgrad_ref[...] += t_dot(act_ref[...], dproj)
    cgrad_ref[CONVB : CONVB + 1, :] += jnp.sum(dconv, axis=0, keepdims=True)
    stream = stream_ref[...].astype(f32)
    dstream = jnp.zeros((rows, c), f32)
    for tap in range(taps):
        back = taps - 1 - tap
        moved = wide_ref[back : back + rows, :]
        cgrad_ref[CONV + tap : CONV + tap + 1, :] += jnp.sum(stream * moved, axis=0, keepdims=True)
        dstream = dstream + vec_ref[CONV + tap : CONV + tap + 1, :] * moved
    wide_ref[rows:, :] = dconv[:8, :]
    dstream_low = dstream.astype(bf16)
    dn_ref[...] = (dot_t(dstream_low, ws_ref[...]) + dot_t(dg_ref[...], wg_ref[...])).astype(bf16)
    ds_ref[...] = dstream_low

    @pl.when(pl.program_id(0) == pl.num_programs(0) - 1)
    def _():
        for k in range(c // LANES):
            at = slice(k * LANES, (k + 1) * LANES)
            turned_ref[at, :] = cgrad_ref[:, at].T
        lines = 2 * own * LANES // c
        for b in range(c // own):
            at = slice(b * own, (b + 1) * own)
            both = jnp.concatenate([xgrad_ref[at, :], turned_ref[at, :]], axis=0)
            for k in range(c // LANES):
                small_ref[b * lines : (b + 1) * lines, k * LANES : (k + 1) * LANES] = both[k * lines : (k + 1) * lines]


def call(kernel, me, ins, outs, scratch, total, local, reverse=False):
    steps = total // ROWS
    per = local // ROWS
    turn = (lambda i: steps - 1 - i) if reverse else (lambda i: i)

    def spec(shape, kind):
        if kind == "f":
            return pl.BlockSpec(shape, lambda i, me_ref: (0,) * len(shape))
        if kind == "x":
            return pl.BlockSpec(
                (None, ROWS, shape[2]), lambda i, me_ref: ((turn(i) // per) ^ me_ref[0], turn(i) % per, 0)
            )
        return pl.BlockSpec((shape[0] // steps, shape[1]), lambda i, me_ref: (turn(i), 0))

    return pl.pallas_call(
        kernel,
        out_shape=[jax.ShapeDtypeStruct(s, d) for s, d, _ in outs],
        grid_spec=pltpu.PrefetchScalarGridSpec(
            num_scalar_prefetch=1,
            grid=(steps,),
            in_specs=[spec(a.shape, k) for a, k in ins],
            out_specs=[spec(s, k) for s, _, k in outs],
            scratch_shapes=scratch,
        ),
        compiler_params=pltpu.CompilerParams(dimension_semantics=("arbitrary",), vmem_limit_bytes=60 << 20),
    )(me, *[a for a, _ in ins])


def split_kernel(seqs, batches, own, w_ref, extra_ref, out_ref):
    half, chans = w_ref.shape[1] // 2, batches * own
    for s in range(seqs):
        for k in range(2):
            pieces = [
                w_ref[:, k * half + (b * seqs + s) * own : k * half + (b * seqs + s + 1) * own].astype(f32)
                for b in range(batches)
            ]
            first = k * (chans + LANES)
            out_ref[s, :, first : first + chans] = jnp.concatenate(pieces, axis=1).astype(bf16)
        out_ref[s, :, chans : chans + LANES] = extra_ref[...]


def split_columns(weight, extra, seqs, batches, own):
    shape = jax.ShapeDtypeStruct((seqs, weight.shape[0], 2 * batches * own + LANES), bf16)
    return pl.pallas_call(lambda *refs: split_kernel(seqs, batches, own, *refs), out_shape=shape)(weight, extra)


def join_kernel(
    batches, stream_ref, gate_ref, small_ref, w_ref, gain_ref,
    out_ref, gain_out_ref, xproj_ref, dt_ref, alog_ref, conv_ref, convb_ref, dtb_ref, skip_ref,
):
    seqs, half = stream_ref.shape[0], w_ref.shape[1] // 2
    chans = half // seqs
    own = chans // batches
    for k, part in enumerate((stream_ref, gate_ref)):
        whole = [part[s] for s in range(seqs)]
        pieces = [whole[s][:, b * own : (b + 1) * own] for b in range(batches) for s in range(seqs)]
        out_ref[:, k * half : (k + 1) * half] = jnp.concatenate(pieces, axis=1)
    products = out_ref[...] * w_ref[...].astype(f32)
    gain_out_ref[...] = jnp.sum(products, axis=1, keepdims=True) / gain_ref[...]
    small = small_ref[...]
    both = jnp.concatenate([small[:, k : k + LANES] for k in range(0, chans, LANES)], axis=0)
    xproj_ref[...] = both[:own, :CARRY]
    table = both[own:]
    alog_ref[...] = table[:, ALOG:CONV]
    table = jnp.concatenate([table, jnp.zeros((LANES - own, LANES), f32)], axis=0).T[:, :own]
    dt_ref[...] = table[:INTO]
    conv_ref[...] = table[CONV:CONVB]
    convb_ref[...] = table[CONVB : CONVB + 1]
    dtb_ref[...] = table[DTB : DTB + 1]
    skip_ref[...] = table[SKIP : SKIP + 1]


def join_columns(stream, gate, small, weight, gain, batches, own):
    depth = weight.shape[0]
    shapes = [weight.shape, (depth, 1), (own, CARRY), (INTO, own), (own, CONV - ALOG), (CONVB - CONV, own)]
    shapes += [(1, own)] * 3
    return pl.pallas_call(
        lambda *refs: join_kernel(batches, *refs), out_shape=[jax.ShapeDtypeStruct(s, f32) for s in shapes]
    )(stream, gate, small, weight, gain)


def partner(value, axis, k):
    return lax.ppermute(value, axis, [(i, i ^ k) for i in range(lax.axis_size(axis))])


def gather_parts(value, axis):
    n = lax.axis_size(axis)
    if n > 4:
        return lax.all_gather(value, axis)
    return jnp.stack([value] + [partner(value, axis, k) for k in range(1, n)])


def gather_batch(value):
    n = lax.axis_size("batch")
    if n > 8:
        return [lax.all_gather(value, "batch")], [jnp.int32(k) for k in range(n)]
    me = lax.axis_index("batch")
    chips = jnp.stack([value] + [partner(value, "batch", 2 * k) for k in range(1, n // 2)])
    other = partner(chips, "batch", 1)
    places = [me ^ (2 * k) for k in range(n // 2)] + [me ^ (2 * k + 1) for k in range(n // 2)]
    return [chips, other], places


def exact(total, rows):
    terms = []
    for _ in range(3):
        term = lax.reduce_precision(total, 8, 7)
        terms.append(term)
        total = total - term
    return jnp.concatenate(terms + [jnp.zeros((rows - 3, total.shape[1]), f32)], axis=0).astype(bf16)


def row_sum(rows):
    a = rows[:3].astype(f32)
    return (a[:1] + a[1:2]) + a[2:]


def tree(values):
    while len(values) > 1:
        values = [a + b for a, b in zip(values[::2], values[1::2])]
    return values[0]


def scatter_batch(value, total):
    n = lax.axis_size("batch")
    if n > 8:
        return lax.psum_scatter(value, "batch", scatter_dimension=0), sum_everywhere(total, ("batch",)), value
    me = lax.axis_index("batch")
    rows, c = value.shape[1:]
    block = lambda t: jnp.broadcast_to(exact(jnp.tile(t, (1, c // LANES)), BLOCK)[None], (n // 2, BLOCK, c))
    pairs = value.reshape((n // 2, 2) + value.shape[1:])
    mine = lax.dynamic_index_in_dim(pairs, me % 2, 1, False)
    theirs = lax.dynamic_index_in_dim(pairs, 1 - me % 2, 1, False).astype(bf16)
    got = partner(jnp.concatenate([theirs, block(total)], axis=1), "batch", 1)
    mine = mine + got[:, :rows].astype(f32)
    total = row_sum(exact(total, BLOCK)) + row_sum(got[0, rows:, :LANES])
    low = jnp.concatenate([mine.astype(bf16), block(total)], axis=1)
    got = [
        partner(lax.dynamic_index_in_dim(low, (me // 2) ^ k, 0, False), "batch", 2 * k) for k in range(1, n // 2)
    ]
    result = lax.dynamic_index_in_dim(mine, me // 2, 0, False)
    for part in got:
        result = result + part[:rows].astype(f32)
    return result, tree([row_sum(exact(total, BLOCK))] + [row_sum(part[rows:, :LANES]) for part in got]), low


def scatter_parts(value, axis):
    n = lax.axis_size(axis)
    if n > 4:
        return [lax.psum_scatter(value.astype(f32), axis, scatter_dimension=0)]
    return [value[0]] + [partner(value[k], axis, k) for k in range(1, n)]


def share_parts(value, axis):
    n = lax.axis_size(axis)
    if n > 4:
        return [lax.psum(value.astype(f32), axis)]
    return [value] + [partner(value, axis, k) for k in range(1, n)]


def added(parts):
    total = parts[0].astype(f32)
    for part in parts[1:]:
        total = total + part.astype(f32)
    return total


def sum_everywhere(value, axes):
    for axis in axes:
        k = 1
        while k < lax.axis_size(axis):
            value = value + partner(value, axis, k)
            k *= 2
    return value


def body(
    tokens,
    teacher,
    piece_starts,
    valid_rows,
    norm_gain,
    in_weight,
    conv_weight,
    conv_bias,
    xproj_weight,
    dtproj_weight,
    dt_bias,
    a_log,
    skip_weight,
    out_weight,
):
    seqs = lax.axis_size("seq")
    batches = lax.axis_size("batch")
    _, rows, width = tokens.shape
    total = rows * seqs
    taps, own = conv_weight.shape
    chans = own * batches
    depth = in_weight.shape[0]
    rank = dtproj_weight.shape[0]
    states = a_log.shape[1]
    lines = depth * seqs
    packed = 2 * LANES * own // chans
    place = lax.axis_index("seq") if seqs <= 4 else jnp.int32(0)
    me = place.astype(jnp.int32).reshape(1)
    tok = tokens.reshape(rows, width)

    counted = jnp.sum(valid_rows, axis=1, keepdims=True)
    extra = jnp.concatenate(
        [
            jnp.zeros((depth, LANES - 3), bf16),
            norm_gain[:, None],
            jnp.broadcast_to((counted // 128).astype(bf16), (depth, 1)),
            jnp.broadcast_to((counted % 128).astype(bf16), (depth, 1)),
        ],
        axis=1,
    )
    split = split_columns(in_weight, extra, seqs, batches, own)
    split = lax.all_to_all(split, "seq", 0, 0).reshape(lines, 2 * chans + LANES)
    vectors = jnp.concatenate(
        [
            dtproj_weight.T,
            a_log,
            conv_weight.T,
            conv_bias[:, None],
            dt_bias[:, None],
            skip_weight[:, None],
        ],
        axis=1,
    )
    vectors = jnp.pad(vectors, ((0, 0), (0, LANES - vectors.shape[1])))
    columns_x = jnp.pad(xproj_weight, ((0, 0), (0, LANES - xproj_weight.shape[1])))
    local = jnp.pad(jnp.concatenate([vectors, columns_x], axis=0), ((0, lines - 2 * own), (chans, 0)))
    blocks, places = gather_batch(split[:, : chans + LANES] + local)
    second = jnp.concatenate(
        [split[:, chans + LANES :]] + [out_weight[:, k : k + chans] for k in range(0, width, chans)], axis=0
    )
    second = lax.all_gather(second, "batch")

    flags = jnp.pad(piece_starts.astype(bf16), ((0, 15), (0, width - rows)))
    held = jnp.concatenate([tok, flags], axis=0)
    held, split = lax.optimization_barrier((held, split))
    everything = gather_parts(held, "seq")

    tile = ((total, chans), f32, "t")
    low_tile = ((total, chans), bf16, "t")
    state = ((total * states, chans), bf16, "t")
    normed, stream, conv_pre, act, proj, w_stream, vec, xproj, gain, marks = call(
        start_kernel,
        jnp.concatenate([me] + [p.astype(jnp.int32).reshape(1) for p in places]),
        [(everything, "x")] + [(block, "f") for block in blocks],
        [
            ((seqs, rows, width), bf16, "x"),
            low_tile,
            tile,
            low_tile,
            ((total, LANES), bf16, "t"),
            ((width, chans), bf16, "f"),
            ((LANES, chans), f32, "f"),
            ((chans, LANES), bf16, "f"),
            ((1, width), f32, "f"),
            ((1, LANES), f32, "f"),
        ],
        [pltpu.VMEM((ROWS + 8, chans), f32), pltpu.VMEM((width, LANES), f32), pltpu.VMEM((chans, LANES), f32)],
        total,
        rows,
    )
    total_valid = (marks[:, LANES - 2 : LANES - 1] * 128.0 + marks[:, LANES - 1 :]) / depth
    slots = jnp.arange(seqs) ^ place
    starts = jnp.take(everything[:, rows, :rows].astype(f32), slots, axis=0).reshape(total)
    running = jnp.cumsum(starts)
    lagged = jnp.concatenate([jnp.zeros((PIECE,), f32), running[: total - PIECE]])
    carry_on = jnp.where(running - lagged > 0.5, 1.0 - starts, 0.0)
    proj = added(share_parts(proj, "seq"))
    proj = jnp.where(jnp.arange(LANES)[None, :] == CARRY, carry_on[:, None], proj)
    groups = (ROWS // BLOCK, states, BLOCK)
    (g,) = call(
        piece_kernel,
        me,
        [(proj, "t"), (act, "t"), (vec, "f")],
        [state],
        [
            pltpu.VMEM((states, chans), f32),
            pltpu.VMEM((ROWS, chans), f32),
            pltpu.VMEM((ROWS, chans), f32),
            pltpu.VMEM(groups, f32),
        ],
        total,
        rows,
        reverse=True,
    )
    hp, mixed, gate, gated, branch, w_gate, out_w = call(
        ahead_kernel,
        me,
        [(proj, "t"), (act, "t"), (normed, "x"), (g, "t"), (vec, "f"), (second, "f")],
        [
            state,
            tile,
            tile,
            ((seqs, rows, chans), bf16, "x"),
            ((seqs, rows, width), bf16, "x"),
            ((width, chans), bf16, "f"),
            ((chans, width), bf16, "f"),
        ],
        [
            pltpu.VMEM((states, chans), f32),
            pltpu.VMEM((ROWS, chans), f32),
            pltpu.VMEM((ROWS, chans), f32),
            pltpu.VMEM(groups, f32),
            pltpu.VMEM((2, ROWS + BLOCK, BLOCK * states), bf16),
            pltpu.VMEM((BLOCK * states, chans), bf16),
            pltpu.VMEM((ROWS + BLOCK, chans), f32),
        ],
        total,
        rows,
    )
    tok_f = tok.astype(f32)
    valid_f = valid_rows.reshape(rows, 1).astype(f32)
    result = tok_f + added(scatter_parts(branch, "seq"))
    output = result.astype(bf16)
    misfit = result - teacher.reshape(rows, width).astype(f32)
    squares = jnp.sum(valid_f * misfit * misfit, axis=0, keepdims=True)
    square_sum = jnp.broadcast_to(jnp.sum(squares, axis=1, keepdims=True), (1, LANES))
    d_result = 2.0 * (total * batches) / total_valid * valid_f * misfit

    d_branch = gather_parts(d_result.astype(bf16), "seq")
    q, d_mixed, d_gate, skip_grad = call(
        piece_grad_kernel,
        me,
        [
            (proj, "t"),
            (act, "t"),
            (mixed, "t"),
            (gate, "t"),
            (d_branch, "x"),
            (vec, "f"),
            (out_w, "f"),
        ],
        [state, tile, ((seqs, rows, chans), bf16, "x"), ((1, chans), f32, "f")],
        [pltpu.VMEM((states, chans), f32), pltpu.VMEM((ROWS, chans), f32), pltpu.VMEM(groups, f32)],
        total,
        rows,
    )
    flat = lambda v: v.reshape(total, v.shape[2])
    gate_grad = t_dot(flat(normed), flat(d_gate))
    out_grad = t_dot(flat(gated), flat(d_branch))
    gate_out = lax.psum_scatter(gate_grad, "batch", scatter_dimension=0, tiled=True)
    out_out = lax.psum_scatter(out_grad, "batch", scatter_dimension=0, tiled=True)
    d_act, d_proj, table = call(
        state_grad_kernel,
        me,
        [(proj, "t"), (act, "t"), (d_mixed, "t"), (g, "t"), (hp, "t"), (q, "t"), (vec, "f"), (skip_grad, "f")],
        [tile, ((total, LANES), bf16, "t"), ((LANES, chans), f32, "f")],
        [
            pltpu.VMEM((states, chans), f32),
            pltpu.VMEM((ROWS, chans), f32),
            pltpu.VMEM((ROWS, chans), f32),
            pltpu.VMEM(groups, f32),
            pltpu.VMEM((ROWS + BLOCK, BLOCK * states), bf16),
        ]
        + [pltpu.VMEM((BLOCK * states, chans), bf16)] * 3
        + [
            pltpu.VMEM((BLOCK * states, 2 * min(chans, 2 * LANES)), bf16),
            pltpu.VMEM((BLOCK * states, LANES), bf16),
        ]
        + [pltpu.VMEM((ROWS + 2 * BLOCK, chans), f32)] * 2
        + [pltpu.VMEM((ROWS + 2 * BLOCK, LANES), f32)],
        total,
        rows,
        reverse=True,
    )
    if seqs <= 4:
        d_proj = lax.dynamic_update_slice(d_proj, exact(square_sum[:, CARRY:], BLOCK), (0, CARRY))
        d_proj = share_parts(d_proj, "seq")
        square_sum = jnp.tile(tree([row_sum(part[:BLOCK, CARRY:]) for part in d_proj]), (1, LANES // (LANES - CARRY)))
    else:
        d_proj = share_parts(d_proj, "seq")
        square_sum = sum_everywhere(square_sum, ("seq",))
    d_normed, d_stream, small = call(
        lambda *refs: end_kernel(own, *refs),
        me,
        [(part, "t") for part in d_proj]
        + [
            (d_act, "t"),
            (conv_pre, "t"),
            (stream, "t"),
            (act, "t"),
            (d_gate, "x"),
            (vec, "f"),
            (xproj, "f"),
            (w_stream, "f"),
            (w_gate, "f"),
            (table, "f"),
        ],
        [
            ((seqs, rows, width), bf16, "x"),
            ((seqs, rows, chans), bf16, "x"),
            ((batches * packed, chans), f32, "f"),
        ],
        [
            pltpu.VMEM((ROWS + 8, chans), f32),
            pltpu.VMEM((chans, LANES), f32),
            pltpu.VMEM((LANES, chans), f32),
            pltpu.VMEM((chans, LANES), f32),
        ],
        total,
        rows,
        reverse=True,
    )
    stream_grad = t_dot(flat(normed), flat(d_stream))
    late = jnp.concatenate(
        [stream_grad.reshape(batches, lines, chans), small.reshape(batches, packed, chans)], axis=1
    )
    d_normed, late = lax.optimization_barrier((d_normed, late))
    late, square_sum, waiting = scatter_batch(late, square_sum)
    loss = (square_sum / (total_valid * width))[0, 0]
    nothing = waiting[0, :1].astype(f32) * 0.0
    gate_out = lax.all_to_all((gate_out + nothing).reshape(seqs, depth, chans), "seq", 0, 0)
    d_normed = [jnp.tile(nothing, (1, width // chans))] + scatter_parts(d_normed, "seq")
    stream_out = lax.all_to_all(late[:lines].reshape(seqs, depth, chans), "seq", 0, 0)
    in_out, gain_out, xproj_out, dt_out, alog_out, conv_out, convb_out, dtb_out, skip_out = join_columns(
        stream_out, gate_out, late[lines:], in_weight, norm_gain.astype(f32)[:, None], batches, own
    )
    d_normed = added(d_normed)
    mean_sq = jnp.mean(tok_f * tok_f, axis=-1, keepdims=True)
    root_inv = lax.rsqrt(mean_sq + 1e-05)
    own_unit = tok_f * root_inv
    scaled = d_normed * gain
    input_grad = d_result + root_inv * (scaled - own_unit * jnp.mean(scaled * own_unit, axis=-1, keepdims=True))
    return (
        output[None],
        loss,
        input_grad[None],
        gain_out[:, 0],
        in_out,
        conv_out,
        convb_out[0],
        xproj_out,
        dt_out,
        dtb_out[0],
        alog_out,
        skip_out[0],
        out_out,
    )


def solution(mesh):
    return jax.shard_map(
        body,
        mesh=mesh,
        in_specs=(
            P("batch", "seq", None),
            P("batch", "seq", None),
            P("batch", "seq"),
            P("batch", "seq"),
            P(("batch", "seq")),
            P(("batch", "seq"), None),
            P(None, ("batch", "seq")),
            P(("batch", "seq")),
            P(("batch", "seq"), None),
            P(None, ("batch", "seq")),
            P(("batch", "seq")),
            P(("batch", "seq"), None),
            P(("batch", "seq")),
            P(("batch", "seq"), None),
        ),
        out_specs=(
            P("batch", "seq", None),
            P(),
            P("batch", "seq", None),
            P(("batch", "seq")),
            P(("batch", "seq"), None),
            P(None, ("batch", "seq")),
            P(("batch", "seq")),
            P(("batch", "seq"), None),
            P(None, ("batch", "seq")),
            P(("batch", "seq")),
            P(("batch", "seq"), None),
            P(("batch", "seq")),
            P(("batch", "seq"), None),
        ),
        check_vma=False,
    )
```

```python
import jax
import jax.numpy as jnp
from jax import lax
from jax.experimental import pallas as pl
from jax.experimental.pallas import tpu as pltpu
from jax.sharding import PartitionSpec as P

PIECE = 256
BLOCK = 16
ROWS = 128
LOG2E = 1.4426950408889634
LN2 = 0.6931471805599453
NEVER = 1e9
LANES = 128
f32 = jnp.float32
bf16 = jnp.bfloat16

ALOG, CONV, CONVB, DTB, SKIP = 64, 80, 84, 85, 86
INTO, OUT, CARRY = 64, 80, 96


def dot(a, b):
    return jnp.dot(a, b, preferred_element_type=f32)


def dot_t(a, b):
    return lax.dot_general(a, b, (((1,), (1,)), ((), ())), preferred_element_type=f32)


def t_dot(a, b):
    return lax.dot_general(a, b, (((0,), (0,)), ((), ())), preferred_element_type=f32)


def sigmoid(v):
    return 1.0 / (1.0 + jnp.exp(-v))


def row_of(ref, t, n):
    return jnp.broadcast_to(ref[pl.ds(t, 1), :], (n, ref.shape[1]))


def col_of(block, tt, c):
    return jnp.broadcast_to(block[:, tt : tt + 1], (block.shape[0], c))


def rates_of(vec_ref, n):
    return -jnp.exp(vec_ref[ALOG : ALOG + n, :]) * LOG2E


def dt_of(proj, vec_ref, rank):
    low = proj[:, :rank].astype(bf16)
    return low, dot(low, vec_ref[:rank, :].astype(bf16)) + vec_ref[DTB : DTB + 1, :]


def softplus(v):
    return jnp.maximum(v, 0.0) + jnp.log1p(jnp.exp(-jnp.abs(v)))


def columns(proj_t, first, n, into_ref):
    for j in range(into_ref.shape[0]):
        into_ref[j] = proj_t[first : first + n, j * BLOCK : (j + 1) * BLOCK]


def block_diag(values, n):
    rows, wide = values.shape[0], BLOCK * n
    spread = (
        lax.broadcasted_iota(jnp.int32, (n, wide), 1) % n == lax.broadcasted_iota(jnp.int32, (n, wide), 0)
    ).astype(f32).astype(bf16)
    keep = lax.broadcasted_iota(jnp.int32, (rows, wide), 1) // n == lax.broadcasted_iota(
        jnp.int32, (rows, wide), 0
    ) % BLOCK
    return jnp.where(keep, dot(values, spread), 0.0).astype(bf16)


def unit_of(x):
    return x * lax.rsqrt(jnp.mean(x * x, axis=-1, keepdims=True) + 1e-05)


def start_kernel(me_ref, x_ref, *refs):
    parts = refs[:-14]
    (
        normed_ref, turned_ref, stream_ref, pre_ref, act_ref, proj_ref, w_ref, vec_ref, xproj_ref, gain_ref, marks_ref,
        wide_ref, ext_ref, cols_ref,
    ) = refs[-14:]
    rows, chans = stream_ref.shape
    taps = CONVB - CONV

    @pl.when(pl.program_id(0) == 0)
    def _():
        wide_ref[:8, :] = jnp.zeros((8, chans), f32)
        place = 1
        for part in parts:
            count, lines, _ = part.shape
            own = chans * lines // w_ref.shape[0]
            for k in range(count):
                block = me_ref[place]
                place += 1
                at = pl.ds(pl.multiple_of(block * lines, lines), lines)
                w_ref[at, :] = part[k, :, :chans]
                ext = part[k, :, chans:].astype(f32)
                ext_ref[at, :] = ext
                at = pl.ds(pl.multiple_of(block * own, own), own)
                cols_ref[at, :] = ext[:own]
                used = lax.broadcasted_iota(jnp.int32, (own, LANES), 1) < CARRY
                xproj_ref[at, :] = jnp.where(used, ext[own : 2 * own], 0.0).astype(bf16)
        for k in range(w_ref.shape[0] // LANES):
            at = slice(k * LANES, (k + 1) * LANES)
            gain_ref[:, at] = ext_ref[at, :].T[LANES - 3 : LANES - 2]
        for k in range(chans // LANES):
            at = slice(k * LANES, (k + 1) * LANES)
            vec_ref[:, at] = cols_ref[at, :].T
        marks_ref[...] = jnp.sum(ext_ref[...], axis=0, keepdims=True)

    normed = (unit_of(x_ref[...].astype(f32)) * gain_ref[...]).astype(bf16)
    normed_ref[...] = normed
    turned_ref[...] = normed.T
    stream = dot(normed, w_ref[...]).astype(bf16)
    stream_ref[...] = stream
    wide_ref[8:, :] = stream.astype(f32)
    pre = jnp.broadcast_to(vec_ref[CONVB : CONVB + 1, :], (rows, chans))
    for tap in range(taps):
        first = 8 - taps + 1 + tap
        pre = pre + vec_ref[CONV + tap : CONV + tap + 1, :] * wide_ref[first : first + rows, :]
    wide_ref[:8, :] = wide_ref[rows:, :]
    pre_ref[...] = pre
    act = (pre * sigmoid(pre)).astype(bf16)
    act_ref[...] = act
    proj_ref[...] = dot(act, xproj_ref[...]).astype(bf16)


def piece_kernel(me_ref, proj_ref, act_ref, vec_ref, g_ref, carry_ref, u_ref, stepm_ref, col_ref):
    rows, c = act_ref.shape
    n = carry_ref.shape[0]

    @pl.when(pl.program_id(0) == 0)
    def _():
        carry_ref[...] = jnp.zeros_like(carry_ref)

    proj = proj_ref[...]
    _, pre = dt_of(proj, vec_ref, INTO)
    step = softplus(pre)
    u_ref[...] = step * act_ref[...].astype(f32)
    stepm_ref[...] = jnp.where(proj[:, CARRY : CARRY + 1] > 0.5, step, NEVER)
    columns(proj.T, INTO, n, col_ref)
    r2 = rates_of(vec_ref, n)

    def block(i, carry):
        j = rows // BLOCK - 1 - i
        into = col_ref[j]
        for tt in reversed(range(BLOCK)):
            t = j * BLOCK + tt
            g = row_of(u_ref, t, n) * col_of(into, tt, c) + carry
            g_ref[pl.ds(pl.multiple_of(t * n, n), n), :] = g.astype(bf16)
            carry = jnp.exp2(row_of(stepm_ref, t, n) * r2) * g
        return carry

    carry_ref[...] = lax.fori_loop(0, rows // BLOCK, block, carry_ref[...])


def ahead_kernel(
    local, me_ref, proj_ref, act_ref, normed_ref, g_ref, vec_ref, second_ref,
    hp_ref, mixed_ref, gate_ref, gated_ref, wgate_ref, outw_ref,
    *refs,
):
    branch_refs = refs[:-7]
    carry_ref, u_ref, step_ref, col_ref, diag_ref, s_ref, y_ref = refs[-7:]
    rows, c = act_ref.shape
    n = carry_ref.shape[0]

    @pl.when(pl.program_id(0) == 0)
    def _():
        carry_ref[...] = jnp.zeros_like(carry_ref)
        blocks = second_ref.shape[0]
        lines, own = wgate_ref.shape[0] // blocks, outw_ref.shape[0] // blocks
        for b in range(blocks):
            wgate_ref[b * lines : (b + 1) * lines, :] = second_ref[b, :lines, :]
            for k in range(outw_ref.shape[1] // c):
                outw_ref[b * own : (b + 1) * own, k * c : (k + 1) * c] = second_ref[
                    b, lines + k * own : lines + (k + 1) * own, :
                ]

    proj = proj_ref[...]
    act = act_ref[...].astype(f32)
    _, pre = dt_of(proj, vec_ref, INTO)
    step = softplus(pre)
    step_ref[...] = step
    u_ref[...] = step * act
    columns(proj.T, INTO, n, col_ref)
    read = proj[:, OUT : OUT + n]
    high = read.astype(bf16)
    diag_ref[0, BLOCK:] = block_diag(high, n)
    diag_ref[1, BLOCK:] = block_diag((read - high.astype(f32)).astype(bf16), n)
    r2 = rates_of(vec_ref, n)

    def read_out(j):
        r16 = pl.ds(pl.multiple_of(j * BLOCK, BLOCK), BLOCK)
        both = dot(jnp.concatenate([diag_ref[0, r16, :], diag_ref[1, r16, :]], axis=0), s_ref[...])
        y_ref[r16, :] = both[:BLOCK] + both[BLOCK:]

    def block(j, h):
        read_out(j)
        into = col_ref[j]
        for tt in range(BLOCK):
            t = j * BLOCK + tt
            at = pl.ds(pl.multiple_of(t * n, n), n)
            hp = jnp.exp2(row_of(step_ref, t, n) * r2) * h
            h = hp + row_of(u_ref, t, n) * col_of(into, tt, c)
            hp_ref[at, :] = hp.astype(bf16)
            s_ref[tt * n : (tt + 1) * n, :] = (hp + g_ref[at, :].astype(f32)).astype(bf16)
        return h

    carry_ref[...] = lax.fori_loop(0, rows // BLOCK, block, carry_ref[...])
    read_out(rows // BLOCK)
    mixed = y_ref[BLOCK:] + vec_ref[SKIP : SKIP + 1, :] * act
    mixed_ref[...] = mixed
    gate = dot(normed_ref[...], wgate_ref[...])
    gate_ref[...] = gate
    gated = (mixed * (gate * sigmoid(gate))).astype(bf16)
    gated_ref[...] = gated.T
    write_slot(branch_refs, slot_of(me_ref, local), dot(gated, outw_ref[...]).astype(bf16))


def piece_grad_kernel(
    local, me_ref, proj_ref, act_ref, mixed_ref, gate_ref, vec_ref, outw_ref, *refs,
):
    db_refs = refs[:-7]
    q_ref, dm_ref, dg_ref, sgrad_ref, carry_ref, stepm_ref, col_ref = refs[-7:]
    rows, c = act_ref.shape
    n = carry_ref.shape[0]

    @pl.when(pl.program_id(0) == 0)
    def _():
        carry_ref[...] = jnp.zeros_like(carry_ref)
        sgrad_ref[...] = jnp.zeros_like(sgrad_ref)

    proj = proj_ref[...]
    _, pre = dt_of(proj, vec_ref, INTO)
    stepm_ref[...] = jnp.where(proj[:, CARRY : CARRY + 1] > 0.5, softplus(pre), NEVER)
    columns(proj.T, OUT, n, col_ref)
    dgated = dot_t(read_slot(db_refs, slot_of(me_ref, local)), outw_ref[...])
    gate = gate_ref[...]
    s = sigmoid(gate)
    dm = dgated * (gate * s)
    dm_ref[...] = dm
    dg = (dgated * mixed_ref[...] * (s * (1.0 + gate * (1.0 - s)))).astype(bf16)
    dg_ref[...] = dg
    sgrad_ref[...] += jnp.sum(dm * act_ref[...].astype(f32), axis=0, keepdims=True)
    r2 = rates_of(vec_ref, n)

    def block(j, w):
        read = col_ref[j]
        for tt in range(BLOCK):
            t = j * BLOCK + tt
            q = jnp.exp2(row_of(stepm_ref, t, n) * r2) * w
            q_ref[pl.ds(pl.multiple_of(t * n, n), n), :] = q.astype(bf16)
            w = q + row_of(dm_ref, t, n) * col_of(read, tt, c)
        return w

    carry_ref[...] = lax.fori_loop(0, rows // BLOCK, block, carry_ref[...])


def state_grad_kernel(
    me_ref, proj_ref, act_ref, dm_ref, g_ref, hp_ref, q_ref, vec_ref, sgrad_ref, pieces_ref,
    dact_ref, dproj_ref, table_ref,
    carry_ref, u_ref, step_ref, col_ref, diag_ref, ig_ref, rr_ref, rs_ref, pair_ref, own_ref, x_ref, y_ref, dp_ref,
):
    rows, c = act_ref.shape
    n = carry_ref.shape[0]
    wide = BLOCK * n

    @pl.when(pl.program_id(0) == 0)
    def _():
        carry_ref[...] = jnp.zeros_like(carry_ref)
        table_ref[...] = jnp.zeros_like(table_ref)
        table_ref[SKIP : SKIP + 1, :] = sgrad_ref[...]
        rs_ref[...] = jnp.zeros_like(rs_ref)

    proj = proj_ref[...]
    act = act_ref[...].astype(f32)
    low, pre = dt_of(proj, vec_ref, INTO)
    step = softplus(pre)
    step_ref[...] = step
    u_ref[...] = step * act
    columns(proj.T, OUT, n, col_ref)
    diag_ref[:rows] = block_diag(proj[:, INTO : INTO + n].astype(bf16), n)
    r2 = rates_of(vec_ref, n)
    iota = lambda shape, axis: lax.broadcasted_iota(jnp.int32, shape, axis)
    mask = lambda v: v.astype(f32).astype(bf16)
    by_row = mask(iota((BLOCK, wide), 1) // n == iota((BLOCK, wide), 0))
    by_state = mask(iota((n, wide), 1) % n == iota((n, wide), 0))
    part = min(c, 2 * LANES)
    which = mask(iota((2 * part, LANES), 0) // part == iota((2 * part, LANES), 1) // n % 2)
    own_lane = iota((wide, LANES), 1) % n == iota((wide, LANES), 0) % n

    def sums(j):
        r16 = pl.ds(pl.multiple_of(j * BLOCK, BLOCK), BLOCK)
        x_ref[r16, :] = dot(diag_ref[r16, :], ig_ref[...])
        y_ref[r16, :] = dot(by_row, rr_ref[...])
        table_ref[ALOG : ALOG + n, :] += dot(by_state, rs_ref[...])
        dp_ref[pl.ds(pl.multiple_of((j + 1) * BLOCK, BLOCK), BLOCK), :] = dot(by_row, own_ref[...])
        own_ref[...] = jnp.where(own_lane, dot(pair_ref[...], which), 0.0).astype(bf16)

    def block(i, m):
        j = rows // BLOCK - 1 - i
        sums(j + 1)
        read = col_ref[j]
        for tt in reversed(range(BLOCK)):
            t = j * BLOCK + tt
            at = pl.ds(pl.multiple_of(t * n, n), n)
            loc = slice(tt * n, (tt + 1) * n)
            drow = row_of(dm_ref, t, n)
            mu = m + drow * col_of(read, tt, c)
            srow = row_of(step_ref, t, n)
            m = jnp.exp2(srow * r2) * mu
            low_mu = mu.astype(bf16)
            q = q_ref[at, :]
            g = g_ref[at, :]
            hp = hp_ref[at, :]
            rg = low_mu * hp + q * g
            ig = low_mu + q
            ig_ref[loc, :] = ig
            rr_ref[loc, :] = (rg.astype(f32) * r2).astype(bf16)
            rs_ref[loc, :] = rg * srow.astype(bf16)
            pb = ig * row_of(u_ref, t, n).astype(bf16)
            pc = (hp + g) * drow.astype(bf16)
            sb, sc = pb[:, :part], pc[:, :part]
            for k in range(1, c // part):
                sb = sb + pb[:, k * part : (k + 1) * part]
                sc = sc + pc[:, k * part : (k + 1) * part]
            pair_ref[loc, :part] = sb
            pair_ref[loc, part:] = sc
        return m

    carry_ref[...] = lax.fori_loop(0, rows // BLOCK, block, carry_ref[...])
    sums(0)
    dp_ref[:BLOCK, :] = dot(by_row, own_ref[...])
    rs_ref[...] = jnp.zeros_like(rs_ref)
    xs = x_ref[:rows]
    dact_ref[...] = step_ref[...] * xs + vec_ref[SKIP : SKIP + 1, :] * dm_ref[...]
    dpre = (y_ref[:rows] * LN2 + act * xs) * sigmoid(pre)
    table_ref[DTB : DTB + 1, :] += jnp.sum(dpre, axis=0, keepdims=True)
    dpre_low = dpre.astype(bf16)
    table_ref[:INTO, :] += t_dot(low, dpre_low)
    dproj_ref[...] = dp_ref[:rows].astype(bf16)
    dproj_ref[:, :INTO] = dot_t(dpre_low, vec_ref[:INTO, :].astype(bf16)).astype(bf16)

    @pl.when(pl.program_id(0) == pl.num_programs(0) - 1)
    def _():
        dproj_ref[:BLOCK, CARRY:] = pieces_ref[:, CARRY:]
        table_ref[ALOG : ALOG + n, :] *= -jnp.exp(vec_ref[ALOG : ALOG + n, :])


def end_kernel(own, local, count, me_ref, *refs):
    dn_refs, refs = refs[-count - 8 : -8], refs[: -count - 8] + refs[-8:]
    parts = refs[:-18]
    (
        dact_ref, pre_ref, stream_ref, act_ref, dg_ref, vec_ref, xproj_ref, ws_ref, wg_ref, table_ref,
        ds_ref, small_ref, pieces_ref, sum_ref,
        wide_ref, xgrad_ref, cgrad_ref, turned_ref,
    ) = refs[-18:]
    rows, c = act_ref.shape
    taps = CONVB - CONV

    @pl.when(pl.program_id(0) == 0)
    def _():
        wide_ref[rows:, :] = jnp.zeros((8, c), f32)
        xgrad_ref[...] = jnp.zeros_like(xgrad_ref)
        cgrad_ref[...] = table_ref[...]

    dproj = parts[0][...].astype(f32)
    for part in parts[1:]:
        dproj = dproj + part[...].astype(f32)
    used = lax.broadcasted_iota(jnp.int32, dproj.shape, 1) < CARRY
    dproj = jnp.where(used, dproj, 0.0).astype(bf16)
    pre = pre_ref[...]
    s = sigmoid(pre)
    dconv = (dact_ref[...] + dot_t(dproj, xproj_ref[...])) * (s * (1.0 + pre * (1.0 - s)))
    wide_ref[:rows, :] = dconv
    xgrad_ref[...] += t_dot(act_ref[...], dproj)
    cgrad_ref[CONVB : CONVB + 1, :] += jnp.sum(dconv, axis=0, keepdims=True)
    stream = stream_ref[...].astype(f32)
    dstream = jnp.zeros((rows, c), f32)
    for tap in range(taps):
        back = taps - 1 - tap
        moved = wide_ref[back : back + rows, :]
        cgrad_ref[CONV + tap : CONV + tap + 1, :] += jnp.sum(stream * moved, axis=0, keepdims=True)
        dstream = dstream + vec_ref[CONV + tap : CONV + tap + 1, :] * moved
    wide_ref[rows:, :] = dconv[:8, :]
    dstream_low = dstream.astype(bf16)
    dn = (dot_t(dstream_low, ws_ref[...]) + dot_t(dg_ref[...], wg_ref[...])).astype(bf16)
    write_slot(dn_refs, slot_of(me_ref, local, True), dn)
    ds_ref[...] = dstream_low

    @pl.when(pl.program_id(0) == pl.num_programs(0) - 1)
    def _():
        for k in range(c // LANES):
            at = slice(k * LANES, (k + 1) * LANES)
            turned_ref[at, :] = cgrad_ref[:, at].T
        sums = tree([row_sum(part[:BLOCK, :]) for part in parts])
        sums = jnp.where(lax.broadcasted_iota(jnp.int32, sums.shape, 1) < CARRY, 0.0, sums)
        sum_ref[...] = sums
        pieces = [jnp.zeros((BLOCK, LANES), f32)]
        row = lax.broadcasted_iota(jnp.int32, (BLOCK, LANES), 0)
        for k in range(3):
            term = sums.astype(bf16).astype(f32)
            pieces = [jnp.where(row == k, term, pieces[0])]
            sums = sums - term
        for k in range(c // LANES):
            pieces_ref[:, k * LANES : (k + 1) * LANES] = pieces[0].astype(bf16)
        lines = 2 * own * LANES // c
        for b in range(c // own):
            at = slice(b * own, (b + 1) * own)
            both = jnp.concatenate([xgrad_ref[at, :], turned_ref[at, :]], axis=0)
            for k in range(c // LANES):
                small_ref[b * lines : (b + 1) * lines, k * LANES : (k + 1) * LANES] = both[k * lines : (k + 1) * lines]


def slot_of(me_ref, local, reverse=False):
    step = pl.program_id(0)
    if reverse:
        step = pl.num_programs(0) - 1 - step
    return (step // (local // ROWS)) ^ me_ref[0]


def read_slot(refs, slot):
    value = refs[0][...]
    for k in range(1, len(refs)):
        value = jnp.where(slot == k, refs[k][...], value)
    return value


def write_slot(refs, slot, value):
    if len(refs) == 1:
        refs[0][...] = value
        return
    for k, ref in enumerate(refs):

        @pl.when(slot == k)
        def _(ref=ref):
            ref[...] = value


def call(kernel, me, ins, outs, scratch, total, local, reverse=False):
    steps = total // ROWS
    per = local // ROWS
    turn = (lambda i: steps - 1 - i) if reverse else (lambda i: i)

    def slot_map(k):
        def index(i, me_ref):
            group = k ^ me_ref[0]
            if reverse:
                group = steps // per - 1 - group
            first, last = (per - 1, 0) if reverse else (0, per - 1)
            now = i // per
            return (jnp.where(now < group, first, jnp.where(now > group, last, turn(i) % per)), 0)

        return index

    def spec(shape, kind):
        if isinstance(kind, int):
            return pl.BlockSpec((ROWS, shape[1]), slot_map(kind))
        if kind == "f":
            return pl.BlockSpec(shape, lambda i, me_ref: (0,) * len(shape))
        if kind == "c":
            return pl.BlockSpec(
                (shape[0], ROWS), lambda i, me_ref: (0, ((turn(i) // per) ^ me_ref[0]) * per + turn(i) % per)
            )
        if kind == "y":
            return pl.BlockSpec((None, ROWS, shape[2]), lambda i, me_ref: (turn(i) // per, turn(i) % per, 0))
        if kind == "x":
            return pl.BlockSpec(
                (None, ROWS, shape[2]), lambda i, me_ref: ((turn(i) // per) ^ me_ref[0], turn(i) % per, 0)
            )
        return pl.BlockSpec((shape[0] // steps, shape[1]), lambda i, me_ref: (turn(i), 0))

    return pl.pallas_call(
        kernel,
        out_shape=[jax.ShapeDtypeStruct(s, d) for s, d, _ in outs],
        grid_spec=pltpu.PrefetchScalarGridSpec(
            num_scalar_prefetch=1,
            grid=(steps,),
            in_specs=[spec(a.shape, k) for a, k in ins],
            out_specs=[spec(s, k) for s, _, k in outs],
            scratch_shapes=scratch,
        ),
        compiler_params=pltpu.CompilerParams(dimension_semantics=("arbitrary",), vmem_limit_bytes=60 << 20),
    )(me, *[a for a, _ in ins])


def slots_in(parts):
    if len(parts) == 1:
        return [(parts[0], "x")]
    return [(part, k) for k, part in enumerate(parts)]


def slots_out(seqs, rows, width):
    if seqs > 4:
        return [((seqs, rows, width), bf16, "x")]
    return [((rows, width), bf16, k) for k in range(seqs)]


def early_grad_kernel(normed_ref, gated_ref, dg_ref, *refs):
    parts, out_ref = refs[:-1], refs[-1]
    group, _, c = out_ref.shape
    lines, own = normed_ref.shape[0] // group, gated_ref.shape[0] // group
    gate = dot(normed_ref[...], dg_ref[...])
    out, first = 0.0, 0
    for part in parts:
        last = first + part.shape[0]
        out = out + dot(gated_ref[:, first:last], part[...])
        first = last
    for b in range(group):
        out_ref[b, :lines, :] = gate[b * lines : (b + 1) * lines]
        for k in range(out.shape[1] // c):
            out_ref[b, lines + k * own : lines + (k + 1) * own, :] = out[
                b * own : (b + 1) * own, k * c : (k + 1) * c
            ]


def late_grad_kernel(normed_ref, small_ref, ds_ref, out_ref):
    group, rows, c = out_ref.shape
    lines = normed_ref.shape[0] // group
    packed = rows - lines
    stream = dot(normed_ref[...], ds_ref[...])
    for b in range(group):
        out_ref[b, :lines, :] = stream[b * lines : (b + 1) * lines]
        out_ref[b, lines:, :] = small_ref[b * packed : (b + 1) * packed, :]


def late_pair_kernel(me_ref, normed_ref, small_ref, ds_ref, pieces_ref, mine_ref, theirs_ref):
    rows = mine_ref.shape[1]
    lines = normed_ref.shape[0] // 2
    packed = rows - lines
    stream = dot(normed_ref[...], ds_ref[...])
    small = small_ref[...]
    first = me_ref[0] == 0
    mine_ref[0, :lines, :] = jnp.where(first, stream[:lines], stream[lines:])
    mine_ref[0, lines:, :] = jnp.where(first, small[:packed], small[packed:])
    theirs_ref[0, :lines, :] = jnp.where(first, stream[lines:], stream[:lines]).astype(bf16)
    theirs_ref[0, lines:rows, :] = jnp.where(first, small[packed:], small[:packed]).astype(bf16)
    theirs_ref[0, rows:, :] = pieces_ref[...]


def late_pairs(normed_t, small, ds, pieces, batches, rows, chans):
    steps = batches // 2
    whole = lambda a: pl.BlockSpec(a.shape, lambda i, me_ref: (0, 0))
    cut = lambda a: pl.BlockSpec((a.shape[0] // steps, a.shape[1]), lambda i, me_ref: (i, 0))
    block = lambda r: pl.BlockSpec((1, r, chans), lambda i, me_ref: (i, 0, 0))
    return pl.pallas_call(
        late_pair_kernel,
        out_shape=[
            jax.ShapeDtypeStruct((steps, rows, chans), f32),
            jax.ShapeDtypeStruct((steps, rows + BLOCK, chans), bf16),
        ],
        grid_spec=pltpu.PrefetchScalarGridSpec(
            num_scalar_prefetch=1,
            grid=(steps,),
            in_specs=[cut(normed_t), cut(small), whole(ds), whole(pieces)],
            out_specs=[block(rows), block(rows + BLOCK)],
        ),
        compiler_params=pltpu.CompilerParams(dimension_semantics=("arbitrary",), vmem_limit_bytes=60 << 20),
    )((lax.axis_index("batch") % 2).astype(jnp.int32).reshape(1), normed_t, small, ds, pieces)


def by_blocks(kernel, batches, own, columns, whole, rows, chans):
    group = LANES // own
    steps = batches // group

    def spec(array, cut):
        if cut:
            return pl.BlockSpec((array.shape[0] // steps, array.shape[1]), lambda i: (i, 0))
        return pl.BlockSpec(array.shape, lambda i: (0,) * array.ndim)

    return pl.pallas_call(
        kernel,
        out_shape=jax.ShapeDtypeStruct((batches, rows, chans), f32),
        grid=(steps,),
        in_specs=[spec(a, True) for a in columns] + [spec(a, False) for a in whole],
        out_specs=pl.BlockSpec((group, rows, chans), lambda i: (i, 0, 0)),
        compiler_params=pltpu.CompilerParams(dimension_semantics=("arbitrary",), vmem_limit_bytes=60 << 20),
    )(*columns, *whole)


def split_kernel(seqs, batches, own, w_ref, gain_ref, valid_ref, out_ref):
    depth, half, chans = w_ref.shape[0], w_ref.shape[1] // 2, batches * own
    count = jnp.sum(valid_ref[...].astype(f32), keepdims=True)
    high = jnp.floor(count * (1.0 / 128.0))
    iota = lambda shape, axis: lax.broadcasted_iota(jnp.int32, shape, axis)
    gain = jnp.broadcast_to(gain_ref[...].astype(f32), (depth, depth))
    gain = jnp.where(iota((depth, depth), 0) == iota((depth, depth), 1), gain, 0.0)
    gain = jnp.sum(gain, axis=1, keepdims=True)
    lane = iota((depth, LANES), 1)
    extra = jnp.where(lane == LANES - 3, gain, 0.0)
    extra = jnp.where(lane == LANES - 2, high, extra)
    extra = jnp.where(lane == LANES - 1, count - high * 128.0, extra).astype(bf16)
    for s in range(seqs):
        for k in range(2):
            pieces = [
                w_ref[:, k * half + (b * seqs + s) * own : k * half + (b * seqs + s + 1) * own].astype(f32)
                for b in range(batches)
            ]
            first = k * (chans + LANES)
            out_ref[s, :, first : first + chans] = jnp.concatenate(pieces, axis=1).astype(bf16)
        out_ref[s, :, chans : chans + LANES] = extra


def split_columns(weight, gain, valid, seqs, batches, own):
    shape = jax.ShapeDtypeStruct((seqs, weight.shape[0], 2 * batches * own + LANES), bf16)
    return pl.pallas_call(lambda *refs: split_kernel(seqs, batches, own, *refs), out_shape=shape)(weight, gain, valid)


def join_kernel(
    batches, both_ref, small_ref, w_ref, gain_ref,
    out_ref, gain_out_ref, xproj_ref, dt_ref, alog_ref, conv_ref, convb_ref, dtb_ref, skip_ref,
):
    seqs, half = both_ref.shape[0], w_ref.shape[1] // 2
    chans = half // seqs
    own = chans // batches
    for k in range(2):
        whole = [both_ref[s, :, k * chans : (k + 1) * chans].astype(f32) for s in range(seqs)]
        pieces = [whole[s][:, b * own : (b + 1) * own] for b in range(batches) for s in range(seqs)]
        out_ref[:, k * half : (k + 1) * half] = jnp.concatenate(pieces, axis=1)
    products = out_ref[...] * w_ref[...].astype(f32)
    depth = products.shape[0]
    sums = jnp.broadcast_to(jnp.sum(products, axis=1, keepdims=True), (depth, depth))
    eye = lax.broadcasted_iota(jnp.int32, (depth, depth), 0) == lax.broadcasted_iota(jnp.int32, (depth, depth), 1)
    gain_out_ref[...] = jnp.sum(jnp.where(eye, sums, 0.0), axis=0, keepdims=True) / gain_ref[...].astype(f32)
    small = small_ref[...]
    both = jnp.concatenate([small[:, k : k + LANES] for k in range(0, chans, LANES)], axis=0)
    xproj_ref[...] = both[:own, :CARRY]
    table = both[own:]
    alog_ref[...] = table[:, ALOG:CONV]
    table = jnp.concatenate([table, jnp.zeros((LANES - own, LANES), f32)], axis=0).T[:, :own]
    dt_ref[...] = table[:INTO]
    conv_ref[...] = table[CONV:CONVB]
    convb_ref[...] = table[CONVB : CONVB + 1]
    dtb_ref[...] = table[DTB : DTB + 1]
    skip_ref[...] = table[SKIP : SKIP + 1]


def join_columns(both, small, weight, gain, batches, own):
    depth = weight.shape[0]
    shapes = [weight.shape, (1, depth), (own, CARRY), (INTO, own), (own, CONV - ALOG), (CONVB - CONV, own)]
    shapes += [(1, own)] * 3
    return pl.pallas_call(
        lambda *refs: join_kernel(batches, *refs), out_shape=[jax.ShapeDtypeStruct(s, f32) for s in shapes]
    )(both, small, weight, gain)


def partner(value, axis, k):
    return lax.ppermute(value, axis, [(i, i ^ k) for i in range(lax.axis_size(axis))])


def gather_parts(value, axis):
    n = lax.axis_size(axis)
    if n > 4:
        return [lax.all_gather(value, axis)]
    return [value] + [partner(value, axis, k) for k in range(1, n)]


def gather_batch(value, after):
    n = lax.axis_size("batch")
    if n > 8:
        return [lax.all_gather(value, "batch")], [jnp.int32(k) for k in range(n)], after
    me = lax.axis_index("batch")
    chips = jnp.stack([value] + [partner(value, "batch", 2 * k) for k in range(1, n // 2)])
    other = partner(chips, "batch", 1)
    places = [me ^ (2 * k) for k in range(n // 2)] + [me ^ (2 * k + 1) for k in range(n // 2)]
    return [chips, other], places, after


def exact(total, rows):
    terms = []
    for _ in range(3):
        term = lax.reduce_precision(total, 8, 7)
        terms.append(term)
        total = total - term
    return jnp.concatenate(terms + [jnp.zeros((rows - 3, total.shape[1]), f32)], axis=0).astype(bf16)


def row_sum(rows):
    a = rows[:3].astype(f32)
    return (a[:1] + a[1:2]) + a[2:]


def tree(values):
    while len(values) > 1:
        values = [a + b for a, b in zip(values[::2], values[1::2])]
    return values[0]


def scatter_batch(mine, theirs, total):
    n = lax.axis_size("batch")
    me = lax.axis_index("batch")
    rows, c = mine.shape[1:]
    got = partner(theirs, "batch", 1)
    mine = mine + got[:, :rows].astype(f32)
    total = row_sum(exact(total, BLOCK)) + row_sum(got[0, rows:, :LANES])
    pieces = exact(jnp.tile(total, (1, c // LANES)), BLOCK)
    low = jnp.concatenate([mine.astype(bf16), jnp.broadcast_to(pieces[None], (n // 2, BLOCK, c))], axis=1)
    got = [
        partner(lax.dynamic_index_in_dim(low, (me // 2) ^ k, 0, False), "batch", 2 * k) for k in range(1, n // 2)
    ]
    result = lax.dynamic_index_in_dim(mine, me // 2, 0, False)
    for part in got:
        result = result + part[:rows].astype(f32)
    return result, tree([row_sum(exact(total, BLOCK))] + [row_sum(part[rows:, :LANES]) for part in got]), low


def scatter_parts(values, axis):
    n = lax.axis_size(axis)
    if n > 4:
        return [lax.psum_scatter(values[0].astype(f32), axis, scatter_dimension=0)]
    return [values[0]] + [partner(values[k], axis, k) for k in range(1, n)]


def share_parts(value, axis):
    n = lax.axis_size(axis)
    if n > 4:
        return [lax.psum(value.astype(f32), axis)]
    return [value] + [partner(value, axis, k) for k in range(1, n)]


def added(parts):
    total = parts[0].astype(f32)
    for part in parts[1:]:
        total = total + part.astype(f32)
    return total


def sum_everywhere(value, axes):
    for axis in axes:
        k = 1
        while k < lax.axis_size(axis):
            value = value + partner(value, axis, k)
            k *= 2
    return value


def body(
    tokens,
    teacher,
    piece_starts,
    valid_rows,
    norm_gain,
    in_weight,
    conv_weight,
    conv_bias,
    xproj_weight,
    dtproj_weight,
    dt_bias,
    a_log,
    skip_weight,
    out_weight,
):
    seqs = lax.axis_size("seq")
    batches = lax.axis_size("batch")
    _, rows, width = tokens.shape
    total = rows * seqs
    taps, own = conv_weight.shape
    chans = own * batches
    depth = in_weight.shape[0]
    rank = dtproj_weight.shape[0]
    states = a_log.shape[1]
    lines = depth * seqs
    packed = 2 * LANES * own // chans
    place = lax.axis_index("seq") if seqs <= 4 else jnp.int32(0)
    me = place.astype(jnp.int32).reshape(1)
    tok = tokens.reshape(rows, width)

    flags = jnp.pad(piece_starts.astype(bf16), ((0, 15), (0, width - rows)))
    everything = lax.all_gather(jnp.concatenate([tok, flags], axis=0), "seq")
    split = split_columns(in_weight, norm_gain.reshape(1, depth), valid_rows, seqs, batches, own)
    split = lax.all_to_all(split, "seq", 0, 0).reshape(lines, 2 * chans + LANES)
    vectors = jnp.concatenate(
        [
            dtproj_weight.T,
            a_log,
            conv_weight.T,
            conv_bias[:, None],
            dt_bias[:, None],
            skip_weight[:, None],
        ],
        axis=1,
    )
    vectors = jnp.pad(vectors, ((0, 0), (0, LANES - vectors.shape[1])))
    columns_x = jnp.pad(xproj_weight, ((0, 0), (0, LANES - xproj_weight.shape[1])))
    local = jnp.pad(jnp.concatenate([vectors, columns_x], axis=0), ((0, lines - 2 * own), (chans, 0)))
    second = jnp.concatenate(
        [split[:, chans + LANES :]] + [out_weight[:, k : k + chans] for k in range(0, width, chans)], axis=0
    )
    blocks, places, second = gather_batch(split[:, : chans + LANES] + local, second)
    second = lax.all_gather(second, "batch")


    tile = ((total, chans), f32, "t")
    low_tile = ((total, chans), bf16, "t")
    state = ((total * states, chans), bf16, "t")
    normed, normed_t, stream, conv_pre, act, proj, w_stream, vec, xproj, gain, marks = call(
        start_kernel,
        jnp.concatenate([me] + [p.astype(jnp.int32).reshape(1) for p in places]),
        [(everything, "y")] + [(block, "f") for block in blocks],
        [
            ((seqs, rows, width), bf16, "x"),
            ((width, total), bf16, "c"),
            low_tile,
            tile,
            low_tile,
            ((total, LANES), bf16, "t"),
            ((width, chans), bf16, "f"),
            ((LANES, chans), f32, "f"),
            ((chans, LANES), bf16, "f"),
            ((1, width), f32, "f"),
            ((1, LANES), f32, "f"),
        ],
        [pltpu.VMEM((ROWS + 8, chans), f32), pltpu.VMEM((width, LANES), f32), pltpu.VMEM((chans, LANES), f32)],
        total,
        rows,
    )
    total_valid = (marks[:, LANES - 2 : LANES - 1] * 128.0 + marks[:, LANES - 1 :]) / depth
    starts = everything[:, rows, :rows].astype(f32).reshape(total)
    running = jnp.cumsum(starts)
    lagged = jnp.concatenate([jnp.zeros((PIECE,), f32), running[: total - PIECE]])
    carry_on = jnp.where(running - lagged > 0.5, 1.0 - starts, 0.0)
    proj = added(share_parts(proj, "seq"))
    proj = jnp.where(jnp.arange(LANES)[None, :] == CARRY, carry_on[:, None], proj)
    groups = (ROWS // BLOCK, states, BLOCK)
    (g,) = call(
        piece_kernel,
        me,
        [(proj, "t"), (act, "t"), (vec, "f")],
        [state],
        [
            pltpu.VMEM((states, chans), f32),
            pltpu.VMEM((ROWS, chans), f32),
            pltpu.VMEM((ROWS, chans), f32),
            pltpu.VMEM(groups, f32),
        ],
        total,
        rows,
        reverse=True,
    )
    hp, mixed, gate, gated_t, w_gate, out_w, *branch = call(
        lambda *refs: ahead_kernel(rows, *refs),
        me,
        [(proj, "t"), (act, "t"), (normed, "x"), (g, "t"), (vec, "f"), (second, "f")],
        [
            state,
            tile,
            tile,
            ((chans, total), bf16, "c"),
            ((width, chans), bf16, "f"),
            ((chans, width), bf16, "f"),
        ]
        + slots_out(seqs, rows, width),
        [
            pltpu.VMEM((states, chans), f32),
            pltpu.VMEM((ROWS, chans), f32),
            pltpu.VMEM((ROWS, chans), f32),
            pltpu.VMEM(groups, f32),
            pltpu.VMEM((2, ROWS + BLOCK, BLOCK * states), bf16),
            pltpu.VMEM((BLOCK * states, chans), bf16),
            pltpu.VMEM((ROWS + BLOCK, chans), f32),
        ],
        total,
        rows,
    )
    tok_f = tok.astype(f32)
    valid_f = valid_rows.reshape(rows, 1).astype(f32)
    result = tok_f + added(scatter_parts(branch, "seq"))
    output = result.astype(bf16)
    misfit = result - teacher.reshape(rows, width).astype(f32)
    squares = jnp.sum(valid_f * misfit * misfit, axis=0, keepdims=True)
    part = LANES - CARRY
    square_sum = squares[:, :LANES]
    for k in range(LANES, width, LANES):
        square_sum = square_sum + squares[:, k : k + LANES]
    square_sum = sum(square_sum[:, k : k + part] for k in range(0, LANES, part))
    square_sum = jnp.pad(square_sum, ((0, 0), (CARRY, 0)))
    d_result = 2.0 * (total * batches) / total_valid * valid_f * misfit

    d_branch = gather_parts(d_result.astype(bf16), "seq")
    q, d_mixed, d_gate, skip_grad = call(
        lambda *refs: piece_grad_kernel(rows, *refs),
        me,
        [
            (proj, "t"),
            (act, "t"),
            (mixed, "t"),
            (gate, "t"),
            (vec, "f"),
            (out_w, "f"),
        ]
        + slots_in(d_branch),
        [state, tile, ((seqs, rows, chans), bf16, "x"), ((1, chans), f32, "f")],
        [pltpu.VMEM((states, chans), f32), pltpu.VMEM((ROWS, chans), f32), pltpu.VMEM(groups, f32)],
        total,
        rows,
    )
    flat = lambda v: v.reshape(total, v.shape[2])
    branches = d_branch if seqs <= 4 else [flat(d_branch[0])]
    early_sum = by_blocks(
        early_grad_kernel,
        batches,
        own,
        [normed_t, gated_t],
        [flat(d_gate)] + branches,
        lines + own * width // chans,
        chans,
    )
    early = lax.psum_scatter(early_sum, "batch", scatter_dimension=0)
    pieces = exact(square_sum, BLOCK)
    d_act, d_proj, table = call(
        state_grad_kernel,
        me,
        [(proj, "t"), (act, "t"), (d_mixed, "t"), (g, "t"), (hp, "t"), (q, "t"), (vec, "f"), (skip_grad, "f"), (pieces, "f")],
        [tile, ((total, LANES), bf16, "t"), ((LANES, chans), f32, "f")],
        [
            pltpu.VMEM((states, chans), f32),
            pltpu.VMEM((ROWS, chans), f32),
            pltpu.VMEM((ROWS, chans), f32),
            pltpu.VMEM(groups, f32),
            pltpu.VMEM((ROWS + BLOCK, BLOCK * states), bf16),
        ]
        + [pltpu.VMEM((BLOCK * states, chans), bf16)] * 3
        + [
            pltpu.VMEM((BLOCK * states, 2 * min(chans, 2 * LANES)), bf16),
            pltpu.VMEM((BLOCK * states, LANES), bf16),
        ]
        + [pltpu.VMEM((ROWS + 2 * BLOCK, chans), f32)] * 2
        + [pltpu.VMEM((ROWS + 2 * BLOCK, LANES), f32)],
        total,
        rows,
        reverse=True,
    )
    d_proj = share_parts(d_proj, "seq")
    slots = slots_out(seqs, rows, width)
    *d_normed, d_stream, small, sent, seq_sum = call(
        lambda *refs: end_kernel(own, rows, len(slots), *refs),
        me,
        [(part, "t") for part in d_proj]
        + [
            (d_act, "t"),
            (conv_pre, "t"),
            (stream, "t"),
            (act, "t"),
            (d_gate, "x"),
            (vec, "f"),
            (xproj, "f"),
            (w_stream, "f"),
            (w_gate, "f"),
            (table, "f"),
        ],
        slots
        + [
            ((seqs, rows, chans), bf16, "x"),
            ((batches * packed, chans), f32, "f"),
            ((BLOCK, chans), bf16, "f"),
            ((1, LANES), f32, "f"),
        ],
        [
            pltpu.VMEM((ROWS + 8, chans), f32),
            pltpu.VMEM((chans, LANES), f32),
            pltpu.VMEM((LANES, chans), f32),
            pltpu.VMEM((chans, LANES), f32),
        ],
        total,
        rows,
        reverse=True,
    )
    if batches <= 8:
        mine, theirs = late_pairs(normed_t, small, flat(d_stream), sent, batches, lines + packed, chans)
        late, square_sum, waiting = scatter_batch(mine, theirs, seq_sum)
    else:
        late = by_blocks(
            late_grad_kernel, batches, own, [normed_t, small], [flat(d_stream)], lines + packed, chans
        )
        waiting = late
        late = lax.psum_scatter(late, "batch", scatter_dimension=0)
        square_sum = sum_everywhere(square_sum, ("batch", "seq"))
    loss = jnp.sum(square_sum) / (total_valid * width)[0, 0]
    nothing = waiting[0, :1].astype(f32) * 0.0
    d_normed = added([jnp.tile(nothing, (1, width // chans))] + scatter_parts(d_normed, "seq"))
    in_out = jnp.concatenate([late[:lines], early[:lines]], axis=1).astype(bf16)
    in_out = lax.all_to_all(in_out.reshape(seqs, depth, 2 * chans), "seq", 0, 0)
    in_out, gain_out, xproj_out, dt_out, alog_out, conv_out, convb_out, dtb_out, skip_out = join_columns(
        in_out, late[lines:], in_weight, norm_gain.reshape(1, depth), batches, own
    )
    out_out = early[lines:].reshape(-1, own, chans).transpose(1, 0, 2).reshape(own, width)
    mean_sq = jnp.mean(tok_f * tok_f, axis=-1, keepdims=True)
    root_inv = lax.rsqrt(mean_sq + 1e-05)
    own_unit = tok_f * root_inv
    scaled = d_normed * gain
    input_grad = d_result + root_inv * (scaled - own_unit * jnp.mean(scaled * own_unit, axis=-1, keepdims=True))
    return (
        output[None],
        loss,
        input_grad[None],
        gain_out[0],
        in_out,
        conv_out,
        convb_out[0],
        xproj_out,
        dt_out,
        dtb_out[0],
        alog_out,
        skip_out[0],
        out_out,
    )


def solution(mesh):
    return jax.shard_map(
        body,
        mesh=mesh,
        in_specs=(
            P("batch", "seq", None),
            P("batch", "seq", None),
            P("batch", "seq"),
            P("batch", "seq"),
            P(("batch", "seq")),
            P(("batch", "seq"), None),
            P(None, ("batch", "seq")),
            P(("batch", "seq")),
            P(("batch", "seq"), None),
            P(None, ("batch", "seq")),
            P(("batch", "seq")),
            P(("batch", "seq"), None),
            P(("batch", "seq")),
            P(("batch", "seq"), None),
        ),
        out_specs=(
            P("batch", "seq", None),
            P(),
            P("batch", "seq", None),
            P(("batch", "seq")),
            P(("batch", "seq"), None),
            P(None, ("batch", "seq")),
            P(("batch", "seq")),
            P(("batch", "seq"), None),
            P(None, ("batch", "seq")),
            P(("batch", "seq")),
            P(("batch", "seq"), None),
            P(("batch", "seq")),
            P(("batch", "seq"), None),
        ),
        check_vma=False,
    )
```

```python
import jax
import jax.numpy as jnp
from jax import lax
from jax.experimental import pallas as pl
from jax.experimental.pallas import tpu as pltpu
from jax.sharding import PartitionSpec as P

PIECE = 256
BLOCK = 16
ROWS = 256
HALF = 128
LOG2E = 1.4426950408889634
LN2 = 0.6931471805599453
NEVER = 1e9
LANES = 128
f32 = jnp.float32
bf16 = jnp.bfloat16

ALOG, CONV, CONVB, DTB, SKIP = 64, 80, 84, 85, 86
INTO, OUT, CARRY = 64, 80, 96


def dot(a, b):
    return jnp.dot(a, b, preferred_element_type=f32)


def dot_t(a, b):
    return lax.dot_general(a, b, (((1,), (1,)), ((), ())), preferred_element_type=f32)


def t_dot(a, b):
    return lax.dot_general(a, b, (((0,), (0,)), ((), ())), preferred_element_type=f32)


def sigmoid(v):
    return 1.0 / (1.0 + jnp.exp(-v))


def row_of(ref, t, n):
    return jnp.broadcast_to(ref[pl.ds(t, 1), :], (n, ref.shape[1]))


def col_of(block, tt, c):
    return jnp.broadcast_to(block[:, tt : tt + 1], (block.shape[0], c))


def rates_of(vec_ref, n):
    return -jnp.exp(vec_ref[ALOG : ALOG + n, :]) * LOG2E


def dt_of(proj, vec_ref, rank):
    low = proj[:, :rank].astype(bf16)
    return low, dot(low, vec_ref[:rank, :].astype(bf16)) + vec_ref[DTB : DTB + 1, :]


def softplus(v):
    return jnp.maximum(v, 0.0) + jnp.log1p(jnp.exp(-jnp.abs(v)))


def columns(proj_t, first, n, into_ref):
    for j in range(into_ref.shape[0]):
        into_ref[j] = proj_t[first : first + n, j * BLOCK : (j + 1) * BLOCK]


def block_diag(values, n):
    rows, wide = values.shape[0], BLOCK * n
    spread = (
        lax.broadcasted_iota(jnp.int32, (n, wide), 1) % n == lax.broadcasted_iota(jnp.int32, (n, wide), 0)
    ).astype(f32).astype(bf16)
    keep = lax.broadcasted_iota(jnp.int32, (rows, wide), 1) // n == lax.broadcasted_iota(
        jnp.int32, (rows, wide), 0
    ) % BLOCK
    return jnp.where(keep, dot(values, spread), 0.0).astype(bf16)


def unit_of(x):
    return x * lax.rsqrt(jnp.mean(x * x, axis=-1, keepdims=True) + 1e-05)


def start_kernel(me_ref, x_ref, *refs):
    parts = refs[:-14]
    (
        normed_ref, turned_ref, stream_ref, pre_ref, act_ref, proj_ref, w_ref, vec_ref, xproj_ref, gain_ref, marks_ref,
        wide_ref, ext_ref, cols_ref,
    ) = refs[-14:]
    rows, chans = stream_ref.shape
    taps = CONVB - CONV

    @pl.when(pl.program_id(0) == 0)
    def _():
        wide_ref[:8, :] = jnp.zeros((8, chans), f32)
        place = 1
        for part in parts:
            count, lines, _ = part.shape
            own = chans * lines // w_ref.shape[0]
            for k in range(count):
                block = me_ref[place]
                place += 1
                at = pl.ds(pl.multiple_of(block * lines, lines), lines)
                w_ref[at, :] = part[k, :, :chans]
                ext = part[k, :, chans:].astype(f32)
                ext_ref[at, :] = ext
                at = pl.ds(pl.multiple_of(block * own, own), own)
                cols_ref[at, :] = ext[:own]
                used = lax.broadcasted_iota(jnp.int32, (own, LANES), 1) < CARRY
                xproj_ref[at, :] = jnp.where(used, ext[own : 2 * own], 0.0).astype(bf16)
        for k in range(w_ref.shape[0] // LANES):
            at = slice(k * LANES, (k + 1) * LANES)
            gain_ref[:, at] = ext_ref[at, :].T[LANES - 3 : LANES - 2]
        for k in range(chans // LANES):
            at = slice(k * LANES, (k + 1) * LANES)
            vec_ref[:, at] = cols_ref[at, :].T
        marks_ref[...] = jnp.sum(ext_ref[...], axis=0, keepdims=True)

    normed = (unit_of(x_ref[...].astype(f32)) * gain_ref[...]).astype(bf16)
    normed_ref[...] = normed
    turned_ref[...] = normed.T
    stream = dot(normed, w_ref[...]).astype(bf16)
    stream_ref[...] = stream
    wide_ref[8:, :] = stream.astype(f32)
    pre = jnp.broadcast_to(vec_ref[CONVB : CONVB + 1, :], (rows, chans))
    for tap in range(taps):
        first = 8 - taps + 1 + tap
        pre = pre + vec_ref[CONV + tap : CONV + tap + 1, :] * wide_ref[first : first + rows, :]
    wide_ref[:8, :] = wide_ref[rows:, :]
    pre_ref[...] = pre
    act = (pre * sigmoid(pre)).astype(bf16)
    act_ref[...] = act
    proj_ref[...] = dot(act, xproj_ref[...]).astype(bf16)


def piece_kernel(me_ref, proj_ref, act_ref, vec_ref, g_ref, carry_ref, u_ref, stepm_ref, col_ref):
    rows, c = act_ref.shape
    n = carry_ref.shape[0]

    @pl.when(pl.program_id(0) == 0)
    def _():
        carry_ref[...] = jnp.zeros_like(carry_ref)

    proj = proj_ref[...]
    _, pre = dt_of(proj, vec_ref, INTO)
    step = softplus(pre)
    u_ref[...] = step * act_ref[...].astype(f32)
    stepm_ref[...] = jnp.where(proj[:, CARRY : CARRY + 1] > 0.5, step, NEVER)
    columns(proj.T, INTO, n, col_ref)
    r2 = rates_of(vec_ref, n)

    def block(i, carry):
        j = rows // BLOCK - 1 - i
        into = col_ref[j]
        for tt in reversed(range(BLOCK)):
            t = j * BLOCK + tt
            g = row_of(u_ref, t, n) * col_of(into, tt, c) + carry
            g_ref[pl.ds(pl.multiple_of(t * n, n), n), :] = g.astype(bf16)
            carry = jnp.exp2(row_of(stepm_ref, t, n) * r2) * g
        return carry

    carry_ref[...] = lax.fori_loop(0, rows // BLOCK, block, carry_ref[...])


def ahead_kernel(
    first, places, per, local, me_ref, *refs,
):
    proj_ref, act_ref, normed_ref, g_ref, vec_ref, enter_ref = refs[:6]
    if first:
        wgate_ref, outw_ref = refs[6:8]
        hp_ref, mixed_ref, gate_ref, gated_ref, leave_ref = refs[-8 - places - 5 : -8 - places]
    else:
        second_ref = refs[6]
        hp_ref, mixed_ref, gate_ref, gated_ref, leave_ref, wgate_ref, outw_ref = refs[-8 - places - 7 : -8 - places]
    branch_refs = refs[-8 - places : -8]
    carry_ref, u_ref, step_ref, col_ref, diag_ref, s_ref, y_ref, out_ref = refs[-8:]
    rows, c = act_ref.shape
    n = carry_ref.shape[0]

    @pl.when(pl.program_id(0) == 0)
    def _():
        carry_ref[...] = enter_ref[...]
        if first:
            return
        blocks = second_ref.shape[0]
        lines, own = wgate_ref.shape[0] // blocks, outw_ref.shape[0] // blocks
        for b in range(blocks):
            wgate_ref[b * lines : (b + 1) * lines, :] = second_ref[b, :lines, :]
            for k in range(outw_ref.shape[1] // c):
                outw_ref[b * own : (b + 1) * own, k * c : (k + 1) * c] = second_ref[
                    b, lines + k * own : lines + (k + 1) * own, :
                ]

    proj = proj_ref[...]
    act = act_ref[...].astype(f32)
    _, pre = dt_of(proj, vec_ref, INTO)
    step = softplus(pre)
    step_ref[...] = step
    u_ref[...] = step * act
    columns(proj.T, INTO, n, col_ref)
    read = proj[:, OUT : OUT + n]
    high = read.astype(bf16)
    diag_ref[0, BLOCK:] = block_diag(high, n)
    diag_ref[1, BLOCK:] = block_diag((read - high.astype(f32)).astype(bf16), n)
    r2 = rates_of(vec_ref, n)

    def read_out(j):
        r16 = pl.ds(pl.multiple_of(j * BLOCK, BLOCK), BLOCK)
        both = dot(jnp.concatenate([diag_ref[0, r16, :], diag_ref[1, r16, :]], axis=0), s_ref[...])
        y_ref[r16, :] = both[:BLOCK] + both[BLOCK:]

    def block(j, h):
        read_out(j)
        into = col_ref[j]
        for tt in range(BLOCK):
            t = j * BLOCK + tt
            at = pl.ds(pl.multiple_of(t * n, n), n)
            hp = jnp.exp2(row_of(step_ref, t, n) * r2) * h
            h = hp + row_of(u_ref, t, n) * col_of(into, tt, c)
            hp_ref[at, :] = hp.astype(bf16)
            s_ref[tt * n : (tt + 1) * n, :] = (hp + g_ref[at, :].astype(f32)).astype(bf16)
        return h

    carry_ref[...] = lax.fori_loop(0, rows // BLOCK, block, carry_ref[...])
    read_out(rows // BLOCK)
    mixed = y_ref[BLOCK:] + vec_ref[SKIP : SKIP + 1, :] * act
    mixed_ref[...] = mixed
    gate = dot(normed_ref[...], wgate_ref[...])
    gate_ref[...] = gate
    gated = (mixed * (gate * sigmoid(gate))).astype(bf16)
    gated_ref[...] = gated.T
    out_ref[...] = dot(gated, outw_ref[...]).astype(bf16)
    write_rows(branch_refs, me_ref, places, per, local, out_ref)
    leave_ref[...] = carry_ref[...]


def piece_grad_kernel(
    first, places, per, local, me_ref, *refs,
):
    proj_ref, act_ref, mixed_ref, gate_ref, vec_ref, outw_ref, enter_ref, before_ref = refs[:8]
    db_refs = refs[8 : 8 + places]
    q_ref, dm_ref, dg_ref, db_ref, sgrad_ref, leave_ref = refs[-9:-3]
    carry_ref, stepm_ref, col_ref = refs[-3:]
    rows, c = act_ref.shape
    n = carry_ref.shape[0]

    @pl.when(pl.program_id(0) == 0)
    def _():
        carry_ref[...] = enter_ref[...]
        sgrad_ref[...] = before_ref[...]

    proj = proj_ref[...]
    _, pre = dt_of(proj, vec_ref, INTO)
    stepm_ref[...] = jnp.where(proj[:, CARRY : CARRY + 1] > 0.5, softplus(pre), NEVER)
    columns(proj.T, OUT, n, col_ref)
    db = read_rows(db_refs, me_ref, places, per, local)
    db_ref[...] = db
    dgated = dot_t(db, outw_ref[...])
    gate = gate_ref[...]
    s = sigmoid(gate)
    dm = dgated * (gate * s)
    dm_ref[...] = dm
    dg = (dgated * mixed_ref[...] * (s * (1.0 + gate * (1.0 - s)))).astype(bf16)
    dg_ref[...] = dg
    sgrad_ref[...] += jnp.sum(dm * act_ref[...].astype(f32), axis=0, keepdims=True)
    r2 = rates_of(vec_ref, n)

    chunk = first + pl.program_id(0)

    def scan(j, w):
        read = col_ref[j]
        for tt in range(BLOCK):
            t = j * BLOCK + tt
            q = jnp.exp2(row_of(stepm_ref, t, n) * r2) * w
            q_ref[pl.ds(pl.multiple_of(t * n, n), n), :] = q.astype(bf16)
            w = q + row_of(dm_ref, t, n) * col_of(read, tt, c)
        return w

    def fill(j, w):
        at = pl.ds(pl.multiple_of(j * BLOCK * n, BLOCK * n), BLOCK * n)
        q_ref[at, :] = jnp.zeros((BLOCK * n, c), bf16)
        return row_of(dm_ref, j * BLOCK + BLOCK - 1, n) * col_of(col_ref[j], BLOCK - 1, c)

    def block(j, w):
        return lax.cond(me_ref[1 + chunk * (rows // BLOCK) + j] > 0, scan, fill, j, w)

    carry_ref[...] = lax.fori_loop(0, rows // BLOCK, block, carry_ref[...])
    leave_ref[...] = carry_ref[...]


def state_grad_kernel(
    me_ref, proj_ref, act_ref, dm_ref, g_ref, hp_ref, q_ref, vec_ref, sgrad_ref, pieces_ref,
    dact_ref, dproj_ref, table_ref,
    carry_ref, u_ref, step_ref, col_ref, diag_ref, ig_ref, rr_ref, rs_ref, pair_ref, own_ref, x_ref, y_ref, dp_ref,
):
    rows, c = act_ref.shape
    n = carry_ref.shape[0]
    wide = BLOCK * n

    @pl.when(pl.program_id(0) == 0)
    def _():
        carry_ref[...] = jnp.zeros_like(carry_ref)
        table_ref[...] = jnp.zeros_like(table_ref)
        table_ref[SKIP : SKIP + 1, :] = sgrad_ref[...]
        rs_ref[...] = jnp.zeros_like(rs_ref)

    proj = proj_ref[...]
    act = act_ref[...].astype(f32)
    low, pre = dt_of(proj, vec_ref, INTO)
    step = softplus(pre)
    step_ref[...] = step
    u_ref[...] = step * act
    columns(proj.T, OUT, n, col_ref)
    diag_ref[:rows] = block_diag(proj[:, INTO : INTO + n].astype(bf16), n)
    r2 = rates_of(vec_ref, n)
    iota = lambda shape, axis: lax.broadcasted_iota(jnp.int32, shape, axis)
    mask = lambda v: v.astype(f32).astype(bf16)
    by_row = mask(iota((BLOCK, wide), 1) // n == iota((BLOCK, wide), 0))
    by_state = mask(iota((n, wide), 1) % n == iota((n, wide), 0))
    part = min(c, 2 * LANES)
    which = mask(iota((2 * part, LANES), 0) // part == iota((2 * part, LANES), 1) // n % 2)
    own_lane = iota((wide, LANES), 1) % n == iota((wide, LANES), 0) % n

    def sums(j):
        r16 = pl.ds(pl.multiple_of(j * BLOCK, BLOCK), BLOCK)
        x_ref[r16, :] = dot(diag_ref[r16, :], ig_ref[...])
        y_ref[r16, :] = dot(by_row, rr_ref[...])
        table_ref[ALOG : ALOG + n, :] += dot(by_state, rs_ref[...])
        dp_ref[pl.ds(pl.multiple_of((j + 1) * BLOCK, BLOCK), BLOCK), :] = dot(by_row, own_ref[...])
        own_ref[...] = jnp.where(own_lane, dot(pair_ref[...], which), 0.0).astype(bf16)

    def block(i, m):
        j = rows // BLOCK - 1 - i
        sums(j + 1)
        read = col_ref[j]
        for tt in reversed(range(BLOCK)):
            t = j * BLOCK + tt
            at = pl.ds(pl.multiple_of(t * n, n), n)
            loc = slice(tt * n, (tt + 1) * n)
            drow = row_of(dm_ref, t, n)
            mu = m + drow * col_of(read, tt, c)
            srow = row_of(step_ref, t, n)
            m = jnp.exp2(srow * r2) * mu
            low_mu = mu.astype(bf16)
            q = q_ref[at, :]
            g = g_ref[at, :]
            hp = hp_ref[at, :]
            rg = low_mu * hp + q * g
            ig = low_mu + q
            ig_ref[loc, :] = ig
            rr_ref[loc, :] = (rg.astype(f32) * r2).astype(bf16)
            rs_ref[loc, :] = rg * srow.astype(bf16)
            pb = ig * row_of(u_ref, t, n).astype(bf16)
            pc = (hp + g) * drow.astype(bf16)
            sb, sc = pb[:, :part], pc[:, :part]
            for k in range(1, c // part):
                sb = sb + pb[:, k * part : (k + 1) * part]
                sc = sc + pc[:, k * part : (k + 1) * part]
            pair_ref[loc, :part] = sb
            pair_ref[loc, part:] = sc
        return m

    carry_ref[...] = lax.fori_loop(0, rows // BLOCK, block, carry_ref[...])
    sums(0)
    dp_ref[:BLOCK, :] = dot(by_row, own_ref[...])
    rs_ref[...] = jnp.zeros_like(rs_ref)
    xs = x_ref[:rows]
    dact_ref[...] = step_ref[...] * xs + vec_ref[SKIP : SKIP + 1, :] * dm_ref[...]
    dpre = (y_ref[:rows] * LN2 + act * xs) * sigmoid(pre)
    table_ref[DTB : DTB + 1, :] += jnp.sum(dpre, axis=0, keepdims=True)
    dpre_low = dpre.astype(bf16)
    table_ref[:INTO, :] += t_dot(low, dpre_low)
    dproj_ref[...] = dp_ref[:rows].astype(bf16)
    dproj_ref[:, :INTO] = dot_t(dpre_low, vec_ref[:INTO, :].astype(bf16)).astype(bf16)

    @pl.when(pl.program_id(0) == pl.num_programs(0) - 1)
    def _():
        dproj_ref[:BLOCK, CARRY:] = pieces_ref[:, CARRY:]
        table_ref[ALOG : ALOG + n, :] *= -jnp.exp(vec_ref[ALOG : ALOG + n, :])


def end_kernel(own, local, count, me_ref, *refs):
    dn_refs, refs = refs[-count - 8 : -8], refs[: -count - 8] + refs[-8:]
    parts = refs[:-18]
    (
        dact_ref, pre_ref, stream_ref, act_ref, dg_ref, vec_ref, xproj_ref, ws_ref, wg_ref, table_ref,
        ds_ref, small_ref, pieces_ref, sum_ref,
        wide_ref, xgrad_ref, cgrad_ref, turned_ref,
    ) = refs[-18:]
    rows, c = act_ref.shape
    taps = CONVB - CONV

    @pl.when(pl.program_id(0) == 0)
    def _():
        wide_ref[rows:, :] = jnp.zeros((8, c), f32)
        xgrad_ref[...] = jnp.zeros_like(xgrad_ref)
        cgrad_ref[...] = table_ref[...]

    dproj = parts[0][...].astype(f32)
    for part in parts[1:]:
        dproj = dproj + part[...].astype(f32)
    used = lax.broadcasted_iota(jnp.int32, dproj.shape, 1) < CARRY
    dproj = jnp.where(used, dproj, 0.0).astype(bf16)
    pre = pre_ref[...]
    s = sigmoid(pre)
    dconv = (dact_ref[...] + dot_t(dproj, xproj_ref[...])) * (s * (1.0 + pre * (1.0 - s)))
    wide_ref[:rows, :] = dconv
    xgrad_ref[...] += t_dot(act_ref[...], dproj)
    cgrad_ref[CONVB : CONVB + 1, :] += jnp.sum(dconv, axis=0, keepdims=True)
    stream = stream_ref[...].astype(f32)
    dstream = jnp.zeros((rows, c), f32)
    for tap in range(taps):
        back = taps - 1 - tap
        moved = wide_ref[back : back + rows, :]
        cgrad_ref[CONV + tap : CONV + tap + 1, :] += jnp.sum(stream * moved, axis=0, keepdims=True)
        dstream = dstream + vec_ref[CONV + tap : CONV + tap + 1, :] * moved
    wide_ref[rows:, :] = dconv[:8, :]
    dstream_low = dstream.astype(bf16)
    dn = (dot_t(dstream_low, ws_ref[...]) + dot_t(dg_ref[...], wg_ref[...])).astype(bf16)
    write_slot(dn_refs, slot_of(me_ref, local, True), dn)
    ds_ref[...] = dstream_low

    @pl.when(pl.program_id(0) == pl.num_programs(0) - 1)
    def _():
        for k in range(c // LANES):
            at = slice(k * LANES, (k + 1) * LANES)
            turned_ref[at, :] = cgrad_ref[:, at].T
        sums = tree([row_sum(part[:BLOCK, :]) for part in parts])
        sums = jnp.where(lax.broadcasted_iota(jnp.int32, sums.shape, 1) < CARRY, 0.0, sums)
        sum_ref[...] = sums
        pieces = [jnp.zeros((BLOCK, LANES), f32)]
        row = lax.broadcasted_iota(jnp.int32, (BLOCK, LANES), 0)
        for k in range(3):
            term = sums.astype(bf16).astype(f32)
            pieces = [jnp.where(row == k, term, pieces[0])]
            sums = sums - term
        for k in range(c // LANES):
            pieces_ref[:, k * LANES : (k + 1) * LANES] = pieces[0].astype(bf16)
        lines = 2 * own * LANES // c
        for b in range(c // own):
            at = slice(b * own, (b + 1) * own)
            both = jnp.concatenate([xgrad_ref[at, :], turned_ref[at, :]], axis=0)
            for k in range(c // LANES):
                small_ref[b * lines : (b + 1) * lines, k * LANES : (k + 1) * LANES] = both[k * lines : (k + 1) * lines]


def slot_of(me_ref, local, reverse=False):
    step = pl.program_id(0)
    if reverse:
        step = pl.num_programs(0) - 1 - step
    return (step // (local // ROWS)) ^ me_ref[0]


def read_rows(refs, me_ref, places, per, local):
    step = pl.program_id(0)
    each = ROWS // per
    at = pl.ds(pl.multiple_of(step // (local // ROWS) * per, per), per)
    pieces = []
    for p in range(each):
        j = step % (local // ROWS) * each + p
        if len(refs) == 1:
            pieces.append(refs[0][j, at, :])
            continue
        value = refs[0][at, :]
        for k in range(1, places):
            value = jnp.where(j ^ me_ref[0] == k, refs[k][at, :], value)
        pieces.append(value)
    return jnp.concatenate(pieces, axis=0)


def write_rows(refs, me_ref, places, per, local, from_ref):
    step = pl.program_id(0)
    each = ROWS // per
    at = pl.ds(pl.multiple_of(step // (local // ROWS) * per, per), per)
    sub = step % (local // ROWS)
    if len(refs) == 1:
        for p in range(each):
            refs[0][sub * each + p, at, :] = from_ref[p * per : (p + 1) * per, :]
        return
    for k, ref in enumerate(refs):
        j = k ^ me_ref[0]

        @pl.when(j // each == sub)
        def _(ref=ref, j=j):
            ref[at, :] = from_ref[pl.ds(pl.multiple_of(j % each * per, per), per), :]


def write_slot(refs, slot, value):
    if len(refs) == 1:
        refs[0][...] = value
        return
    for k, ref in enumerate(refs):

        @pl.when(slot == k)
        def _(ref=ref):
            ref[...] = value


def call(kernel, me, ins, outs, scratch, total, local, reverse=False, first=0, count=None, size=ROWS):
    steps = total // size
    per = local // size
    turn = (lambda i: steps - 1 - i) if reverse else (lambda i: i + first)
    aliases = {}
    for index, (_, kind) in enumerate(ins):
        if kind == "o":
            aliases[index + 1] = len(aliases)

    def slot_map(k):
        def index(i, me_ref):
            group = k ^ me_ref[0]
            if reverse:
                group = steps // per - 1 - group
            first, last = (per - 1, 0) if reverse else (0, per - 1)
            now = i // per
            return (jnp.where(now < group, first, jnp.where(now > group, last, turn(i) % per)), 0)

        return index

    def spec(shape, kind):
        if isinstance(kind, int):
            return pl.BlockSpec((size, shape[1]), slot_map(kind))
        if kind == "f":
            return pl.BlockSpec(shape, lambda i, me_ref: (0,) * len(shape))
        if kind == "o":
            return pl.BlockSpec(memory_space=pl.ANY)
        if kind == "c":
            return pl.BlockSpec(
                (shape[0], size), lambda i, me_ref: (0, turn(i))
            )
        if kind == "y":
            return pl.BlockSpec((None, size, shape[2]), lambda i, me_ref: (turn(i) // per, turn(i) % per, 0))
        if kind == "x":
            return pl.BlockSpec(
                (None, size, shape[2]), lambda i, me_ref: ((turn(i) // per) ^ me_ref[0], turn(i) % per, 0)
            )
        return pl.BlockSpec((shape[0] // steps, shape[1]), lambda i, me_ref: (turn(i), 0))

    return pl.pallas_call(
        kernel,
        out_shape=[jax.ShapeDtypeStruct(s, d) for s, d, _ in outs],
        grid_spec=pltpu.PrefetchScalarGridSpec(
            num_scalar_prefetch=1,
            grid=(count or steps,),
            in_specs=[spec(a.shape, k) for a, k in ins],
            out_specs=[spec(s, k) for s, _, k in outs],
            scratch_shapes=scratch,
        ),
        input_output_aliases=aliases,
        compiler_params=pltpu.CompilerParams(dimension_semantics=("arbitrary",), vmem_limit_bytes=60 << 20),
    )(me, *[a for a, _ in ins])


def slots_in(parts):
    if len(parts) == 1:
        return [(parts[0], "x")]
    return [(part, k) for k, part in enumerate(parts)]


def slots_out(seqs, rows, width):
    if seqs > 4:
        return [((seqs, rows, width), bf16, "x")]
    return [((rows, width), bf16, k) for k in range(seqs)]


def early_grad_kernel(normed_ref, gated_ref, dg_ref, *refs):
    parts, out_ref = refs[:-1], refs[-1]
    group, _, c = out_ref.shape
    lines, own = normed_ref.shape[0] // group, gated_ref.shape[0] // group
    gate = dot(normed_ref[...], dg_ref[...])
    out, first = 0.0, 0
    for part in parts:
        last = first + part.shape[0]
        out = out + dot(gated_ref[:, first:last], part[...])
        first = last
    for b in range(group):
        out_ref[b, :lines, :] = gate[b * lines : (b + 1) * lines]
        for k in range(out.shape[1] // c):
            out_ref[b, lines + k * own : lines + (k + 1) * own, :] = out[
                b * own : (b + 1) * own, k * c : (k + 1) * c
            ]


def late_grad_kernel(normed_ref, small_ref, ds_ref, out_ref):
    group, rows, c = out_ref.shape
    lines = normed_ref.shape[0] // group
    packed = rows - lines
    stream = dot(normed_ref[...], ds_ref[...])
    for b in range(group):
        out_ref[b, :lines, :] = stream[b * lines : (b + 1) * lines]
        out_ref[b, lines:, :] = small_ref[b * packed : (b + 1) * packed, :]


def late_pair_kernel(me_ref, normed_ref, small_ref, ds_ref, pieces_ref, mine_ref, theirs_ref):
    rows = mine_ref.shape[1]
    lines = normed_ref.shape[0] // 2
    packed = rows - lines
    stream = dot(normed_ref[...], ds_ref[...])
    small = small_ref[...]
    first = me_ref[0] == 0
    mine_ref[0, :lines, :] = jnp.where(first, stream[:lines], stream[lines:])
    mine_ref[0, lines:, :] = jnp.where(first, small[:packed], small[packed:])
    theirs_ref[0, :lines, :] = jnp.where(first, stream[lines:], stream[:lines]).astype(bf16)
    theirs_ref[0, lines:rows, :] = jnp.where(first, small[packed:], small[:packed]).astype(bf16)
    theirs_ref[0, rows:, :] = pieces_ref[...]


def late_pairs(normed_t, small, ds, pieces, batches, rows, chans):
    steps = batches // 2
    whole = lambda a: pl.BlockSpec(a.shape, lambda i, me_ref: (0, 0))
    cut = lambda a: pl.BlockSpec((a.shape[0] // steps, a.shape[1]), lambda i, me_ref: (i, 0))
    block = lambda r: pl.BlockSpec((1, r, chans), lambda i, me_ref: (i, 0, 0))
    return pl.pallas_call(
        late_pair_kernel,
        out_shape=[
            jax.ShapeDtypeStruct((steps, rows, chans), f32),
            jax.ShapeDtypeStruct((steps, rows + BLOCK, chans), bf16),
        ],
        grid_spec=pltpu.PrefetchScalarGridSpec(
            num_scalar_prefetch=1,
            grid=(steps,),
            in_specs=[cut(normed_t), cut(small), whole(ds), whole(pieces)],
            out_specs=[block(rows), block(rows + BLOCK)],
        ),
        compiler_params=pltpu.CompilerParams(dimension_semantics=("arbitrary",), vmem_limit_bytes=60 << 20),
    )((lax.axis_index("batch") % 2).astype(jnp.int32).reshape(1), normed_t, small, ds, pieces)


def by_blocks(kernel, batches, own, columns, whole, rows, chans):
    group = LANES // own
    steps = batches // group

    def spec(array, cut):
        if cut:
            return pl.BlockSpec((array.shape[0] // steps, array.shape[1]), lambda i: (i, 0))
        return pl.BlockSpec(array.shape, lambda i: (0,) * array.ndim)

    return pl.pallas_call(
        kernel,
        out_shape=jax.ShapeDtypeStruct((batches, rows, chans), f32),
        grid=(steps,),
        in_specs=[spec(a, True) for a in columns] + [spec(a, False) for a in whole],
        out_specs=pl.BlockSpec((group, rows, chans), lambda i: (i, 0, 0)),
        compiler_params=pltpu.CompilerParams(dimension_semantics=("arbitrary",), vmem_limit_bytes=60 << 20),
    )(*columns, *whole)


def split_kernel(seqs, batches, own, w_ref, gain_ref, valid_ref, out_ref):
    depth, half, chans = w_ref.shape[0], w_ref.shape[1] // 2, batches * own
    count = jnp.sum(valid_ref[...].astype(f32), keepdims=True)
    high = jnp.floor(count * (1.0 / 128.0))
    iota = lambda shape, axis: lax.broadcasted_iota(jnp.int32, shape, axis)
    gain = jnp.broadcast_to(gain_ref[...].astype(f32), (depth, depth))
    gain = jnp.where(iota((depth, depth), 0) == iota((depth, depth), 1), gain, 0.0)
    gain = jnp.sum(gain, axis=1, keepdims=True)
    lane = iota((depth, LANES), 1)
    extra = jnp.where(lane == LANES - 3, gain, 0.0)
    extra = jnp.where(lane == LANES - 2, high, extra)
    extra = jnp.where(lane == LANES - 1, count - high * 128.0, extra).astype(bf16)
    for s in range(seqs):
        for k in range(2):
            pieces = [
                w_ref[:, k * half + (b * seqs + s) * own : k * half + (b * seqs + s + 1) * own].astype(f32)
                for b in range(batches)
            ]
            first = k * (chans + LANES)
            out_ref[s, :, first : first + chans] = jnp.concatenate(pieces, axis=1).astype(bf16)
        out_ref[s, :, chans : chans + LANES] = extra


def split_columns(weight, gain, valid, seqs, batches, own):
    shape = jax.ShapeDtypeStruct((seqs, weight.shape[0], 2 * batches * own + LANES), bf16)
    return pl.pallas_call(lambda *refs: split_kernel(seqs, batches, own, *refs), out_shape=shape)(weight, gain, valid)


def join_kernel(
    batches, both_ref, small_ref, w_ref, gain_ref,
    out_ref, gain_out_ref, xproj_ref, dt_ref, alog_ref, conv_ref, convb_ref, dtb_ref, skip_ref,
):
    seqs, half = both_ref.shape[0], w_ref.shape[1] // 2
    chans = half // seqs
    own = chans // batches
    for k in range(2):
        whole = [both_ref[s, :, k * chans : (k + 1) * chans].astype(f32) for s in range(seqs)]
        pieces = [whole[s][:, b * own : (b + 1) * own] for b in range(batches) for s in range(seqs)]
        out_ref[:, k * half : (k + 1) * half] = jnp.concatenate(pieces, axis=1)
    products = out_ref[...] * w_ref[...].astype(f32)
    depth = products.shape[0]
    sums = jnp.broadcast_to(jnp.sum(products, axis=1, keepdims=True), (depth, depth))
    eye = lax.broadcasted_iota(jnp.int32, (depth, depth), 0) == lax.broadcasted_iota(jnp.int32, (depth, depth), 1)
    gain_out_ref[...] = jnp.sum(jnp.where(eye, sums, 0.0), axis=0, keepdims=True) / gain_ref[...].astype(f32)
    small = small_ref[...]
    both = jnp.concatenate([small[:, k : k + LANES] for k in range(0, chans, LANES)], axis=0)
    xproj_ref[...] = both[:own, :CARRY]
    table = both[own:]
    alog_ref[...] = table[:, ALOG:CONV]
    table = jnp.concatenate([table, jnp.zeros((LANES - own, LANES), f32)], axis=0).T[:, :own]
    dt_ref[...] = table[:INTO]
    conv_ref[...] = table[CONV:CONVB]
    convb_ref[...] = table[CONVB : CONVB + 1]
    dtb_ref[...] = table[DTB : DTB + 1]
    skip_ref[...] = table[SKIP : SKIP + 1]


def join_columns(both, small, weight, gain, batches, own):
    depth = weight.shape[0]
    shapes = [weight.shape, (1, depth), (own, CARRY), (INTO, own), (own, CONV - ALOG), (CONVB - CONV, own)]
    shapes += [(1, own)] * 3
    return pl.pallas_call(
        lambda *refs: join_kernel(batches, *refs), out_shape=[jax.ShapeDtypeStruct(s, f32) for s in shapes]
    )(both, small, weight, gain)


def partner(value, axis, k):
    return lax.ppermute(value, axis, [(i, i ^ k) for i in range(lax.axis_size(axis))])


def gather_parts(value, axis):
    n = lax.axis_size(axis)
    if n > 4:
        return [lax.all_gather(value, axis)]
    return [value] + [partner(value, axis, k) for k in range(1, n)]


def gather_batch(value, after):
    n = lax.axis_size("batch")
    if n > 8:
        return [lax.all_gather(value, "batch")], [jnp.int32(k) for k in range(n)], after
    me = lax.axis_index("batch")
    chips = jnp.stack([value] + [partner(value, "batch", 2 * k) for k in range(1, n // 2)])
    other = partner(chips, "batch", 1)
    places = [me ^ (2 * k) for k in range(n // 2)] + [me ^ (2 * k + 1) for k in range(n // 2)]
    return [chips, other], places, after


def exact(total, rows):
    terms = []
    for _ in range(3):
        term = lax.reduce_precision(total, 8, 7)
        terms.append(term)
        total = total - term
    return jnp.concatenate(terms + [jnp.zeros((rows - 3, total.shape[1]), f32)], axis=0).astype(bf16)


def row_sum(rows):
    a = rows[:3].astype(f32)
    return (a[:1] + a[1:2]) + a[2:]


def tree(values):
    while len(values) > 1:
        values = [a + b for a, b in zip(values[::2], values[1::2])]
    return values[0]


def scatter_batch(mine, theirs, total):
    n = lax.axis_size("batch")
    me = lax.axis_index("batch")
    rows, c = mine.shape[1:]
    got = partner(theirs, "batch", 1)
    mine = mine + got[:, :rows].astype(f32)
    total = row_sum(exact(total, BLOCK)) + row_sum(got[0, rows:, :LANES])
    pieces = exact(jnp.tile(total, (1, c // LANES)), BLOCK)
    low = jnp.concatenate([mine.astype(bf16), jnp.broadcast_to(pieces[None], (n // 2, BLOCK, c))], axis=1)
    got = [
        partner(lax.dynamic_index_in_dim(low, (me // 2) ^ k, 0, False), "batch", 2 * k) for k in range(1, n // 2)
    ]
    result = lax.dynamic_index_in_dim(mine, me // 2, 0, False)
    for part in got:
        result = result + part[:rows].astype(f32)
    return result, tree([row_sum(exact(total, BLOCK))] + [row_sum(part[rows:, :LANES]) for part in got]), low


def scatter_parts(values, axis):
    n = lax.axis_size(axis)
    if n > 4:
        return [lax.psum_scatter(values[0].astype(f32), axis, scatter_dimension=0)]
    return [values[0]] + [partner(values[k], axis, k) for k in range(1, n)]


def share_parts(value, axis):
    n = lax.axis_size(axis)
    if n > 4:
        return [lax.psum(value.astype(f32), axis)]
    return [value] + [partner(value, axis, k) for k in range(1, n)]


def added(parts):
    total = parts[0].astype(f32)
    for part in parts[1:]:
        total = total + part.astype(f32)
    return total


def sum_everywhere(value, axes):
    for axis in axes:
        k = 1
        while k < lax.axis_size(axis):
            value = value + partner(value, axis, k)
            k *= 2
    return value


def body(
    tokens,
    teacher,
    piece_starts,
    valid_rows,
    norm_gain,
    in_weight,
    conv_weight,
    conv_bias,
    xproj_weight,
    dtproj_weight,
    dt_bias,
    a_log,
    skip_weight,
    out_weight,
):
    seqs = lax.axis_size("seq")
    batches = lax.axis_size("batch")
    _, rows, width = tokens.shape
    total = rows * seqs
    taps, own = conv_weight.shape
    chans = own * batches
    depth = in_weight.shape[0]
    rank = dtproj_weight.shape[0]
    states = a_log.shape[1]
    lines = depth * seqs
    packed = 2 * LANES * own // chans
    place = lax.axis_index("seq") if seqs <= 4 else jnp.int32(0)
    me = place.astype(jnp.int32).reshape(1)
    tok = tokens.reshape(rows, width)

    flags = jnp.concatenate([piece_starts, valid_rows], axis=0).astype(bf16)
    flags = jnp.pad(flags, ((0, 14), (0, width - rows)))
    everything = lax.all_gather(jnp.concatenate([tok, flags], axis=0), "seq")
    split = split_columns(in_weight, norm_gain.reshape(1, depth), valid_rows, seqs, batches, own)
    split = lax.all_to_all(split, "seq", 0, 0).reshape(lines, 2 * chans + LANES)
    vectors = jnp.concatenate(
        [
            dtproj_weight.T,
            a_log,
            conv_weight.T,
            conv_bias[:, None],
            dt_bias[:, None],
            skip_weight[:, None],
        ],
        axis=1,
    )
    vectors = jnp.pad(vectors, ((0, 0), (0, LANES - vectors.shape[1])))
    columns_x = jnp.pad(xproj_weight, ((0, 0), (0, LANES - xproj_weight.shape[1])))
    local = jnp.pad(jnp.concatenate([vectors, columns_x], axis=0), ((0, lines - 2 * own), (chans, 0)))
    second = jnp.concatenate(
        [split[:, chans + LANES :]] + [out_weight[:, k : k + chans] for k in range(0, width, chans)], axis=0
    )
    blocks, places, second = gather_batch(split[:, : chans + LANES] + local, second)
    second = lax.all_gather(second, "batch")


    tile = ((total, chans), f32, "t")
    low_tile = ((total, chans), bf16, "t")
    state = ((total * states, chans), bf16, "t")
    normed, normed_t, stream, conv_pre, act, proj, w_stream, vec, xproj, gain, marks = call(
        start_kernel,
        jnp.concatenate([me] + [p.astype(jnp.int32).reshape(1) for p in places]),
        [(everything, "y")] + [(block, "f") for block in blocks],
        [
            ((total, width), bf16, "t"),
            ((width, total), bf16, "c"),
            low_tile,
            tile,
            low_tile,
            ((total, LANES), bf16, "t"),
            ((width, chans), bf16, "f"),
            ((LANES, chans), f32, "f"),
            ((chans, LANES), bf16, "f"),
            ((1, width), f32, "f"),
            ((1, LANES), f32, "f"),
        ],
        [pltpu.VMEM((ROWS + 8, chans), f32), pltpu.VMEM((width, LANES), f32), pltpu.VMEM((chans, LANES), f32)],
        total,
        rows,
    )
    total_valid = (marks[:, LANES - 2 : LANES - 1] * 128.0 + marks[:, LANES - 1 :]) / depth
    starts = everything[:, rows, :rows].astype(f32).reshape(total)
    running = jnp.cumsum(starts)
    lagged = jnp.concatenate([jnp.zeros((PIECE,), f32), running[: total - PIECE]])
    carry_on = jnp.where(running - lagged > 0.5, 1.0 - starts, 0.0)
    flags = jnp.max(carry_on.reshape(total // BLOCK, BLOCK), axis=1).astype(jnp.int32)
    proj = added(share_parts(proj, "seq"))
    me = jnp.concatenate([me, flags])
    proj = jnp.where(jnp.arange(LANES)[None, :] == CARRY, carry_on[:, None], proj)
    groups = (ROWS // BLOCK, states, BLOCK)
    (g,) = call(
        piece_kernel,
        me,
        [(proj, "t"), (act, "t"), (vec, "f")],
        [state],
        [
            pltpu.VMEM((states, chans), f32),
            pltpu.VMEM((ROWS, chans), f32),
            pltpu.VMEM((ROWS, chans), f32),
            pltpu.VMEM(groups, f32),
        ],
        total,
        rows,
        reverse=True,
    )
    halves = 2
    per = rows // seqs
    held = seqs // halves * per
    count = total // ROWS // halves
    places = seqs if seqs <= 4 else 1
    if seqs <= 4:
        messages = [((held, width), bf16, "f")] * seqs
    else:
        messages = [((seqs, held, width), bf16, "f")]
    by_time = [state, tile, tile, ((chans, total), bf16, "c")]
    weights = [((width, chans), bf16, "f"), ((chans, width), bf16, "f")]
    mine = lambda v: lax.dynamic_slice_in_dim(v, lax.axis_index("seq") * per, per, axis=1)
    tok_v = mine(everything[:, :rows]).astype(f32)
    valid_v = mine(everything[:, rows + 1, :rows].reshape(seqs, rows, 1)).astype(f32)
    teacher, g = lax.optimization_barrier((teacher, g))
    teach_v = lax.all_to_all(teacher.reshape(seqs, per, width), "seq", 0, 0).astype(f32)
    enter = jnp.zeros((states, chans), f32)
    kept = []
    branches = []
    for half in range(halves):
        out = call(
            lambda *refs, half=half: ahead_kernel(half, places, per, rows, *refs),
            me,
            [(proj, "t"), (act, "t"), (normed, "t"), (g, "t"), (vec, "f"), (enter, "f")]
            + ([(w_gate, "f"), (out_w, "f")] if half else [(second, "f")])
            + [(array, "o") for array in kept],
            by_time + [((states, chans), f32, "f")] + ([] if half else weights) + messages,
            [
                pltpu.VMEM((states, chans), f32),
                pltpu.VMEM((ROWS, chans), f32),
                pltpu.VMEM((ROWS, chans), f32),
                pltpu.VMEM(groups, f32),
                pltpu.VMEM((2, ROWS + BLOCK, BLOCK * states), bf16),
                pltpu.VMEM((BLOCK * states, chans), bf16),
                pltpu.VMEM((ROWS + BLOCK, chans), f32),
                pltpu.VMEM((ROWS, width), bf16),
            ],
            total,
            rows,
            first=half * count,
            count=count,
        )
        kept, enter = out[:4], out[4]
        if not half:
            w_gate, out_w = out[5:7]
        branches.append(out[-places:])
    hp, mixed, gate, gated_t = kept

    factor = 2.0 * (total * batches) / total_valid
    squares = jnp.zeros((1, width), f32)
    results, d_branches = [], []
    for half in range(halves):
        at = slice(half * (seqs // halves), (half + 1) * (seqs // halves))
        flat_half = lambda v: v[at].reshape(held, v.shape[2])
        result = flat_half(tok_v) + added(scatter_parts(branches[half], "seq"))
        results.append(result.astype(bf16).reshape(seqs // halves, per, width))
        misfit = result - flat_half(teach_v)
        valid_f = flat_half(valid_v)
        squares = squares + jnp.sum(valid_f * misfit * misfit, axis=0, keepdims=True)
        d_branches.append(gather_parts((factor * valid_f * misfit).astype(bf16), "seq"))
    part = LANES - CARRY
    square_sum = squares[:, :LANES]
    for k in range(LANES, width, LANES):
        square_sum = square_sum + squares[:, k : k + LANES]
    square_sum = sum(square_sum[:, k : k + part] for k in range(0, LANES, part))
    square_sum = jnp.pad(square_sum, ((0, 0), (CARRY, 0)))

    kept = []
    enter = jnp.zeros((states, chans), f32)
    skip_grad = jnp.zeros((1, chans), f32)
    for half in range(halves):
        *kept, skip_grad, enter = call(
            lambda *refs, half=half: piece_grad_kernel(half * count, places, per, rows, *refs),
            me,
            [
                (proj, "t"),
                (act, "t"),
                (mixed, "t"),
                (gate, "t"),
                (vec, "f"),
                (out_w, "f"),
                (enter, "f"),
                (skip_grad, "f"),
            ]
            + [(part, "f") for part in d_branches[half]]
            + [(array, "o") for array in kept],
            [
                state,
                tile,
                low_tile,
                ((total, width), bf16, "t"),
                ((1, chans), f32, "f"),
                ((states, chans), f32, "f"),
            ],
            [pltpu.VMEM((states, chans), f32), pltpu.VMEM((ROWS, chans), f32), pltpu.VMEM(groups, f32)],
            total,
            rows,
            first=half * count,
            count=count,
        )
    q, d_mixed, d_gate, d_branch = kept
    output = lax.all_to_all(jnp.concatenate(results, axis=0), "seq", 0, 0).reshape(rows, width)
    d_result = lax.dynamic_slice_in_dim(d_branch, lax.axis_index("seq") * rows, rows, axis=0).astype(f32)
    early_sum = by_blocks(
        early_grad_kernel,
        batches,
        own,
        [normed_t, gated_t],
        [d_gate, d_branch],
        lines + own * width // chans,
        chans,
    )
    early = lax.psum_scatter(early_sum, "batch", scatter_dimension=0)
    pieces = exact(square_sum, BLOCK)
    d_act, d_proj, table = call(
        state_grad_kernel,
        me,
        [(proj, "t"), (act, "t"), (d_mixed, "t"), (g, "t"), (hp, "t"), (q, "t"), (vec, "f"), (skip_grad, "f"), (pieces, "f")],
        [tile, ((total, LANES), bf16, "t"), ((LANES, chans), f32, "f")],
        [
            pltpu.VMEM((states, chans), f32),
            pltpu.VMEM((HALF, chans), f32),
            pltpu.VMEM((HALF, chans), f32),
            pltpu.VMEM((HALF // BLOCK, states, BLOCK), f32),
            pltpu.VMEM((HALF + BLOCK, BLOCK * states), bf16),
        ]
        + [pltpu.VMEM((BLOCK * states, chans), bf16)] * 3
        + [
            pltpu.VMEM((BLOCK * states, 2 * min(chans, 2 * LANES)), bf16),
            pltpu.VMEM((BLOCK * states, LANES), bf16),
        ]
        + [pltpu.VMEM((HALF + 2 * BLOCK, chans), f32)] * 2
        + [pltpu.VMEM((HALF + 2 * BLOCK, LANES), f32)],
        total,
        rows,
        size=HALF,
        reverse=True,
    )
    d_proj = share_parts(d_proj, "seq")
    slots = slots_out(seqs, rows, width)
    *d_normed, d_stream, small, sent, seq_sum = call(
        lambda *refs: end_kernel(own, rows, len(slots), *refs),
        me,
        [(part, "t") for part in d_proj]
        + [
            (d_act, "t"),
            (conv_pre, "t"),
            (stream, "t"),
            (act, "t"),
            (d_gate, "t"),
            (vec, "f"),
            (xproj, "f"),
            (w_stream, "f"),
            (w_gate, "f"),
            (table, "f"),
        ],
        slots
        + [
            low_tile,
            ((batches * packed, chans), f32, "f"),
            ((BLOCK, chans), bf16, "f"),
            ((1, LANES), f32, "f"),
        ],
        [
            pltpu.VMEM((ROWS + 8, chans), f32),
            pltpu.VMEM((chans, LANES), f32),
            pltpu.VMEM((LANES, chans), f32),
            pltpu.VMEM((chans, LANES), f32),
        ],
        total,
        rows,
        reverse=True,
    )
    if batches <= 8:
        mine, theirs = late_pairs(normed_t, small, d_stream, sent, batches, lines + packed, chans)
        late, square_sum, waiting = scatter_batch(mine, theirs, seq_sum)
    else:
        late = by_blocks(
            late_grad_kernel, batches, own, [normed_t, small], [d_stream], lines + packed, chans
        )
        waiting = late
        late = lax.psum_scatter(late, "batch", scatter_dimension=0)
        square_sum = sum_everywhere(square_sum, ("batch", "seq"))
    loss = jnp.sum(square_sum) / (total_valid * width)[0, 0]
    nothing = waiting[0, :1].astype(f32) * 0.0
    d_normed = added([jnp.tile(nothing, (1, width // chans))] + scatter_parts(d_normed, "seq"))
    in_out = jnp.concatenate([late[:lines], early[:lines]], axis=1).astype(bf16)
    in_out = lax.all_to_all(in_out.reshape(seqs, depth, 2 * chans), "seq", 0, 0)
    in_out, gain_out, xproj_out, dt_out, alog_out, conv_out, convb_out, dtb_out, skip_out = join_columns(
        in_out, late[lines:], in_weight, norm_gain.reshape(1, depth), batches, own
    )
    out_out = early[lines:].reshape(-1, own, chans).transpose(1, 0, 2).reshape(own, width)
    tok_f = tok.astype(f32)
    mean_sq = jnp.mean(tok_f * tok_f, axis=-1, keepdims=True)
    root_inv = lax.rsqrt(mean_sq + 1e-05)
    own_unit = tok_f * root_inv
    scaled = d_normed * gain
    input_grad = d_result + root_inv * (scaled - own_unit * jnp.mean(scaled * own_unit, axis=-1, keepdims=True))
    return (
        output[None],
        loss,
        input_grad[None],
        gain_out[0],
        in_out,
        conv_out,
        convb_out[0],
        xproj_out,
        dt_out,
        dtb_out[0],
        alog_out,
        skip_out[0],
        out_out,
    )


def solution(mesh):
    return jax.shard_map(
        body,
        mesh=mesh,
        in_specs=(
            P("batch", "seq", None),
            P("batch", "seq", None),
            P("batch", "seq"),
            P("batch", "seq"),
            P(("batch", "seq")),
            P(("batch", "seq"), None),
            P(None, ("batch", "seq")),
            P(("batch", "seq")),
            P(("batch", "seq"), None),
            P(None, ("batch", "seq")),
            P(("batch", "seq")),
            P(("batch", "seq"), None),
            P(("batch", "seq")),
            P(("batch", "seq"), None),
        ),
        out_specs=(
            P("batch", "seq", None),
            P(),
            P("batch", "seq", None),
            P(("batch", "seq")),
            P(("batch", "seq"), None),
            P(None, ("batch", "seq")),
            P(("batch", "seq")),
            P(("batch", "seq"), None),
            P(None, ("batch", "seq")),
            P(("batch", "seq")),
            P(("batch", "seq"), None),
            P(("batch", "seq")),
            P(("batch", "seq"), None),
        ),
        check_vma=False,
    )
```

```python
import jax
import jax.numpy as jnp
from jax import lax
from jax.experimental import pallas as pl
from jax.experimental.pallas import tpu as pltpu
from jax.sharding import PartitionSpec as P

PIECE = 256
BLOCK = 16
UNROLL = 4
ROWS = 256
HALF = 128
LOG2E = 1.4426950408889634
LN2 = 0.6931471805599453
NEVER = 1e9
LANES = 128
f32 = jnp.float32
bf16 = jnp.bfloat16

ALOG, CONV, CONVB, DTB, SKIP = 64, 80, 84, 85, 86
INTO, OUT, CARRY = 64, 80, 96


def dot(a, b):
    return jnp.dot(a, b, preferred_element_type=f32)


def dot_t(a, b):
    return lax.dot_general(a, b, (((1,), (1,)), ((), ())), preferred_element_type=f32)


def t_dot(a, b):
    return lax.dot_general(a, b, (((0,), (0,)), ((), ())), preferred_element_type=f32)


def sigmoid(v):
    return 1.0 / (1.0 + jnp.exp(-v))


def row_of(ref, t, n):
    return jnp.broadcast_to(ref[pl.ds(t, 1), :], (n, ref.shape[1]))


def col_of(block, tt, c):
    return jnp.broadcast_to(block[:, tt : tt + 1], (block.shape[0], c))


def rates_of(vec_ref, n):
    return -jnp.exp(vec_ref[ALOG : ALOG + n, :]) * LOG2E


def dt_of(proj, vec_ref, rank):
    low = proj[:, :rank].astype(bf16)
    return low, dot(low, vec_ref[:rank, :].astype(bf16)) + vec_ref[DTB : DTB + 1, :]


def softplus(v):
    return jnp.maximum(v, 0.0) + jnp.log1p(jnp.exp(-jnp.abs(v)))


def columns(proj_t, first, n, into_ref):
    for j in range(into_ref.shape[0]):
        into_ref[j] = proj_t[first : first + n, j * BLOCK : (j + 1) * BLOCK]


def block_diag(values, n):
    rows, wide = values.shape[0], BLOCK * n
    spread = (
        lax.broadcasted_iota(jnp.int32, (n, wide), 1) % n == lax.broadcasted_iota(jnp.int32, (n, wide), 0)
    ).astype(f32).astype(bf16)
    keep = lax.broadcasted_iota(jnp.int32, (rows, wide), 1) // n == lax.broadcasted_iota(
        jnp.int32, (rows, wide), 0
    ) % BLOCK
    return jnp.where(keep, dot(values, spread), 0.0).astype(bf16)


def unit_of(x):
    return x * lax.rsqrt(jnp.mean(x * x, axis=-1, keepdims=True) + 1e-05)


def start_kernel(me_ref, x_ref, *refs):
    parts = refs[:-14]
    (
        normed_ref, turned_ref, stream_ref, pre_ref, act_ref, proj_ref, w_ref, vec_ref, xproj_ref, gain_ref, marks_ref,
        wide_ref, ext_ref, cols_ref,
    ) = refs[-14:]
    rows, chans = stream_ref.shape
    taps = CONVB - CONV

    @pl.when(pl.program_id(0) == 0)
    def _():
        wide_ref[:8, :] = jnp.zeros((8, chans), f32)
        place = 1
        for part in parts:
            count, lines, _ = part.shape
            own = chans * lines // w_ref.shape[0]
            for k in range(count):
                block = me_ref[place]
                place += 1
                at = pl.ds(pl.multiple_of(block * lines, lines), lines)
                w_ref[at, :] = part[k, :, :chans]
                ext = part[k, :, chans:].astype(f32)
                ext_ref[at, :] = ext
                at = pl.ds(pl.multiple_of(block * own, own), own)
                cols_ref[at, :] = ext[:own]
                used = lax.broadcasted_iota(jnp.int32, (own, LANES), 1) < CARRY
                xproj_ref[at, :] = jnp.where(used, ext[own : 2 * own], 0.0).astype(bf16)
        for k in range(w_ref.shape[0] // LANES):
            at = slice(k * LANES, (k + 1) * LANES)
            gain_ref[:, at] = ext_ref[at, :].T[LANES - 3 : LANES - 2]
        for k in range(chans // LANES):
            at = slice(k * LANES, (k + 1) * LANES)
            vec_ref[:, at] = cols_ref[at, :].T
        marks_ref[...] = jnp.sum(ext_ref[...], axis=0, keepdims=True)

    normed = (unit_of(x_ref[...].astype(f32)) * gain_ref[...]).astype(bf16)
    normed_ref[...] = normed
    turned_ref[...] = normed.T
    stream = dot(normed, w_ref[...]).astype(bf16)
    stream_ref[...] = stream
    wide_ref[8:, :] = stream.astype(f32)
    pre = jnp.broadcast_to(vec_ref[CONVB : CONVB + 1, :], (rows, chans))
    for tap in range(taps):
        first = 8 - taps + 1 + tap
        pre = pre + vec_ref[CONV + tap : CONV + tap + 1, :] * wide_ref[first : first + rows, :]
    wide_ref[:8, :] = wide_ref[rows:, :]
    pre_ref[...] = pre
    act = (pre * sigmoid(pre)).astype(bf16)
    act_ref[...] = act
    proj_ref[...] = dot(act, xproj_ref[...]).astype(bf16)


def several(block):
    def blocks(i, carry):
        for k in range(UNROLL):
            carry = block(UNROLL * i + k, carry)
        return carry

    return blocks


def piece_kernel(me_ref, proj_ref, act_ref, vec_ref, g_ref, carry_ref, u_ref, stepm_ref, col_ref):
    rows, c = act_ref.shape
    n = carry_ref.shape[0]

    @pl.when(pl.program_id(0) == 0)
    def _():
        carry_ref[...] = jnp.zeros_like(carry_ref)

    proj = proj_ref[...]
    _, pre = dt_of(proj, vec_ref, INTO)
    step = softplus(pre)
    u_ref[...] = step * act_ref[...].astype(f32)
    stepm_ref[...] = jnp.where(proj[:, CARRY : CARRY + 1] > 0.5, step, NEVER)
    columns(proj.T, INTO, n, col_ref)
    r2 = rates_of(vec_ref, n)

    def block(i, carry):
        j = rows // BLOCK - 1 - i
        into = col_ref[j]
        for tt in reversed(range(BLOCK)):
            t = j * BLOCK + tt
            g = row_of(u_ref, t, n) * col_of(into, tt, c) + carry
            g_ref[pl.ds(pl.multiple_of(t * n, n), n), :] = g.astype(bf16)
            carry = jnp.exp2(row_of(stepm_ref, t, n) * r2) * g
        return carry

    carry_ref[...] = lax.fori_loop(0, rows // BLOCK // UNROLL, several(block), carry_ref[...])


def ahead_kernel(
    first, places, per, local, me_ref, *refs,
):
    proj_ref, act_ref, normed_ref, g_ref, vec_ref, enter_ref = refs[:6]
    if first:
        wgate_ref, outw_ref = refs[6:8]
        hp_ref, mixed_ref, gate_ref, gated_ref, leave_ref = refs[-8 - places - 5 : -8 - places]
    else:
        second_ref = refs[6]
        hp_ref, mixed_ref, gate_ref, gated_ref, leave_ref, wgate_ref, outw_ref = refs[-8 - places - 7 : -8 - places]
    branch_refs = refs[-8 - places : -8]
    carry_ref, u_ref, step_ref, col_ref, diag_ref, s_ref, y_ref, out_ref = refs[-8:]
    rows, c = act_ref.shape
    n = carry_ref.shape[0]

    @pl.when(pl.program_id(0) == 0)
    def _():
        carry_ref[...] = enter_ref[...]
        if first:
            return
        blocks = second_ref.shape[0]
        lines, own = wgate_ref.shape[0] // blocks, outw_ref.shape[0] // blocks
        for b in range(blocks):
            wgate_ref[b * lines : (b + 1) * lines, :] = second_ref[b, :lines, :]
            for k in range(outw_ref.shape[1] // c):
                outw_ref[b * own : (b + 1) * own, k * c : (k + 1) * c] = second_ref[
                    b, lines + k * own : lines + (k + 1) * own, :
                ]

    proj = proj_ref[...]
    act = act_ref[...].astype(f32)
    _, pre = dt_of(proj, vec_ref, INTO)
    step = softplus(pre)
    step_ref[...] = step
    u_ref[...] = step * act
    columns(proj.T, INTO, n, col_ref)
    read = proj[:, OUT : OUT + n]
    high = read.astype(bf16)
    diag_ref[0, BLOCK:] = block_diag(high, n)
    diag_ref[1, BLOCK:] = block_diag((read - high.astype(f32)).astype(bf16), n)
    r2 = rates_of(vec_ref, n)

    def read_out(j):
        r16 = pl.ds(pl.multiple_of(j * BLOCK, BLOCK), BLOCK)
        both = dot(jnp.concatenate([diag_ref[0, r16, :], diag_ref[1, r16, :]], axis=0), s_ref[...])
        y_ref[r16, :] = both[:BLOCK] + both[BLOCK:]

    def block(j, h):
        read_out(j)
        into = col_ref[j]
        for tt in range(BLOCK):
            t = j * BLOCK + tt
            at = pl.ds(pl.multiple_of(t * n, n), n)
            hp = jnp.exp2(row_of(step_ref, t, n) * r2) * h
            h = hp + row_of(u_ref, t, n) * col_of(into, tt, c)
            hp_ref[at, :] = hp.astype(bf16)
            s_ref[tt * n : (tt + 1) * n, :] = (hp + g_ref[at, :].astype(f32)).astype(bf16)
        return h

    carry_ref[...] = lax.fori_loop(0, rows // BLOCK // UNROLL, several(block), carry_ref[...])
    read_out(rows // BLOCK)
    mixed = y_ref[BLOCK:] + vec_ref[SKIP : SKIP + 1, :] * act
    mixed_ref[...] = mixed
    gate = dot(normed_ref[...], wgate_ref[...])
    gate_ref[...] = gate
    gated = (mixed * (gate * sigmoid(gate))).astype(bf16)
    gated_ref[...] = gated.T
    out_ref[...] = dot(gated, outw_ref[...]).astype(bf16)
    write_rows(branch_refs, me_ref, places, per, local, out_ref)
    leave_ref[...] = carry_ref[...]


def piece_grad_kernel(
    first, places, per, local, me_ref, *refs,
):
    proj_ref, act_ref, mixed_ref, gate_ref, vec_ref, outw_ref, enter_ref, before_ref = refs[:8]
    db_refs = refs[8 : 8 + places]
    q_ref, dm_ref, dg_ref, db_ref, sgrad_ref, leave_ref = refs[-9:-3]
    carry_ref, stepm_ref, col_ref = refs[-3:]
    rows, c = act_ref.shape
    n = carry_ref.shape[0]

    @pl.when(pl.program_id(0) == 0)
    def _():
        carry_ref[...] = enter_ref[...]
        sgrad_ref[...] = before_ref[...]

    proj = proj_ref[...]
    _, pre = dt_of(proj, vec_ref, INTO)
    stepm_ref[...] = jnp.where(proj[:, CARRY : CARRY + 1] > 0.5, softplus(pre), NEVER)
    columns(proj.T, OUT, n, col_ref)
    db = read_rows(db_refs, me_ref, places, per, local)
    db_ref[...] = db
    dgated = dot_t(db, outw_ref[...])
    gate = gate_ref[...]
    s = sigmoid(gate)
    dm = dgated * (gate * s)
    dm_ref[...] = dm
    dg = (dgated * mixed_ref[...] * (s * (1.0 + gate * (1.0 - s)))).astype(bf16)
    dg_ref[...] = dg
    sgrad_ref[...] += jnp.sum(dm * act_ref[...].astype(f32), axis=0, keepdims=True)
    r2 = rates_of(vec_ref, n)

    chunk = first + pl.program_id(0)

    size = UNROLL * BLOCK

    def scan(i, w):
        for k in range(UNROLL):
            j = UNROLL * i + k
            read = col_ref[j]
            for tt in range(BLOCK):
                t = j * BLOCK + tt
                q = jnp.exp2(row_of(stepm_ref, t, n) * r2) * w
                q_ref[pl.ds(pl.multiple_of(t * n, n), n), :] = q.astype(bf16)
                w = q + row_of(dm_ref, t, n) * col_of(read, tt, c)
        return w

    def fill(i, w):
        for k in range(UNROLL):
            at = pl.ds(pl.multiple_of((UNROLL * i + k) * BLOCK * n, BLOCK * n), BLOCK * n)
            q_ref[at, :] = jnp.zeros((BLOCK * n, c), bf16)
        return row_of(dm_ref, (i + 1) * size - 1, n) * col_of(col_ref[(i + 1) * UNROLL - 1], BLOCK - 1, c)

    def group(i, w):
        return lax.cond(me_ref[1 + chunk * (rows // size) + i] > 0, scan, fill, i, w)

    carry_ref[...] = lax.fori_loop(0, rows // size, group, carry_ref[...])
    leave_ref[...] = carry_ref[...]


def state_grad_kernel(
    me_ref, proj_ref, act_ref, dm_ref, g_ref, hp_ref, q_ref, vec_ref, sgrad_ref, pieces_ref,
    dact_ref, dproj_ref, table_ref,
    carry_ref, u_ref, step_ref, col_ref, diag_ref, ig_ref, rr_ref, pair_ref, own_ref, x_ref, y_ref, dp_ref,
):
    rows, c = act_ref.shape
    n = carry_ref.shape[0]
    wide = BLOCK * n

    @pl.when(pl.program_id(0) == 0)
    def _():
        carry_ref[...] = jnp.zeros_like(carry_ref)
        table_ref[...] = jnp.zeros_like(table_ref)
        table_ref[SKIP : SKIP + 1, :] = sgrad_ref[...]

    proj = proj_ref[...]
    act = act_ref[...].astype(f32)
    low, pre = dt_of(proj, vec_ref, INTO)
    step = softplus(pre)
    step_ref[...] = step
    u_ref[...] = step * act
    columns(proj.T, OUT, n, col_ref)
    diag_ref[:rows] = block_diag(proj[:, INTO : INTO + n].astype(bf16), n)
    r2 = rates_of(vec_ref, n)
    iota = lambda shape, axis: lax.broadcasted_iota(jnp.int32, shape, axis)
    mask = lambda v: v.astype(f32).astype(bf16)
    by_row = mask(iota((BLOCK, wide), 1) // n == iota((BLOCK, wide), 0))
    part = min(c, 2 * LANES)
    which = mask(iota((2 * part, LANES), 0) // part == iota((2 * part, LANES), 1) // n % 2)
    own_lane = iota((wide, LANES), 1) % n == iota((wide, LANES), 0) % n

    def sums(j):
        r16 = pl.ds(pl.multiple_of(j * BLOCK, BLOCK), BLOCK)
        x_ref[r16, :] = dot(diag_ref[r16, :], ig_ref[...])
        y_ref[r16, :] = dot(by_row, rr_ref[...])
        dp_ref[pl.ds(pl.multiple_of((j + 1) * BLOCK, BLOCK), BLOCK), :] = dot(by_row, own_ref[...])
        own_ref[...] = jnp.where(own_lane, dot(pair_ref[...], which), 0.0).astype(bf16)

    def block(i, both):
        m, al = both
        j = rows // BLOCK - 1 - i
        sums(j + 1)
        read = col_ref[j]
        for tt in reversed(range(BLOCK)):
            t = j * BLOCK + tt
            at = pl.ds(pl.multiple_of(t * n, n), n)
            loc = slice(tt * n, (tt + 1) * n)
            drow = row_of(dm_ref, t, n)
            mu = m + drow * col_of(read, tt, c)
            srow = row_of(step_ref, t, n)
            m = jnp.exp2(srow * r2) * mu
            low_mu = mu.astype(bf16)
            q = q_ref[at, :]
            g = g_ref[at, :]
            hp = hp_ref[at, :]
            rg = low_mu * hp + q * g
            ig = low_mu + q
            ig_ref[loc, :] = ig
            rg = rg.astype(f32)
            al = al + rg * srow
            rr_ref[loc, :] = (rg * r2).astype(bf16)
            pb = ig * row_of(u_ref, t, n).astype(bf16)
            pc = (hp + g) * drow.astype(bf16)
            sb, sc = pb[:, :part], pc[:, :part]
            for k in range(1, c // part):
                sb = sb + pb[:, k * part : (k + 1) * part]
                sc = sc + pc[:, k * part : (k + 1) * part]
            pair_ref[loc, :part] = sb
            pair_ref[loc, part:] = sc
        return m, al

    m, al = lax.fori_loop(0, rows // BLOCK, block, (carry_ref[...], table_ref[ALOG : ALOG + n, :]))
    carry_ref[...] = m
    table_ref[ALOG : ALOG + n, :] = al
    sums(0)
    dp_ref[:BLOCK, :] = dot(by_row, own_ref[...])
    xs = x_ref[:rows]
    dact_ref[...] = step_ref[...] * xs + vec_ref[SKIP : SKIP + 1, :] * dm_ref[...]
    dpre = (y_ref[:rows] * LN2 + act * xs) * sigmoid(pre)
    table_ref[DTB : DTB + 1, :] += jnp.sum(dpre, axis=0, keepdims=True)
    dpre_low = dpre.astype(bf16)
    table_ref[:INTO, :] += t_dot(low, dpre_low)
    dproj_ref[...] = dp_ref[:rows].astype(bf16)
    dproj_ref[:, :INTO] = dot_t(dpre_low, vec_ref[:INTO, :].astype(bf16)).astype(bf16)

    @pl.when(pl.program_id(0) == pl.num_programs(0) - 1)
    def _():
        dproj_ref[:BLOCK, CARRY:] = pieces_ref[:, CARRY:]
        table_ref[ALOG : ALOG + n, :] *= -jnp.exp(vec_ref[ALOG : ALOG + n, :])


def end_kernel(own, local, count, me_ref, *refs):
    dn_refs, refs = refs[-count - 8 : -8], refs[: -count - 8] + refs[-8:]
    parts = refs[:-18]
    (
        dact_ref, pre_ref, stream_ref, act_ref, dg_ref, vec_ref, xproj_ref, ws_ref, wg_ref, table_ref,
        ds_ref, small_ref, pieces_ref, sum_ref,
        wide_ref, xgrad_ref, cgrad_ref, turned_ref,
    ) = refs[-18:]
    rows, c = act_ref.shape
    taps = CONVB - CONV

    @pl.when(pl.program_id(0) == 0)
    def _():
        wide_ref[rows:, :] = jnp.zeros((8, c), f32)
        xgrad_ref[...] = jnp.zeros_like(xgrad_ref)
        cgrad_ref[...] = table_ref[...]

    dproj = parts[0][...].astype(f32)
    for part in parts[1:]:
        dproj = dproj + part[...].astype(f32)
    used = lax.broadcasted_iota(jnp.int32, dproj.shape, 1) < CARRY
    dproj = jnp.where(used, dproj, 0.0).astype(bf16)
    pre = pre_ref[...]
    s = sigmoid(pre)
    dconv = (dact_ref[...] + dot_t(dproj, xproj_ref[...])) * (s * (1.0 + pre * (1.0 - s)))
    wide_ref[:rows, :] = dconv
    xgrad_ref[...] += t_dot(act_ref[...], dproj)
    cgrad_ref[CONVB : CONVB + 1, :] += jnp.sum(dconv, axis=0, keepdims=True)
    stream = stream_ref[...].astype(f32)
    dstream = jnp.zeros((rows, c), f32)
    for tap in range(taps):
        back = taps - 1 - tap
        moved = wide_ref[back : back + rows, :]
        cgrad_ref[CONV + tap : CONV + tap + 1, :] += jnp.sum(stream * moved, axis=0, keepdims=True)
        dstream = dstream + vec_ref[CONV + tap : CONV + tap + 1, :] * moved
    wide_ref[rows:, :] = dconv[:8, :]
    dstream_low = dstream.astype(bf16)
    dn = (dot_t(dstream_low, ws_ref[...]) + dot_t(dg_ref[...], wg_ref[...])).astype(bf16)
    write_slot(dn_refs, slot_of(me_ref, local, True), dn)
    ds_ref[...] = dstream_low

    @pl.when(pl.program_id(0) == pl.num_programs(0) - 1)
    def _():
        for k in range(c // LANES):
            at = slice(k * LANES, (k + 1) * LANES)
            turned_ref[at, :] = cgrad_ref[:, at].T
        sums = tree([row_sum(part[:BLOCK, :]) for part in parts])
        sums = jnp.where(lax.broadcasted_iota(jnp.int32, sums.shape, 1) < CARRY, 0.0, sums)
        sum_ref[...] = sums
        pieces = [jnp.zeros((BLOCK, LANES), f32)]
        row = lax.broadcasted_iota(jnp.int32, (BLOCK, LANES), 0)
        for k in range(3):
            term = sums.astype(bf16).astype(f32)
            pieces = [jnp.where(row == k, term, pieces[0])]
            sums = sums - term
        for k in range(c // LANES):
            pieces_ref[:, k * LANES : (k + 1) * LANES] = pieces[0].astype(bf16)
        lines = 2 * own * LANES // c
        for b in range(c // own):
            at = slice(b * own, (b + 1) * own)
            both = jnp.concatenate([xgrad_ref[at, :], turned_ref[at, :]], axis=0)
            for k in range(c // LANES):
                small_ref[b * lines : (b + 1) * lines, k * LANES : (k + 1) * LANES] = both[k * lines : (k + 1) * lines]


def slot_of(me_ref, local, reverse=False):
    step = pl.program_id(0)
    if reverse:
        step = pl.num_programs(0) - 1 - step
    return (step // (local // ROWS)) ^ me_ref[0]


def read_rows(refs, me_ref, places, per, local):
    step = pl.program_id(0)
    each = ROWS // per
    at = pl.ds(pl.multiple_of(step // (local // ROWS) * per, per), per)
    pieces = []
    for p in range(each):
        j = step % (local // ROWS) * each + p
        if len(refs) == 1:
            pieces.append(refs[0][j, at, :])
            continue
        value = refs[0][at, :]
        for k in range(1, places):
            value = jnp.where(j ^ me_ref[0] == k, refs[k][at, :], value)
        pieces.append(value)
    return jnp.concatenate(pieces, axis=0)


def write_rows(refs, me_ref, places, per, local, from_ref):
    step = pl.program_id(0)
    each = ROWS // per
    at = pl.ds(pl.multiple_of(step // (local // ROWS) * per, per), per)
    sub = step % (local // ROWS)
    if len(refs) == 1:
        for p in range(each):
            refs[0][sub * each + p, at, :] = from_ref[p * per : (p + 1) * per, :]
        return
    for k, ref in enumerate(refs):
        j = k ^ me_ref[0]

        @pl.when(j // each == sub)
        def _(ref=ref, j=j):
            ref[at, :] = from_ref[pl.ds(pl.multiple_of(j % each * per, per), per), :]


def write_slot(refs, slot, value):
    if len(refs) == 1:
        refs[0][...] = value
        return
    for k, ref in enumerate(refs):

        @pl.when(slot == k)
        def _(ref=ref):
            ref[...] = value


def call(kernel, me, ins, outs, scratch, total, local, reverse=False, first=0, count=None, size=ROWS):
    steps = total // size
    per = local // size
    turn = (lambda i: steps - 1 - i) if reverse else (lambda i: i + first)
    aliases = {}
    for index, (_, kind) in enumerate(ins):
        if kind == "o":
            aliases[index + 1] = len(aliases)

    def slot_map(k):
        def index(i, me_ref):
            group = k ^ me_ref[0]
            if reverse:
                group = steps // per - 1 - group
            first, last = (per - 1, 0) if reverse else (0, per - 1)
            now = i // per
            return (jnp.where(now < group, first, jnp.where(now > group, last, turn(i) % per)), 0)

        return index

    def spec(shape, kind):
        if isinstance(kind, int):
            return pl.BlockSpec((size, shape[1]), slot_map(kind))
        if kind == "f":
            return pl.BlockSpec(shape, lambda i, me_ref: (0,) * len(shape))
        if kind == "o":
            return pl.BlockSpec(memory_space=pl.ANY)
        if kind == "c":
            return pl.BlockSpec(
                (shape[0], size), lambda i, me_ref: (0, turn(i))
            )
        if kind == "y":
            return pl.BlockSpec((None, size, shape[2]), lambda i, me_ref: (turn(i) // per, turn(i) % per, 0))
        if kind == "x":
            return pl.BlockSpec(
                (None, size, shape[2]), lambda i, me_ref: ((turn(i) // per) ^ me_ref[0], turn(i) % per, 0)
            )
        return pl.BlockSpec((shape[0] // steps, shape[1]), lambda i, me_ref: (turn(i), 0))

    return pl.pallas_call(
        kernel,
        out_shape=[jax.ShapeDtypeStruct(s, d) for s, d, _ in outs],
        grid_spec=pltpu.PrefetchScalarGridSpec(
            num_scalar_prefetch=1,
            grid=(count or steps,),
            in_specs=[spec(a.shape, k) for a, k in ins],
            out_specs=[spec(s, k) for s, _, k in outs],
            scratch_shapes=scratch,
        ),
        input_output_aliases=aliases,
        compiler_params=pltpu.CompilerParams(dimension_semantics=("arbitrary",), vmem_limit_bytes=60 << 20),
    )(me, *[a for a, _ in ins])


def slots_in(parts):
    if len(parts) == 1:
        return [(parts[0], "x")]
    return [(part, k) for k, part in enumerate(parts)]


def slots_out(seqs, rows, width):
    if seqs > 4:
        return [((seqs, rows, width), bf16, "x")]
    return [((rows, width), bf16, k) for k in range(seqs)]


def early_grad_kernel(normed_ref, gated_ref, dg_ref, *refs):
    parts, out_ref = refs[:-1], refs[-1]
    group, _, c = out_ref.shape
    lines, own = normed_ref.shape[0] // group, gated_ref.shape[0] // group
    gate = dot(normed_ref[...], dg_ref[...])
    out, first = 0.0, 0
    for part in parts:
        last = first + part.shape[0]
        out = out + dot(gated_ref[:, first:last], part[...])
        first = last
    for b in range(group):
        out_ref[b, :lines, :] = gate[b * lines : (b + 1) * lines]
        for k in range(out.shape[1] // c):
            out_ref[b, lines + k * own : lines + (k + 1) * own, :] = out[
                b * own : (b + 1) * own, k * c : (k + 1) * c
            ]


def late_grad_kernel(normed_ref, small_ref, ds_ref, out_ref):
    group, rows, c = out_ref.shape
    lines = normed_ref.shape[0] // group
    packed = rows - lines
    stream = dot(normed_ref[...], ds_ref[...])
    for b in range(group):
        out_ref[b, :lines, :] = stream[b * lines : (b + 1) * lines]
        out_ref[b, lines:, :] = small_ref[b * packed : (b + 1) * packed, :]


def late_pair_kernel(me_ref, normed_ref, small_ref, ds_ref, pieces_ref, mine_ref, theirs_ref):
    rows = mine_ref.shape[1]
    lines = normed_ref.shape[0] // 2
    packed = rows - lines
    stream = dot(normed_ref[...], ds_ref[...])
    small = small_ref[...]
    first = me_ref[0] == 0
    mine_ref[0, :lines, :] = jnp.where(first, stream[:lines], stream[lines:])
    mine_ref[0, lines:, :] = jnp.where(first, small[:packed], small[packed:])
    theirs_ref[0, :lines, :] = jnp.where(first, stream[lines:], stream[:lines]).astype(bf16)
    theirs_ref[0, lines:rows, :] = jnp.where(first, small[packed:], small[:packed]).astype(bf16)
    theirs_ref[0, rows:, :] = pieces_ref[...]


def late_pairs(normed_t, small, ds, pieces, batches, rows, chans):
    steps = batches // 2
    whole = lambda a: pl.BlockSpec(a.shape, lambda i, me_ref: (0, 0))
    cut = lambda a: pl.BlockSpec((a.shape[0] // steps, a.shape[1]), lambda i, me_ref: (i, 0))
    block = lambda r: pl.BlockSpec((1, r, chans), lambda i, me_ref: (i, 0, 0))
    return pl.pallas_call(
        late_pair_kernel,
        out_shape=[
            jax.ShapeDtypeStruct((steps, rows, chans), f32),
            jax.ShapeDtypeStruct((steps, rows + BLOCK, chans), bf16),
        ],
        grid_spec=pltpu.PrefetchScalarGridSpec(
            num_scalar_prefetch=1,
            grid=(steps,),
            in_specs=[cut(normed_t), cut(small), whole(ds), whole(pieces)],
            out_specs=[block(rows), block(rows + BLOCK)],
        ),
        compiler_params=pltpu.CompilerParams(dimension_semantics=("arbitrary",), vmem_limit_bytes=60 << 20),
    )((lax.axis_index("batch") % 2).astype(jnp.int32).reshape(1), normed_t, small, ds, pieces)


def by_blocks(kernel, batches, own, columns, whole, rows, chans):
    group = LANES // own
    steps = batches // group

    def spec(array, cut):
        if cut:
            return pl.BlockSpec((array.shape[0] // steps, array.shape[1]), lambda i: (i, 0))
        return pl.BlockSpec(array.shape, lambda i: (0,) * array.ndim)

    return pl.pallas_call(
        kernel,
        out_shape=jax.ShapeDtypeStruct((batches, rows, chans), f32),
        grid=(steps,),
        in_specs=[spec(a, True) for a in columns] + [spec(a, False) for a in whole],
        out_specs=pl.BlockSpec((group, rows, chans), lambda i: (i, 0, 0)),
        compiler_params=pltpu.CompilerParams(dimension_semantics=("arbitrary",), vmem_limit_bytes=60 << 20),
    )(*columns, *whole)


def split_kernel(seqs, batches, own, w_ref, gain_ref, valid_ref, out_ref):
    depth, half, chans = w_ref.shape[0], w_ref.shape[1] // 2, batches * own
    count = jnp.sum(valid_ref[...].astype(f32), keepdims=True)
    high = jnp.floor(count * (1.0 / 128.0))
    iota = lambda shape, axis: lax.broadcasted_iota(jnp.int32, shape, axis)
    gain = jnp.broadcast_to(gain_ref[...].astype(f32), (depth, depth))
    gain = jnp.where(iota((depth, depth), 0) == iota((depth, depth), 1), gain, 0.0)
    gain = jnp.sum(gain, axis=1, keepdims=True)
    lane = iota((depth, LANES), 1)
    extra = jnp.where(lane == LANES - 3, gain, 0.0)
    extra = jnp.where(lane == LANES - 2, high, extra)
    extra = jnp.where(lane == LANES - 1, count - high * 128.0, extra).astype(bf16)
    for s in range(seqs):
        for k in range(2):
            pieces = [
                w_ref[:, k * half + (b * seqs + s) * own : k * half + (b * seqs + s + 1) * own].astype(f32)
                for b in range(batches)
            ]
            first = k * (chans + LANES)
            out_ref[s, :, first : first + chans] = jnp.concatenate(pieces, axis=1).astype(bf16)
        out_ref[s, :, chans : chans + LANES] = extra


def split_columns(weight, gain, valid, seqs, batches, own):
    shape = jax.ShapeDtypeStruct((seqs, weight.shape[0], 2 * batches * own + LANES), bf16)
    return pl.pallas_call(lambda *refs: split_kernel(seqs, batches, own, *refs), out_shape=shape)(weight, gain, valid)


def join_kernel(
    batches, both_ref, small_ref, w_ref, gain_ref,
    out_ref, gain_out_ref, xproj_ref, dt_ref, alog_ref, conv_ref, convb_ref, dtb_ref, skip_ref,
):
    seqs, half = both_ref.shape[0], w_ref.shape[1] // 2
    chans = half // seqs
    own = chans // batches
    for k in range(2):
        whole = [both_ref[s, :, k * chans : (k + 1) * chans].astype(f32) for s in range(seqs)]
        pieces = [whole[s][:, b * own : (b + 1) * own] for b in range(batches) for s in range(seqs)]
        out_ref[:, k * half : (k + 1) * half] = jnp.concatenate(pieces, axis=1)
    products = out_ref[...] * w_ref[...].astype(f32)
    depth = products.shape[0]
    sums = jnp.broadcast_to(jnp.sum(products, axis=1, keepdims=True), (depth, depth))
    eye = lax.broadcasted_iota(jnp.int32, (depth, depth), 0) == lax.broadcasted_iota(jnp.int32, (depth, depth), 1)
    gain_out_ref[...] = jnp.sum(jnp.where(eye, sums, 0.0), axis=0, keepdims=True) / gain_ref[...].astype(f32)
    small = small_ref[...]
    both = jnp.concatenate([small[:, k : k + LANES] for k in range(0, chans, LANES)], axis=0)
    xproj_ref[...] = both[:own, :CARRY]
    table = both[own:]
    alog_ref[...] = table[:, ALOG:CONV]
    table = jnp.concatenate([table, jnp.zeros((LANES - own, LANES), f32)], axis=0).T[:, :own]
    dt_ref[...] = table[:INTO]
    conv_ref[...] = table[CONV:CONVB]
    convb_ref[...] = table[CONVB : CONVB + 1]
    dtb_ref[...] = table[DTB : DTB + 1]
    skip_ref[...] = table[SKIP : SKIP + 1]


def join_columns(both, small, weight, gain, batches, own):
    depth = weight.shape[0]
    shapes = [weight.shape, (1, depth), (own, CARRY), (INTO, own), (own, CONV - ALOG), (CONVB - CONV, own)]
    shapes += [(1, own)] * 3
    return pl.pallas_call(
        lambda *refs: join_kernel(batches, *refs), out_shape=[jax.ShapeDtypeStruct(s, f32) for s in shapes]
    )(both, small, weight, gain)


def partner(value, axis, k):
    return lax.ppermute(value, axis, [(i, i ^ k) for i in range(lax.axis_size(axis))])


def gather_parts(value, axis):
    n = lax.axis_size(axis)
    if n > 4:
        return [lax.all_gather(value, axis)]
    return [value] + [partner(value, axis, k) for k in range(1, n)]


def gather_batch(value, after):
    n = lax.axis_size("batch")
    if n > 8:
        return [lax.all_gather(value, "batch")], [jnp.int32(k) for k in range(n)], after
    me = lax.axis_index("batch")
    chips = jnp.stack([value] + [partner(value, "batch", 2 * k) for k in range(1, n // 2)])
    other = partner(chips, "batch", 1)
    places = [me ^ (2 * k) for k in range(n // 2)] + [me ^ (2 * k + 1) for k in range(n // 2)]
    return [chips, other], places, after


def exact(total, rows):
    terms = []
    for _ in range(3):
        term = lax.reduce_precision(total, 8, 7)
        terms.append(term)
        total = total - term
    return jnp.concatenate(terms + [jnp.zeros((rows - 3, total.shape[1]), f32)], axis=0).astype(bf16)


def row_sum(rows):
    a = rows[:3].astype(f32)
    return (a[:1] + a[1:2]) + a[2:]


def tree(values):
    while len(values) > 1:
        values = [a + b for a, b in zip(values[::2], values[1::2])]
    return values[0]


def scatter_batch(mine, theirs, total):
    n = lax.axis_size("batch")
    me = lax.axis_index("batch")
    rows, c = mine.shape[1:]
    got = partner(theirs, "batch", 1)
    mine = mine + got[:, :rows].astype(f32)
    total = row_sum(exact(total, BLOCK)) + row_sum(got[0, rows:, :LANES])
    pieces = exact(jnp.tile(total, (1, c // LANES)), BLOCK)
    low = jnp.concatenate([mine.astype(bf16), jnp.broadcast_to(pieces[None], (n // 2, BLOCK, c))], axis=1)
    got = [
        partner(lax.dynamic_index_in_dim(low, (me // 2) ^ k, 0, False), "batch", 2 * k) for k in range(1, n // 2)
    ]
    result = lax.dynamic_index_in_dim(mine, me // 2, 0, False)
    for part in got:
        result = result + part[:rows].astype(f32)
    return result, tree([row_sum(exact(total, BLOCK))] + [row_sum(part[rows:, :LANES]) for part in got]), low


def scatter_parts(values, axis):
    n = lax.axis_size(axis)
    if n > 4:
        return [lax.psum_scatter(values[0].astype(f32), axis, scatter_dimension=0)]
    return [values[0]] + [partner(values[k], axis, k) for k in range(1, n)]


def share_parts(value, axis):
    n = lax.axis_size(axis)
    if n > 4:
        return [lax.psum(value.astype(f32), axis)]
    return [value] + [partner(value, axis, k) for k in range(1, n)]


def added(parts):
    total = parts[0].astype(f32)
    for part in parts[1:]:
        total = total + part.astype(f32)
    return total


def sum_everywhere(value, axes):
    for axis in axes:
        k = 1
        while k < lax.axis_size(axis):
            value = value + partner(value, axis, k)
            k *= 2
    return value


def body(
    tokens,
    teacher,
    piece_starts,
    valid_rows,
    norm_gain,
    in_weight,
    conv_weight,
    conv_bias,
    xproj_weight,
    dtproj_weight,
    dt_bias,
    a_log,
    skip_weight,
    out_weight,
):
    seqs = lax.axis_size("seq")
    batches = lax.axis_size("batch")
    _, rows, width = tokens.shape
    total = rows * seqs
    taps, own = conv_weight.shape
    chans = own * batches
    depth = in_weight.shape[0]
    rank = dtproj_weight.shape[0]
    states = a_log.shape[1]
    lines = depth * seqs
    packed = 2 * LANES * own // chans
    place = lax.axis_index("seq") if seqs <= 4 else jnp.int32(0)
    me = place.astype(jnp.int32).reshape(1)
    tok = tokens.reshape(rows, width)

    flags = jnp.concatenate([piece_starts, valid_rows], axis=0).astype(bf16)
    flags = jnp.pad(flags, ((0, 14), (0, width - rows)))
    everything = lax.all_gather(jnp.concatenate([tok, flags], axis=0), "seq")
    split = split_columns(in_weight, norm_gain.reshape(1, depth), valid_rows, seqs, batches, own)
    split = lax.all_to_all(split, "seq", 0, 0).reshape(lines, 2 * chans + LANES)
    vectors = jnp.concatenate(
        [
            dtproj_weight.T,
            a_log,
            conv_weight.T,
            conv_bias[:, None],
            dt_bias[:, None],
            skip_weight[:, None],
        ],
        axis=1,
    )
    vectors = jnp.pad(vectors, ((0, 0), (0, LANES - vectors.shape[1])))
    columns_x = jnp.pad(xproj_weight, ((0, 0), (0, LANES - xproj_weight.shape[1])))
    local = jnp.pad(jnp.concatenate([vectors, columns_x], axis=0), ((0, lines - 2 * own), (chans, 0)))
    second = jnp.concatenate(
        [split[:, chans + LANES :]] + [out_weight[:, k : k + chans] for k in range(0, width, chans)], axis=0
    )
    blocks, places, second = gather_batch(split[:, : chans + LANES] + local, second)
    second = lax.all_gather(second, "batch")


    tile = ((total, chans), f32, "t")
    low_tile = ((total, chans), bf16, "t")
    state = ((total * states, chans), bf16, "t")
    normed, normed_t, stream, conv_pre, act, proj, w_stream, vec, xproj, gain, marks = call(
        start_kernel,
        jnp.concatenate([me] + [p.astype(jnp.int32).reshape(1) for p in places]),
        [(everything, "y")] + [(block, "f") for block in blocks],
        [
            ((total, width), bf16, "t"),
            ((width, total), bf16, "c"),
            low_tile,
            tile,
            low_tile,
            ((total, LANES), bf16, "t"),
            ((width, chans), bf16, "f"),
            ((LANES, chans), f32, "f"),
            ((chans, LANES), bf16, "f"),
            ((1, width), f32, "f"),
            ((1, LANES), f32, "f"),
        ],
        [pltpu.VMEM((ROWS + 8, chans), f32), pltpu.VMEM((width, LANES), f32), pltpu.VMEM((chans, LANES), f32)],
        total,
        rows,
    )
    total_valid = (marks[:, LANES - 2 : LANES - 1] * 128.0 + marks[:, LANES - 1 :]) / depth
    starts = everything[:, rows, :rows].astype(f32).reshape(total)
    running = jnp.cumsum(starts)
    lagged = jnp.concatenate([jnp.zeros((PIECE,), f32), running[: total - PIECE]])
    carry_on = jnp.where(running - lagged > 0.5, 1.0 - starts, 0.0)
    flags = jnp.max(carry_on.reshape(-1, UNROLL * BLOCK), axis=1).astype(jnp.int32)
    teacher, proj = lax.optimization_barrier((teacher, proj))
    per = rows // seqs
    teach_v = lax.all_to_all(teacher.reshape(seqs, per, width), "seq", 0, 0).astype(f32)
    proj = added(share_parts(proj, "seq"))
    me = jnp.concatenate([me, flags])
    proj = jnp.where(jnp.arange(LANES)[None, :] == CARRY, carry_on[:, None], proj)
    groups = (ROWS // BLOCK, states, BLOCK)
    (g,) = call(
        piece_kernel,
        me,
        [(proj, "t"), (act, "t"), (vec, "f")],
        [state],
        [
            pltpu.VMEM((states, chans), f32),
            pltpu.VMEM((ROWS, chans), f32),
            pltpu.VMEM((ROWS, chans), f32),
            pltpu.VMEM(groups, f32),
        ],
        total,
        rows,
        reverse=True,
    )
    halves = 2
    held = seqs // halves * per
    count = total // ROWS // halves
    places = seqs if seqs <= 4 else 1
    if seqs <= 4:
        messages = [((held, width), bf16, "f")] * seqs
    else:
        messages = [((seqs, held, width), bf16, "f")]
    by_time = [state, tile, tile, ((chans, total), bf16, "c")]
    weights = [((width, chans), bf16, "f"), ((chans, width), bf16, "f")]
    mine = lambda v: lax.dynamic_slice_in_dim(v, lax.axis_index("seq") * per, per, axis=1)
    tok_v = mine(everything[:, :rows]).astype(f32)
    valid_v = mine(everything[:, rows + 1, :rows].reshape(seqs, rows, 1)).astype(f32)
    enter = jnp.zeros((states, chans), f32)
    kept = []
    branches = []
    for half in range(halves):
        out = call(
            lambda *refs, half=half: ahead_kernel(half, places, per, rows, *refs),
            me,
            [(proj, "t"), (act, "t"), (normed, "t"), (g, "t"), (vec, "f"), (enter, "f")]
            + ([(w_gate, "f"), (out_w, "f")] if half else [(second, "f")])
            + [(array, "o") for array in kept],
            by_time + [((states, chans), f32, "f")] + ([] if half else weights) + messages,
            [
                pltpu.VMEM((states, chans), f32),
                pltpu.VMEM((ROWS, chans), f32),
                pltpu.VMEM((ROWS, chans), f32),
                pltpu.VMEM(groups, f32),
                pltpu.VMEM((2, ROWS + BLOCK, BLOCK * states), bf16),
                pltpu.VMEM((BLOCK * states, chans), bf16),
                pltpu.VMEM((ROWS + BLOCK, chans), f32),
                pltpu.VMEM((ROWS, width), bf16),
            ],
            total,
            rows,
            first=half * count,
            count=count,
        )
        kept, enter = out[:4], out[4]
        if not half:
            w_gate, out_w = out[5:7]
        branches.append(out[-places:])
    hp, mixed, gate, gated_t = kept

    factor = 2.0 * (total * batches) / total_valid
    squares = jnp.zeros((1, width), f32)
    results, d_branches = [], []
    for half in range(halves):
        at = slice(half * (seqs // halves), (half + 1) * (seqs // halves))
        flat_half = lambda v: v[at].reshape(held, v.shape[2])
        result = flat_half(tok_v) + added(scatter_parts(branches[half], "seq"))
        results.append(result.astype(bf16).reshape(seqs // halves, per, width))
        misfit = result - flat_half(teach_v)
        valid_f = flat_half(valid_v)
        squares = squares + jnp.sum(valid_f * misfit * misfit, axis=0, keepdims=True)
        d_branches.append(gather_parts((factor * valid_f * misfit).astype(bf16), "seq"))
    part = LANES - CARRY
    square_sum = squares[:, :LANES]
    for k in range(LANES, width, LANES):
        square_sum = square_sum + squares[:, k : k + LANES]
    square_sum = sum(square_sum[:, k : k + part] for k in range(0, LANES, part))
    square_sum = jnp.pad(square_sum, ((0, 0), (CARRY, 0)))

    kept = []
    enter = jnp.zeros((states, chans), f32)
    skip_grad = jnp.zeros((1, chans), f32)
    for half in range(halves):
        *kept, skip_grad, enter = call(
            lambda *refs, half=half: piece_grad_kernel(half * count, places, per, rows, *refs),
            me,
            [
                (proj, "t"),
                (act, "t"),
                (mixed, "t"),
                (gate, "t"),
                (vec, "f"),
                (out_w, "f"),
                (enter, "f"),
                (skip_grad, "f"),
            ]
            + [(part, "f") for part in d_branches[half]]
            + [(array, "o") for array in kept],
            [
                state,
                tile,
                low_tile,
                ((total, width), bf16, "t"),
                ((1, chans), f32, "f"),
                ((states, chans), f32, "f"),
            ],
            [pltpu.VMEM((states, chans), f32), pltpu.VMEM((ROWS, chans), f32), pltpu.VMEM(groups, f32)],
            total,
            rows,
            first=half * count,
            count=count,
        )
    q, d_mixed, d_gate, d_branch = kept
    output = lax.all_to_all(jnp.concatenate(results, axis=0), "seq", 0, 0).reshape(rows, width)
    d_result = lax.dynamic_slice_in_dim(d_branch, lax.axis_index("seq") * rows, rows, axis=0).astype(f32)
    early_sum = by_blocks(
        early_grad_kernel,
        batches,
        own,
        [normed_t, gated_t],
        [d_gate, d_branch],
        lines + own * width // chans,
        chans,
    )
    early = lax.psum_scatter(early_sum, "batch", scatter_dimension=0)
    pieces = exact(square_sum, BLOCK)
    d_act, d_proj, table = call(
        state_grad_kernel,
        me,
        [(proj, "t"), (act, "t"), (d_mixed, "t"), (g, "t"), (hp, "t"), (q, "t"), (vec, "f"), (skip_grad, "f"), (pieces, "f")],
        [tile, ((total, LANES), bf16, "t"), ((LANES, chans), f32, "f")],
        [
            pltpu.VMEM((states, chans), f32),
            pltpu.VMEM((HALF, chans), f32),
            pltpu.VMEM((HALF, chans), f32),
            pltpu.VMEM((HALF // BLOCK, states, BLOCK), f32),
            pltpu.VMEM((HALF + BLOCK, BLOCK * states), bf16),
        ]
        + [pltpu.VMEM((BLOCK * states, chans), bf16)] * 2
        + [
            pltpu.VMEM((BLOCK * states, 2 * min(chans, 2 * LANES)), bf16),
            pltpu.VMEM((BLOCK * states, LANES), bf16),
        ]
        + [pltpu.VMEM((HALF + 2 * BLOCK, chans), f32)] * 2
        + [pltpu.VMEM((HALF + 2 * BLOCK, LANES), f32)],
        total,
        rows,
        size=HALF,
        reverse=True,
    )
    d_proj = share_parts(d_proj, "seq")
    slots = slots_out(seqs, rows, width)
    *d_normed, d_stream, small, sent, seq_sum = call(
        lambda *refs: end_kernel(own, rows, len(slots), *refs),
        me,
        [(part, "t") for part in d_proj]
        + [
            (d_act, "t"),
            (conv_pre, "t"),
            (stream, "t"),
            (act, "t"),
            (d_gate, "t"),
            (vec, "f"),
            (xproj, "f"),
            (w_stream, "f"),
            (w_gate, "f"),
            (table, "f"),
        ],
        slots
        + [
            low_tile,
            ((batches * packed, chans), f32, "f"),
            ((BLOCK, chans), bf16, "f"),
            ((1, LANES), f32, "f"),
        ],
        [
            pltpu.VMEM((ROWS + 8, chans), f32),
            pltpu.VMEM((chans, LANES), f32),
            pltpu.VMEM((LANES, chans), f32),
            pltpu.VMEM((chans, LANES), f32),
        ],
        total,
        rows,
        reverse=True,
    )
    if batches <= 8:
        mine, theirs = late_pairs(normed_t, small, d_stream, sent, batches, lines + packed, chans)
        late, square_sum, waiting = scatter_batch(mine, theirs, seq_sum)
    else:
        late = by_blocks(
            late_grad_kernel, batches, own, [normed_t, small], [d_stream], lines + packed, chans
        )
        waiting = late
        late = lax.psum_scatter(late, "batch", scatter_dimension=0)
        square_sum = sum_everywhere(square_sum, ("batch", "seq"))
    loss = jnp.sum(square_sum) / (total_valid * width)[0, 0]
    nothing = waiting[0, :1].astype(f32) * 0.0
    d_normed = added([jnp.tile(nothing, (1, width // chans))] + scatter_parts(d_normed, "seq"))
    in_out = jnp.concatenate([late[:lines], early[:lines]], axis=1).astype(bf16)
    in_out = lax.all_to_all(in_out.reshape(seqs, depth, 2 * chans), "seq", 0, 0)
    in_out, gain_out, xproj_out, dt_out, alog_out, conv_out, convb_out, dtb_out, skip_out = join_columns(
        in_out, late[lines:], in_weight, norm_gain.reshape(1, depth), batches, own
    )
    out_out = early[lines:].reshape(-1, own, chans).transpose(1, 0, 2).reshape(own, width)
    tok_f = tok.astype(f32)
    mean_sq = jnp.mean(tok_f * tok_f, axis=-1, keepdims=True)
    root_inv = lax.rsqrt(mean_sq + 1e-05)
    own_unit = tok_f * root_inv
    scaled = d_normed * gain
    input_grad = d_result + root_inv * (scaled - own_unit * jnp.mean(scaled * own_unit, axis=-1, keepdims=True))
    return (
        output[None],
        loss,
        input_grad[None],
        gain_out[0],
        in_out,
        conv_out,
        convb_out[0],
        xproj_out,
        dt_out,
        dtb_out[0],
        alog_out,
        skip_out[0],
        out_out,
    )


def solution(mesh):
    return jax.shard_map(
        body,
        mesh=mesh,
        in_specs=(
            P("batch", "seq", None),
            P("batch", "seq", None),
            P("batch", "seq"),
            P("batch", "seq"),
            P(("batch", "seq")),
            P(("batch", "seq"), None),
            P(None, ("batch", "seq")),
            P(("batch", "seq")),
            P(("batch", "seq"), None),
            P(None, ("batch", "seq")),
            P(("batch", "seq")),
            P(("batch", "seq"), None),
            P(("batch", "seq")),
            P(("batch", "seq"), None),
        ),
        out_specs=(
            P("batch", "seq", None),
            P(),
            P("batch", "seq", None),
            P(("batch", "seq")),
            P(("batch", "seq"), None),
            P(None, ("batch", "seq")),
            P(("batch", "seq")),
            P(("batch", "seq"), None),
            P(None, ("batch", "seq")),
            P(("batch", "seq")),
            P(("batch", "seq"), None),
            P(("batch", "seq")),
            P(("batch", "seq"), None),
        ),
        check_vma=False,
    )
```

```python
import jax
import jax.numpy as jnp
from jax import lax
from jax.experimental import pallas as pl
from jax.experimental.pallas import tpu as pltpu
from jax.sharding import PartitionSpec as P

PIECE = 256
BLOCK = 16
UNROLL = 4
ROWS = 256
HALF = 128
LOG2E = 1.4426950408889634
LN2 = 0.6931471805599453
NEVER = 1e9
LANES = 128
f32 = jnp.float32
bf16 = jnp.bfloat16

ALOG, CONV, CONVB, DTB, SKIP = 64, 80, 84, 85, 86
INTO, OUT, CARRY = 64, 80, 96


def dot(a, b):
    return jnp.dot(a, b, preferred_element_type=f32)


def dot_t(a, b):
    return lax.dot_general(a, b, (((1,), (1,)), ((), ())), preferred_element_type=f32)


def t_dot(a, b):
    return lax.dot_general(a, b, (((0,), (0,)), ((), ())), preferred_element_type=f32)


def sigmoid(v):
    return 1.0 / (1.0 + jnp.exp(-v))


def row_of(ref, t, n):
    return jnp.broadcast_to(ref[pl.ds(t, 1), :], (n, ref.shape[1]))


def col_of(block, tt, c):
    return jnp.broadcast_to(block[:, tt : tt + 1], (block.shape[0], c))


def rates_of(vec_ref, n):
    return -jnp.exp(vec_ref[ALOG : ALOG + n, :]) * LOG2E


def dt_of(proj, vec_ref, rank):
    low = proj[:, :rank].astype(bf16)
    return low, dot(low, vec_ref[:rank, :].astype(bf16)) + vec_ref[DTB : DTB + 1, :]


def softplus(v):
    return jnp.maximum(v, 0.0) + jnp.log1p(jnp.exp(-jnp.abs(v)))


def slope_of(step):
    small = step * (1.0 - step * (0.5 - step * (1.0 / 6.0 - step * (1.0 / 24.0))))
    return jnp.where(step < 0.02, small, 1.0 - jnp.exp(-step))


def columns(proj_t, first, n, into_ref):
    for j in range(into_ref.shape[0]):
        into_ref[j] = proj_t[first : first + n, j * BLOCK : (j + 1) * BLOCK]


def block_diag(values, n):
    rows, wide = values.shape[0], BLOCK * n
    spread = (
        lax.broadcasted_iota(jnp.int32, (n, wide), 1) % n == lax.broadcasted_iota(jnp.int32, (n, wide), 0)
    ).astype(f32).astype(bf16)
    keep = lax.broadcasted_iota(jnp.int32, (rows, wide), 1) // n == lax.broadcasted_iota(
        jnp.int32, (rows, wide), 0
    ) % BLOCK
    return jnp.where(keep, dot(values, spread), 0.0).astype(bf16)


def unit_of(x):
    return x * lax.rsqrt(jnp.mean(x * x, axis=-1, keepdims=True) + 1e-05)


def start_kernel(count, me_ref, x_ref, *refs):
    bottom, parts = refs[:count], refs[count:-14]
    (
        normed_ref, turned_ref, stream_ref, pre_ref, act_ref, proj_ref, w_ref, vec_ref, xproj_ref, gain_ref, marks_ref,
        wide_ref, ext_ref, cols_ref,
    ) = refs[-14:]
    rows, chans = stream_ref.shape
    taps = CONVB - CONV

    @pl.when(pl.program_id(0) == 0)
    def _():
        wide_ref[:8, :] = jnp.zeros((8, chans), f32)
        place = 1
        for part in parts:
            count, lines, _ = part.shape
            own = chans * lines // w_ref.shape[0]
            for k in range(count):
                block = me_ref[place]
                place += 1
                at = pl.ds(pl.multiple_of(block * lines, lines), lines)
                w_ref[at, :] = part[k, :, :chans]
                ext = part[k, :, chans:].astype(f32)
                ext_ref[at, :] = ext
                at = pl.ds(pl.multiple_of(block * own, own), own)
                cols_ref[at, :] = ext[:own]
                used = lax.broadcasted_iota(jnp.int32, (own, LANES), 1) < CARRY
                xproj_ref[at, :] = jnp.where(used, ext[own : 2 * own], 0.0).astype(bf16)
        for k in range(w_ref.shape[0] // LANES):
            at = slice(k * LANES, (k + 1) * LANES)
            gain_ref[:, at] = ext_ref[at, :].T[LANES - 3 : LANES - 2]
        for k in range(chans // LANES):
            at = slice(k * LANES, (k + 1) * LANES)
            vec_ref[:, at] = cols_ref[at, :].T
        marks_ref[...] = jnp.sum(ext_ref[...], axis=0, keepdims=True)

    x = x_ref[...]
    if count:
        x = jnp.concatenate([x, read_slot(bottom, pl.program_id(0) ^ me_ref[0])], axis=0)
    normed = (unit_of(x.astype(f32)) * gain_ref[...]).astype(bf16)
    normed_ref[...] = normed
    turned_ref[...] = normed.T
    stream = dot(normed, w_ref[...]).astype(bf16)
    stream_ref[...] = stream
    wide_ref[8:, :] = stream.astype(f32)
    pre = jnp.broadcast_to(vec_ref[CONVB : CONVB + 1, :], (rows, chans))
    for tap in range(taps):
        first = 8 - taps + 1 + tap
        pre = pre + vec_ref[CONV + tap : CONV + tap + 1, :] * wide_ref[first : first + rows, :]
    wide_ref[:8, :] = wide_ref[rows:, :]
    pre_ref[...] = pre
    act = (pre * sigmoid(pre)).astype(bf16)
    act_ref[...] = act
    proj_ref[...] = dot(act, xproj_ref[...]).astype(bf16)


def several(block):
    def blocks(i, carry):
        for k in range(UNROLL):
            carry = block(UNROLL * i + k, carry)
        return carry

    return blocks


def piece_kernel(me_ref, proj_ref, act_ref, vec_ref, g_ref, step_ref, carry_ref, u_ref, stepm_ref, col_ref):
    rows, c = act_ref.shape
    n = carry_ref.shape[0]

    @pl.when(pl.program_id(0) == 0)
    def _():
        carry_ref[...] = jnp.zeros_like(carry_ref)

    proj = proj_ref[...]
    _, pre = dt_of(proj, vec_ref, INTO)
    step = softplus(pre)
    step_ref[...] = step
    u_ref[...] = step * act_ref[...].astype(f32)
    stepm_ref[...] = jnp.where(proj[:, CARRY : CARRY + 1] > 0.5, step, NEVER)
    columns(proj.T, INTO, n, col_ref)
    r2 = rates_of(vec_ref, n)

    def block(i, carry):
        j = rows // BLOCK - 1 - i
        into = col_ref[j]
        for tt in reversed(range(BLOCK)):
            t = j * BLOCK + tt
            g = row_of(u_ref, t, n) * col_of(into, tt, c) + carry
            g_ref[pl.ds(pl.multiple_of(t * n, n), n), :] = g.astype(bf16)
            carry = jnp.exp2(row_of(stepm_ref, t, n) * r2) * g
        return carry

    carry_ref[...] = lax.fori_loop(0, rows // BLOCK // UNROLL, several(block), carry_ref[...])


def ahead_kernel(
    first, places, per, local, me_ref, *refs,
):
    proj_ref, act_ref, normed_ref, g_ref, step_ref, vec_ref, enter_ref = refs[:7]
    if first:
        wgate_ref, outw_ref = refs[7:9]
        hp_ref, mixed_ref, gate_ref, gated_ref, leave_ref = refs[-7 - places - 5 : -7 - places]
    else:
        second_ref = refs[7]
        hp_ref, mixed_ref, gate_ref, gated_ref, leave_ref, wgate_ref, outw_ref = refs[-7 - places - 7 : -7 - places]
    branch_refs = refs[-7 - places : -7]
    carry_ref, u_ref, col_ref, diag_ref, s_ref, y_ref, out_ref = refs[-7:]
    rows, c = act_ref.shape
    n = carry_ref.shape[0]

    @pl.when(pl.program_id(0) == 0)
    def _():
        carry_ref[...] = enter_ref[...]
        if first:
            return
        blocks = second_ref.shape[0]
        lines, own = wgate_ref.shape[0] // blocks, outw_ref.shape[0] // blocks
        for b in range(blocks):
            wgate_ref[b * lines : (b + 1) * lines, :] = second_ref[b, :lines, :]
            for k in range(outw_ref.shape[1] // c):
                outw_ref[b * own : (b + 1) * own, k * c : (k + 1) * c] = second_ref[
                    b, lines + k * own : lines + (k + 1) * own, :
                ]

    proj = proj_ref[...]
    act = act_ref[...].astype(f32)
    u_ref[...] = step_ref[...] * act
    columns(proj.T, INTO, n, col_ref)
    read = proj[:, OUT : OUT + n]
    high = read.astype(bf16)
    diag_ref[0, BLOCK:] = block_diag(high, n)
    diag_ref[1, BLOCK:] = block_diag((read - high.astype(f32)).astype(bf16), n)
    r2 = rates_of(vec_ref, n)

    def read_out(j):
        r16 = pl.ds(pl.multiple_of(j * BLOCK, BLOCK), BLOCK)
        both = dot(jnp.concatenate([diag_ref[0, r16, :], diag_ref[1, r16, :]], axis=0), s_ref[...])
        y_ref[r16, :] = both[:BLOCK] + both[BLOCK:]

    def block(j, h):
        read_out(j)
        into = col_ref[j]
        for tt in range(BLOCK):
            t = j * BLOCK + tt
            at = pl.ds(pl.multiple_of(t * n, n), n)
            hp = jnp.exp2(row_of(step_ref, t, n) * r2) * h
            h = hp + row_of(u_ref, t, n) * col_of(into, tt, c)
            hp_ref[at, :] = hp.astype(bf16)
            s_ref[tt * n : (tt + 1) * n, :] = (hp + g_ref[at, :].astype(f32)).astype(bf16)
        return h

    carry_ref[...] = lax.fori_loop(0, rows // BLOCK // UNROLL, several(block), carry_ref[...])
    read_out(rows // BLOCK)
    mixed = y_ref[BLOCK:] + vec_ref[SKIP : SKIP + 1, :] * act
    mixed_ref[...] = mixed
    gate = dot(normed_ref[...], wgate_ref[...])
    gate_ref[...] = gate
    gated = (mixed * (gate * sigmoid(gate))).astype(bf16)
    gated_ref[...] = gated.T
    out_ref[...] = dot(gated, outw_ref[...]).astype(bf16)
    write_rows(branch_refs, me_ref, places, per, local, rows, out_ref)
    leave_ref[...] = carry_ref[...]


def piece_grad_kernel(
    first, places, per, local, me_ref, *refs,
):
    proj_ref, act_ref, mixed_ref, gate_ref, step_ref, vec_ref, outw_ref, enter_ref, before_ref = refs[:9]
    db_refs = refs[9 : 9 + places]
    q_ref, dm_ref, dg_ref, db_ref, sgrad_ref, leave_ref = refs[-9:-3]
    carry_ref, stepm_ref, col_ref = refs[-3:]
    rows, c = act_ref.shape
    n = carry_ref.shape[0]

    @pl.when(pl.program_id(0) == 0)
    def _():
        carry_ref[...] = enter_ref[...]
        sgrad_ref[...] = before_ref[...]

    proj = proj_ref[...]
    stepm_ref[...] = jnp.where(proj[:, CARRY : CARRY + 1] > 0.5, step_ref[...], NEVER)
    columns(proj.T, OUT, n, col_ref)
    db = read_rows(db_refs, me_ref, places, per, local, rows)
    db_ref[...] = db
    dgated = dot_t(db, outw_ref[...])
    gate = gate_ref[...]
    s = sigmoid(gate)
    dm = dgated * (gate * s)
    dm_ref[...] = dm
    dg = (dgated * mixed_ref[...] * (s * (1.0 + gate * (1.0 - s)))).astype(bf16)
    dg_ref[...] = dg
    sgrad_ref[...] += jnp.sum(dm * act_ref[...].astype(f32), axis=0, keepdims=True)
    r2 = rates_of(vec_ref, n)

    chunk = first + pl.program_id(0)

    size = UNROLL * BLOCK

    def scan(i, w):
        for k in range(UNROLL):
            j = UNROLL * i + k
            read = col_ref[j]
            for tt in range(BLOCK):
                t = j * BLOCK + tt
                q = jnp.exp2(row_of(stepm_ref, t, n) * r2) * w
                q_ref[pl.ds(pl.multiple_of(t * n, n), n), :] = q.astype(bf16)
                w = q + row_of(dm_ref, t, n) * col_of(read, tt, c)
        return w

    def fill(i, w):
        for k in range(UNROLL):
            at = pl.ds(pl.multiple_of((UNROLL * i + k) * BLOCK * n, BLOCK * n), BLOCK * n)
            q_ref[at, :] = jnp.zeros((BLOCK * n, c), bf16)
        return row_of(dm_ref, (i + 1) * size - 1, n) * col_of(col_ref[(i + 1) * UNROLL - 1], BLOCK - 1, c)

    def group(i, w):
        return lax.cond(me_ref[1 + chunk * (rows // size) + i] > 0, scan, fill, i, w)

    carry_ref[...] = lax.fori_loop(0, rows // size, group, carry_ref[...])
    leave_ref[...] = carry_ref[...]


def state_grad_kernel(
    me_ref, proj_ref, act_ref, dm_ref, g_ref, hp_ref, q_ref, step_ref, vec_ref, sgrad_ref, pieces_ref,
    dact_ref, dproj_ref, table_ref,
    carry_ref, u_ref, col_ref, diag_ref, ig_ref, rr_ref, pair_ref, own_ref, x_ref, y_ref, dp_ref,
):
    rows, c = act_ref.shape
    n = carry_ref.shape[0]
    wide = BLOCK * n

    @pl.when(pl.program_id(0) == 0)
    def _():
        carry_ref[...] = jnp.zeros_like(carry_ref)
        table_ref[...] = jnp.zeros_like(table_ref)
        table_ref[SKIP : SKIP + 1, :] = sgrad_ref[...]

    proj = proj_ref[...]
    act = act_ref[...].astype(f32)
    low = proj[:, :INTO].astype(bf16)
    u_ref[...] = step_ref[...] * act
    columns(proj.T, OUT, n, col_ref)
    diag_ref[:rows] = block_diag(proj[:, INTO : INTO + n].astype(bf16), n)
    r2 = rates_of(vec_ref, n)
    iota = lambda shape, axis: lax.broadcasted_iota(jnp.int32, shape, axis)
    mask = lambda v: v.astype(f32).astype(bf16)
    by_row = mask(iota((BLOCK, wide), 1) // n == iota((BLOCK, wide), 0))
    part = min(c, 2 * LANES)
    which = mask(iota((2 * part, LANES), 0) // part == iota((2 * part, LANES), 1) // n % 2)
    own_lane = iota((wide, LANES), 1) % n == iota((wide, LANES), 0) % n

    def sums(j):
        r16 = pl.ds(pl.multiple_of(j * BLOCK, BLOCK), BLOCK)
        x_ref[r16, :] = dot(diag_ref[r16, :], ig_ref[...])
        y_ref[r16, :] = dot(by_row, rr_ref[...])
        dp_ref[pl.ds(pl.multiple_of((j + 1) * BLOCK, BLOCK), BLOCK), :] = dot(by_row, own_ref[...])
        own_ref[...] = jnp.where(own_lane, dot(pair_ref[...], which), 0.0).astype(bf16)

    def block(i, both):
        m, al = both
        j = rows // BLOCK - 1 - i
        sums(j + 1)
        read = col_ref[j]
        for tt in reversed(range(BLOCK)):
            t = j * BLOCK + tt
            at = pl.ds(pl.multiple_of(t * n, n), n)
            loc = slice(tt * n, (tt + 1) * n)
            drow = row_of(dm_ref, t, n)
            mu = m + drow * col_of(read, tt, c)
            srow = row_of(step_ref, t, n)
            m = jnp.exp2(srow * r2) * mu
            low_mu = mu.astype(bf16)
            q = q_ref[at, :]
            g = g_ref[at, :]
            hp = hp_ref[at, :]
            rg = low_mu * hp + q * g
            ig = low_mu + q
            ig_ref[loc, :] = ig
            rg = rg.astype(f32)
            al = al + rg * srow
            rr_ref[loc, :] = (rg * r2).astype(bf16)
            pb = ig * row_of(u_ref, t, n).astype(bf16)
            pc = (hp + g) * drow.astype(bf16)
            sb, sc = pb[:, :part], pc[:, :part]
            for k in range(1, c // part):
                sb = sb + pb[:, k * part : (k + 1) * part]
                sc = sc + pc[:, k * part : (k + 1) * part]
            pair_ref[loc, :part] = sb
            pair_ref[loc, part:] = sc
        return m, al

    m, al = lax.fori_loop(0, rows // BLOCK, block, (carry_ref[...], table_ref[ALOG : ALOG + n, :]))
    carry_ref[...] = m
    table_ref[ALOG : ALOG + n, :] = al
    sums(0)
    dp_ref[:BLOCK, :] = dot(by_row, own_ref[...])
    xs = x_ref[:rows]
    dact_ref[...] = step_ref[...] * xs + vec_ref[SKIP : SKIP + 1, :] * dm_ref[...]
    dpre = (y_ref[:rows] * LN2 + act * xs) * slope_of(step_ref[...])
    table_ref[DTB : DTB + 1, :] += jnp.sum(dpre, axis=0, keepdims=True)
    dpre_low = dpre.astype(bf16)
    table_ref[:INTO, :] += t_dot(low, dpre_low)
    dproj_ref[...] = dp_ref[:rows].astype(bf16)
    dproj_ref[:, :INTO] = dot_t(dpre_low, vec_ref[:INTO, :].astype(bf16)).astype(bf16)

    @pl.when(pl.program_id(0) == pl.num_programs(0) - 1)
    def _():
        dproj_ref[:BLOCK, CARRY:] = pieces_ref[:, CARRY:]
        table_ref[ALOG : ALOG + n, :] *= -jnp.exp(vec_ref[ALOG : ALOG + n, :])


def end_kernel(own, local, count, paired, me_ref, *refs):
    sent = 2 if paired else 1
    dn_refs, refs = refs[-count - sent - 6 : -sent - 6], refs[: -count - sent - 6] + refs[-sent - 6 :]
    late_refs, refs = refs[-sent - 6 : -6], refs[: -sent - 6] + refs[-6:]
    parts = refs[:-17]
    (
        dact_ref, pre_ref, stream_ref, act_ref, dg_ref, vec_ref, xproj_ref, ws_ref, wg_ref, table_ref, normed_ref,
        sum_ref,
        wide_ref, xgrad_ref, cgrad_ref, turned_ref, grad_ref,
    ) = refs[-17:]
    rows, c = act_ref.shape
    taps = CONVB - CONV

    @pl.when(pl.program_id(0) == 0)
    def _():
        wide_ref[rows:, :] = jnp.zeros((8, c), f32)
        xgrad_ref[...] = jnp.zeros_like(xgrad_ref)
        cgrad_ref[...] = table_ref[...]
        grad_ref[...] = jnp.zeros_like(grad_ref)

    dproj = parts[0][...].astype(f32)
    for part in parts[1:]:
        dproj = dproj + part[...].astype(f32)
    used = lax.broadcasted_iota(jnp.int32, dproj.shape, 1) < CARRY
    dproj = jnp.where(used, dproj, 0.0).astype(bf16)
    pre = pre_ref[...]
    s = sigmoid(pre)
    dconv = (dact_ref[...] + dot_t(dproj, xproj_ref[...])) * (s * (1.0 + pre * (1.0 - s)))
    wide_ref[:rows, :] = dconv
    xgrad_ref[...] += t_dot(act_ref[...], dproj)
    cgrad_ref[CONVB : CONVB + 1, :] += jnp.sum(dconv, axis=0, keepdims=True)
    stream = stream_ref[...].astype(f32)
    dstream = jnp.zeros((rows, c), f32)
    for tap in range(taps):
        back = taps - 1 - tap
        moved = wide_ref[back : back + rows, :]
        cgrad_ref[CONV + tap : CONV + tap + 1, :] += jnp.sum(stream * moved, axis=0, keepdims=True)
        dstream = dstream + vec_ref[CONV + tap : CONV + tap + 1, :] * moved
    wide_ref[rows:, :] = dconv[:8, :]
    dstream_low = dstream.astype(bf16)
    dn = (dot_t(dstream_low, ws_ref[...]) + dot_t(dg_ref[...], wg_ref[...])).astype(bf16)
    write_slot(dn_refs, slot_of(me_ref, local, True), dn)
    grad_ref[...] += dot(normed_ref[...], dstream_low)

    @pl.when(pl.program_id(0) == pl.num_programs(0) - 1)
    def _():
        for k in range(c // LANES):
            at = slice(k * LANES, (k + 1) * LANES)
            turned_ref[at, :] = cgrad_ref[:, at].T
        sums = tree([row_sum(part[:BLOCK, :]) for part in parts])
        sums = jnp.where(lax.broadcasted_iota(jnp.int32, sums.shape, 1) < CARRY, 0.0, sums)
        sum_ref[...] = sums
        pieces = [jnp.zeros((BLOCK, LANES), f32)]
        row = lax.broadcasted_iota(jnp.int32, (BLOCK, LANES), 0)
        for k in range(3):
            term = sums.astype(bf16).astype(f32)
            pieces = [jnp.where(row == k, term, pieces[0])]
            sums = sums - term
        pieces = jnp.concatenate([pieces[0].astype(bf16)] * (c // LANES), axis=1)
        packed, lines = 2 * own * LANES // c, grad_ref.shape[0] * own // c

        def block(b):
            at = slice(b * own, (b + 1) * own)
            both = jnp.concatenate([xgrad_ref[at, :], turned_ref[at, :]], axis=0)
            small = [both[k * packed : (k + 1) * packed] for k in range(c // LANES)]
            return grad_ref[b * lines : (b + 1) * lines, :], jnp.concatenate(small, axis=1)

        if not paired:
            for b in range(c // own):
                late_refs[0][b, :lines, :], late_refs[0][b, lines:, :] = block(b)
            return
        mine_ref, theirs_ref = late_refs
        first = me_ref[me_ref.shape[0] - 1] == 0
        for z in range(c // own // 2):
            for part, at, end in zip(zip(block(2 * z), block(2 * z + 1)), (0, lines), (lines, lines + packed)):
                mine_ref[z, at:end, :] = jnp.where(first, part[0], part[1])
                theirs_ref[z, at:end, :] = jnp.where(first, part[1], part[0]).astype(bf16)
            theirs_ref[z, lines + packed :, :] = pieces


def slot_of(me_ref, local, reverse=False):
    step = pl.program_id(0)
    if reverse:
        step = pl.num_programs(0) - 1 - step
    return (step // (local // ROWS)) ^ me_ref[0]


def read_rows(refs, me_ref, places, per, local, size):
    step = pl.program_id(0)
    each = size // per
    at = pl.ds(pl.multiple_of(step // (local // size) * per, per), per)
    pieces = []
    for p in range(each):
        j = step % (local // size) * each + p
        if len(refs) == 1:
            pieces.append(refs[0][j, at, :])
            continue
        value = refs[0][at, :]
        for k in range(1, places):
            value = jnp.where(j ^ me_ref[0] == k, refs[k][at, :], value)
        pieces.append(value)
    return jnp.concatenate(pieces, axis=0)


def read_slot(refs, slot):
    value = refs[0][...]
    for k in range(1, len(refs)):
        value = jnp.where(slot == k, refs[k][...], value)
    return value


def write_rows(refs, me_ref, places, per, local, size, from_ref):
    step = pl.program_id(0)
    each = size // per
    at = pl.ds(pl.multiple_of(step // (local // size) * per, per), per)
    sub = step % (local // size)
    if len(refs) == 1:
        for p in range(each):
            refs[0][sub * each + p, at, :] = from_ref[p * per : (p + 1) * per, :]
        return
    for k, ref in enumerate(refs):
        j = k ^ me_ref[0]

        @pl.when(j // each == sub)
        def _(ref=ref, j=j):
            ref[at, :] = from_ref[pl.ds(pl.multiple_of(j % each * per, per), per), :]


def write_slot(refs, slot, value):
    if len(refs) == 1:
        refs[0][...] = value
        return
    for k, ref in enumerate(refs):

        @pl.when(slot == k)
        def _(ref=ref):
            ref[...] = value


def call(kernel, me, ins, outs, scratch, total, local, reverse=False, first=0, count=None, size=ROWS):
    steps = total // size
    per = local // size
    turn = (lambda i: steps - 1 - i) if reverse else (lambda i: i + first)
    aliases = {}
    for index, (_, kind) in enumerate(ins):
        if kind == "o":
            aliases[index + 1] = len(aliases)

    def slot_map(k):
        def index(i, me_ref):
            group = k ^ me_ref[0]
            if reverse:
                group = steps // per - 1 - group
            first, last = (per - 1, 0) if reverse else (0, per - 1)
            now = i // per
            return (jnp.where(now < group, first, jnp.where(now > group, last, turn(i) % per)), 0)

        return index

    def spec(shape, kind):
        if isinstance(kind, int):
            return pl.BlockSpec((size, shape[1]), slot_map(kind))
        if kind == "f":
            return pl.BlockSpec(shape, lambda i, me_ref: (0,) * len(shape))
        if kind == "o":
            return pl.BlockSpec(memory_space=pl.ANY)
        if kind == "c":
            return pl.BlockSpec(
                (shape[0], size), lambda i, me_ref: (0, turn(i))
            )
        if isinstance(kind, tuple):
            return pl.BlockSpec(
                (None, min(size, kind[1]), shape[2]), lambda i, me_ref: (turn(i) // per, turn(i) % per, 0)
            )
        if kind == "x":
            return pl.BlockSpec(
                (None, size, shape[2]), lambda i, me_ref: ((turn(i) // per) ^ me_ref[0], turn(i) % per, 0)
            )
        return pl.BlockSpec((shape[0] // steps, shape[1]), lambda i, me_ref: (turn(i), 0))

    return pl.pallas_call(
        kernel,
        out_shape=[jax.ShapeDtypeStruct(s, d) for s, d, _ in outs],
        grid_spec=pltpu.PrefetchScalarGridSpec(
            num_scalar_prefetch=1,
            grid=(count or steps,),
            in_specs=[spec(a.shape, k) for a, k in ins],
            out_specs=[spec(s, k) for s, _, k in outs],
            scratch_shapes=scratch,
        ),
        input_output_aliases=aliases,
        compiler_params=pltpu.CompilerParams(dimension_semantics=("arbitrary",), vmem_limit_bytes=60 << 20),
    )(me, *[a for a, _ in ins])


def slots_in(parts):
    if len(parts) == 1:
        return [(parts[0], "x")]
    return [(part, k) for k, part in enumerate(parts)]


def slots_out(seqs, rows, width):
    if seqs > 4:
        return [((seqs, rows, width), bf16, "x")]
    return [((rows, width), bf16, k) for k in range(seqs)]


def early_grad_kernel(normed_ref, gated_ref, dg_ref, *refs):
    parts, out_ref = refs[:-1], refs[-1]
    group, _, c = out_ref.shape
    lines, own = normed_ref.shape[0] // group, gated_ref.shape[0] // group
    gate = dot(normed_ref[...], dg_ref[...])
    out, first = 0.0, 0
    for part in parts:
        last = first + part.shape[0]
        out = out + dot(gated_ref[:, first:last], part[...])
        first = last
    for b in range(group):
        out_ref[b, :lines, :] = gate[b * lines : (b + 1) * lines]
        for k in range(out.shape[1] // c):
            out_ref[b, lines + k * own : lines + (k + 1) * own, :] = out[
                b * own : (b + 1) * own, k * c : (k + 1) * c
            ]


def by_blocks(kernel, batches, own, columns, whole, rows, chans):
    group = LANES // own
    steps = batches // group

    def spec(array, cut):
        if cut:
            return pl.BlockSpec((array.shape[0] // steps, array.shape[1]), lambda i: (i, 0))
        return pl.BlockSpec(array.shape, lambda i: (0,) * array.ndim)

    return pl.pallas_call(
        kernel,
        out_shape=jax.ShapeDtypeStruct((batches, rows, chans), f32),
        grid=(steps,),
        in_specs=[spec(a, True) for a in columns] + [spec(a, False) for a in whole],
        out_specs=pl.BlockSpec((group, rows, chans), lambda i: (i, 0, 0)),
        compiler_params=pltpu.CompilerParams(dimension_semantics=("arbitrary",), vmem_limit_bytes=60 << 20),
    )(*columns, *whole)


def split_kernel(seqs, batches, own, w_ref, gain_ref, valid_ref, out_ref):
    depth, half, chans = w_ref.shape[0], w_ref.shape[1] // 2, batches * own
    count = jnp.sum(valid_ref[...].astype(f32), keepdims=True)
    high = jnp.floor(count * (1.0 / 128.0))
    iota = lambda shape, axis: lax.broadcasted_iota(jnp.int32, shape, axis)
    gain = jnp.broadcast_to(gain_ref[...].astype(f32), (depth, depth))
    gain = jnp.where(iota((depth, depth), 0) == iota((depth, depth), 1), gain, 0.0)
    gain = jnp.sum(gain, axis=1, keepdims=True)
    lane = iota((depth, LANES), 1)
    extra = jnp.where(lane == LANES - 3, gain, 0.0)
    extra = jnp.where(lane == LANES - 2, high, extra)
    extra = jnp.where(lane == LANES - 1, count - high * 128.0, extra).astype(bf16)
    for s in range(seqs):
        for k in range(2):
            pieces = [
                w_ref[:, k * half + (b * seqs + s) * own : k * half + (b * seqs + s + 1) * own].astype(f32)
                for b in range(batches)
            ]
            first = k * (chans + LANES)
            out_ref[s, :, first : first + chans] = jnp.concatenate(pieces, axis=1).astype(bf16)
        out_ref[s, :, chans : chans + LANES] = extra


def split_columns(weight, gain, valid, seqs, batches, own):
    shape = jax.ShapeDtypeStruct((seqs, weight.shape[0], 2 * batches * own + LANES), bf16)
    return pl.pallas_call(lambda *refs: split_kernel(seqs, batches, own, *refs), out_shape=shape)(weight, gain, valid)


def join_kernel(
    batches, both_ref, small_ref, w_ref, gain_ref,
    out_ref, gain_out_ref, xproj_ref, dt_ref, alog_ref, conv_ref, convb_ref, dtb_ref, skip_ref,
):
    seqs, half = both_ref.shape[0], w_ref.shape[1] // 2
    chans = half // seqs
    own = chans // batches
    for k in range(2):
        whole = [both_ref[s, :, k * chans : (k + 1) * chans].astype(f32) for s in range(seqs)]
        pieces = [whole[s][:, b * own : (b + 1) * own] for b in range(batches) for s in range(seqs)]
        out_ref[:, k * half : (k + 1) * half] = jnp.concatenate(pieces, axis=1)
    products = out_ref[...] * w_ref[...].astype(f32)
    depth = products.shape[0]
    sums = jnp.broadcast_to(jnp.sum(products, axis=1, keepdims=True), (depth, depth))
    eye = lax.broadcasted_iota(jnp.int32, (depth, depth), 0) == lax.broadcasted_iota(jnp.int32, (depth, depth), 1)
    gain_out_ref[...] = jnp.sum(jnp.where(eye, sums, 0.0), axis=0, keepdims=True) / gain_ref[...].astype(f32)
    small = small_ref[...]
    both = jnp.concatenate([small[:, k : k + LANES] for k in range(0, chans, LANES)], axis=0)
    xproj_ref[...] = both[:own, :CARRY]
    table = both[own:]
    alog_ref[...] = table[:, ALOG:CONV]
    table = jnp.concatenate([table, jnp.zeros((LANES - own, LANES), f32)], axis=0).T[:, :own]
    dt_ref[...] = table[:INTO]
    conv_ref[...] = table[CONV:CONVB]
    convb_ref[...] = table[CONVB : CONVB + 1]
    dtb_ref[...] = table[DTB : DTB + 1]
    skip_ref[...] = table[SKIP : SKIP + 1]


def join_columns(both, small, weight, gain, batches, own):
    depth = weight.shape[0]
    shapes = [weight.shape, (1, depth), (own, CARRY), (INTO, own), (own, CONV - ALOG), (CONVB - CONV, own)]
    shapes += [(1, own)] * 3
    return pl.pallas_call(
        lambda *refs: join_kernel(batches, *refs), out_shape=[jax.ShapeDtypeStruct(s, f32) for s in shapes]
    )(both, small, weight, gain)


def partner(value, axis, k):
    return lax.ppermute(value, axis, [(i, i ^ k) for i in range(lax.axis_size(axis))])


def gather_parts(value, axis):
    n = lax.axis_size(axis)
    if n > 4:
        return [lax.all_gather(value, axis)]
    return [value] + [partner(value, axis, k) for k in range(1, n)]


def gather_batch(value, after):
    n = lax.axis_size("batch")
    if n > 8:
        return [lax.all_gather(value, "batch")], [jnp.int32(k) for k in range(n)], after
    me = lax.axis_index("batch")
    chips = jnp.stack([value] + [partner(value, "batch", 2 * k) for k in range(1, n // 2)])
    other = partner(chips, "batch", 1)
    places = [me ^ (2 * k) for k in range(n // 2)] + [me ^ (2 * k + 1) for k in range(n // 2)]
    return [chips, other], places, after


def exact(total, rows):
    terms = []
    for _ in range(3):
        term = lax.reduce_precision(total, 8, 7)
        terms.append(term)
        total = total - term
    return jnp.concatenate(terms + [jnp.zeros((rows - 3, total.shape[1]), f32)], axis=0).astype(bf16)


def row_sum(rows):
    a = rows[:3].astype(f32)
    return (a[:1] + a[1:2]) + a[2:]


def tree(values):
    while len(values) > 1:
        values = [a + b for a, b in zip(values[::2], values[1::2])]
    return values[0]


def scatter_batch(mine, theirs, total):
    n = lax.axis_size("batch")
    me = lax.axis_index("batch")
    rows, c = mine.shape[1:]
    got = partner(theirs, "batch", 1)
    mine = mine + got[:, :rows].astype(f32)
    total = row_sum(exact(total, BLOCK)) + row_sum(got[0, rows:, :LANES])
    pieces = exact(jnp.tile(total, (1, c // LANES)), BLOCK)
    low = jnp.concatenate([mine.astype(bf16), jnp.broadcast_to(pieces[None], (n // 2, BLOCK, c))], axis=1)
    got = [
        partner(lax.dynamic_index_in_dim(low, (me // 2) ^ k, 0, False), "batch", 2 * k) for k in range(1, n // 2)
    ]
    result = lax.dynamic_index_in_dim(mine, me // 2, 0, False)
    for part in got:
        result = result + part[:rows].astype(f32)
    return result, tree([row_sum(exact(total, BLOCK))] + [row_sum(part[rows:, :LANES]) for part in got]), low


def scatter_parts(values, axis):
    n = lax.axis_size(axis)
    if n > 4:
        return [lax.psum_scatter(values[0].astype(f32), axis, scatter_dimension=0)]
    return [values[0]] + [partner(values[k], axis, k) for k in range(1, n)]


def share_parts(value, axis):
    n = lax.axis_size(axis)
    if n > 4:
        return [lax.psum(value.astype(f32), axis)]
    return [value] + [partner(value, axis, k) for k in range(1, n)]


def added(parts):
    total = parts[0].astype(f32)
    for part in parts[1:]:
        total = total + part.astype(f32)
    return total


def sum_everywhere(value, axes):
    for axis in axes:
        k = 1
        while k < lax.axis_size(axis):
            value = value + partner(value, axis, k)
            k *= 2
    return value


def body(
    tokens,
    teacher,
    piece_starts,
    valid_rows,
    norm_gain,
    in_weight,
    conv_weight,
    conv_bias,
    xproj_weight,
    dtproj_weight,
    dt_bias,
    a_log,
    skip_weight,
    out_weight,
):
    seqs = lax.axis_size("seq")
    batches = lax.axis_size("batch")
    _, rows, width = tokens.shape
    total = rows * seqs
    taps, own = conv_weight.shape
    chans = own * batches
    depth = in_weight.shape[0]
    rank = dtproj_weight.shape[0]
    states = a_log.shape[1]
    lines = depth * seqs
    packed = 2 * LANES * own // chans
    place = lax.axis_index("seq") if seqs <= 4 else jnp.int32(0)
    me = place.astype(jnp.int32).reshape(1)
    tok = tokens.reshape(rows, width)

    flags = jnp.concatenate([piece_starts, valid_rows], axis=0).astype(bf16)
    flags = jnp.pad(flags, ((0, 14), (0, width - rows)))
    top = rows // 2 if seqs <= 4 else rows
    bottom = gather_parts(tok[top:], "seq") if top < rows else []
    everything = lax.all_gather(jnp.concatenate([tok[:top], flags], axis=0), "seq")
    split = split_columns(in_weight, norm_gain.reshape(1, depth), valid_rows, seqs, batches, own)
    split = lax.all_to_all(split, "seq", 0, 0).reshape(lines, 2 * chans + LANES)
    vectors = jnp.concatenate(
        [
            dtproj_weight.T,
            a_log,
            conv_weight.T,
            conv_bias[:, None],
            dt_bias[:, None],
            skip_weight[:, None],
        ],
        axis=1,
    )
    vectors = jnp.pad(vectors, ((0, 0), (0, LANES - vectors.shape[1])))
    columns_x = jnp.pad(xproj_weight, ((0, 0), (0, LANES - xproj_weight.shape[1])))
    local = jnp.pad(jnp.concatenate([vectors, columns_x], axis=0), ((0, lines - 2 * own), (chans, 0)))
    second = jnp.concatenate(
        [split[:, chans + LANES :]] + [out_weight[:, k : k + chans] for k in range(0, width, chans)], axis=0
    )
    blocks, places, second = gather_batch(split[:, : chans + LANES] + local, second)
    second = lax.all_gather(second, "batch")


    tile = ((total, chans), f32, "t")
    low_tile = ((total, chans), bf16, "t")
    state = ((total * states, chans), bf16, "t")
    normed, normed_t, stream, conv_pre, act, proj, w_stream, vec, xproj, gain, marks = call(
        lambda *refs: start_kernel(len(bottom), *refs),
        jnp.concatenate([me] + [p.astype(jnp.int32).reshape(1) for p in places]),
        [(everything, ("y", top))] + [(part, "f") for part in bottom] + [(block, "f") for block in blocks],
        [
            ((total, width), bf16, "t"),
            ((width, total), bf16, "c"),
            low_tile,
            tile,
            low_tile,
            ((total, LANES), bf16, "t"),
            ((width, chans), bf16, "f"),
            ((LANES, chans), f32, "f"),
            ((chans, LANES), bf16, "f"),
            ((1, width), f32, "f"),
            ((1, LANES), f32, "f"),
        ],
        [pltpu.VMEM((ROWS + 8, chans), f32), pltpu.VMEM((width, LANES), f32), pltpu.VMEM((chans, LANES), f32)],
        total,
        rows,
    )
    total_valid = (marks[:, LANES - 2 : LANES - 1] * 128.0 + marks[:, LANES - 1 :]) / depth
    starts = everything[:, top, :rows].astype(f32).reshape(total)
    running = jnp.cumsum(starts)
    lagged = jnp.concatenate([jnp.zeros((PIECE,), f32), running[: total - PIECE]])
    carry_on = jnp.where(running - lagged > 0.5, 1.0 - starts, 0.0)
    flags = jnp.max(carry_on.reshape(-1, UNROLL * BLOCK), axis=1).astype(jnp.int32)
    teacher, proj = lax.optimization_barrier((teacher, proj))
    per = rows // seqs
    teach_v = lax.all_to_all(teacher.reshape(seqs, per, width), "seq", 0, 0).astype(f32)
    proj = added(share_parts(proj, "seq"))
    me = jnp.concatenate([me, flags])
    proj = jnp.where(jnp.arange(LANES)[None, :] == CARRY, carry_on[:, None], proj)
    groups = (ROWS // BLOCK, states, BLOCK)
    g, step = call(
        piece_kernel,
        me,
        [(proj, "t"), (act, "t"), (vec, "f")],
        [state, tile],
        [
            pltpu.VMEM((states, chans), f32),
            pltpu.VMEM((ROWS, chans), f32),
            pltpu.VMEM((ROWS, chans), f32),
            pltpu.VMEM(groups, f32),
        ],
        total,
        rows,
        reverse=True,
    )
    halves = 2
    held = seqs // halves * per
    count = total // ROWS // halves
    places = seqs if seqs <= 4 else 1
    if seqs <= 4:
        messages = [((held, width), bf16, "f")] * seqs
    else:
        messages = [((seqs, held, width), bf16, "f")]
    by_time = [state, tile, tile, ((chans, total), bf16, "c")]
    weights = [((width, chans), bf16, "f"), ((chans, width), bf16, "f")]
    mine = lambda v: lax.dynamic_slice_in_dim(v, lax.axis_index("seq") * per, per, axis=1)
    if bottom:
        above = top // per
        tok_v = jnp.stack([lax.dynamic_slice_in_dim(b, jnp.maximum(place - above, 0) * per, per, axis=0) for b in bottom])
        tok_v = jnp.take(tok_v, jnp.arange(seqs) ^ place, axis=0)
        tops = lax.dynamic_slice_in_dim(everything, jnp.minimum(place, above - 1) * per, per, axis=1)
        tok_v = jnp.where(place < above, tops, tok_v).astype(f32)
    else:
        tok_v = mine(everything[:, :rows]).astype(f32)
    valid_v = mine(everything[:, top + 1, :rows].reshape(seqs, rows, 1)).astype(f32)
    enter = jnp.zeros((states, chans), f32)
    kept = []
    branches = []
    for half in range(halves):
        out = call(
            lambda *refs, half=half: ahead_kernel(half, places, per, rows, *refs),
            me,
            [(proj, "t"), (act, "t"), (normed, "t"), (g, "t"), (step, "t"), (vec, "f"), (enter, "f")]
            + ([(w_gate, "f"), (out_w, "f")] if half else [(second, "f")])
            + [(array, "o") for array in kept],
            by_time + [((states, chans), f32, "f")] + ([] if half else weights) + messages,
            [
                pltpu.VMEM((states, chans), f32),
                pltpu.VMEM((HALF, chans), f32),
                pltpu.VMEM((HALF // BLOCK, states, BLOCK), f32),
                pltpu.VMEM((2, HALF + BLOCK, BLOCK * states), bf16),
                pltpu.VMEM((BLOCK * states, chans), bf16),
                pltpu.VMEM((HALF + BLOCK, chans), f32),
                pltpu.VMEM((HALF, width), bf16),
            ],
            total,
            rows,
            first=half * count * ROWS // HALF,
            count=count * ROWS // HALF,
            size=HALF,
        )
        kept, enter = out[:4], out[4]
        if not half:
            w_gate, out_w = out[5:7]
        branches.append(out[-places:])
    hp, mixed, gate, gated_t = kept

    factor = 2.0 * (total * batches) / total_valid
    squares = jnp.zeros((1, width), f32)
    results, d_branches = [], []
    for half in range(halves):
        at = slice(half * (seqs // halves), (half + 1) * (seqs // halves))
        flat_half = lambda v: v[at].reshape(held, v.shape[2])
        result = flat_half(tok_v) + added(scatter_parts(branches[half], "seq"))
        results.append(result.astype(bf16).reshape(seqs // halves, per, width))
        misfit = result - flat_half(teach_v)
        valid_f = flat_half(valid_v)
        squares = squares + jnp.sum(valid_f * misfit * misfit, axis=0, keepdims=True)
        d_branches.append(gather_parts((factor * valid_f * misfit).astype(bf16), "seq"))
    part = LANES - CARRY
    square_sum = squares[:, :LANES]
    for k in range(LANES, width, LANES):
        square_sum = square_sum + squares[:, k : k + LANES]
    square_sum = sum(square_sum[:, k : k + part] for k in range(0, LANES, part))
    square_sum = jnp.pad(square_sum, ((0, 0), (CARRY, 0)))

    kept = []
    enter = jnp.zeros((states, chans), f32)
    skip_grad = jnp.zeros((1, chans), f32)
    for half in range(halves):
        *kept, skip_grad, enter = call(
            lambda *refs, half=half: piece_grad_kernel(half * count, places, per, rows, *refs),
            me,
            [
                (proj, "t"),
                (act, "t"),
                (mixed, "t"),
                (gate, "t"),
                (step, "t"),
                (vec, "f"),
                (out_w, "f"),
                (enter, "f"),
                (skip_grad, "f"),
            ]
            + [(part, "f") for part in d_branches[half]]
            + [(array, "o") for array in kept],
            [
                state,
                tile,
                low_tile,
                ((total, width), bf16, "t"),
                ((1, chans), f32, "f"),
                ((states, chans), f32, "f"),
            ],
            [pltpu.VMEM((states, chans), f32), pltpu.VMEM((ROWS, chans), f32), pltpu.VMEM(groups, f32)],
            total,
            rows,
            first=half * count,
            count=count,
        )
    q, d_mixed, d_gate, d_branch = kept
    output = lax.all_to_all(jnp.concatenate(results, axis=0), "seq", 0, 0).reshape(rows, width)
    d_result = lax.dynamic_slice_in_dim(d_branch, lax.axis_index("seq") * rows, rows, axis=0).astype(f32)
    early_sum = by_blocks(
        early_grad_kernel,
        batches,
        own,
        [normed_t, gated_t],
        [d_gate, d_branch],
        lines + own * width // chans,
        chans,
    )
    early = lax.psum_scatter(early_sum, "batch", scatter_dimension=0)
    pieces = exact(square_sum, BLOCK)
    d_act, d_proj, table = call(
        state_grad_kernel,
        me,
        [(proj, "t"), (act, "t"), (d_mixed, "t"), (g, "t"), (hp, "t"), (q, "t"), (step, "t"), (vec, "f"), (skip_grad, "f"), (pieces, "f")],
        [tile, ((total, LANES), bf16, "t"), ((LANES, chans), f32, "f")],
        [
            pltpu.VMEM((states, chans), f32),
            pltpu.VMEM((HALF, chans), f32),
            pltpu.VMEM((HALF // BLOCK, states, BLOCK), f32),
            pltpu.VMEM((HALF + BLOCK, BLOCK * states), bf16),
        ]
        + [pltpu.VMEM((BLOCK * states, chans), bf16)] * 2
        + [
            pltpu.VMEM((BLOCK * states, 2 * min(chans, 2 * LANES)), bf16),
            pltpu.VMEM((BLOCK * states, LANES), bf16),
        ]
        + [pltpu.VMEM((HALF + 2 * BLOCK, chans), f32)] * 2
        + [pltpu.VMEM((HALF + 2 * BLOCK, LANES), f32)],
        total,
        rows,
        size=HALF,
        reverse=True,
    )
    d_proj = share_parts(d_proj, "seq")
    slots = slots_out(seqs, rows, width)
    paired = batches <= 8
    size = lines + packed
    if paired:
        lates = [((batches // 2, size, chans), f32, "f"), ((batches // 2, size + BLOCK, chans), bf16, "f")]
    else:
        lates = [((batches, size, chans), f32, "f")]
    core = (lax.axis_index("batch") % 2).astype(jnp.int32).reshape(1)
    out = call(
        lambda *refs: end_kernel(own, rows, len(slots), paired, *refs),
        jnp.concatenate([me, core]),
        [(part, "t") for part in d_proj]
        + [
            (d_act, "t"),
            (conv_pre, "t"),
            (stream, "t"),
            (act, "t"),
            (d_gate, "t"),
            (vec, "f"),
            (xproj, "f"),
            (w_stream, "f"),
            (w_gate, "f"),
            (table, "f"),
            (normed_t, "c"),
        ],
        slots + lates + [((1, LANES), f32, "f")],
        [
            pltpu.VMEM((ROWS + 8, chans), f32),
            pltpu.VMEM((chans, LANES), f32),
            pltpu.VMEM((LANES, chans), f32),
            pltpu.VMEM((chans, LANES), f32),
            pltpu.VMEM((width, chans), f32),
        ],
        total,
        rows,
        reverse=True,
    )
    d_normed, seq_sum = out[: len(slots)], out[-1]
    if paired:
        late, square_sum, waiting = scatter_batch(out[-3], out[-2], seq_sum)
    else:
        waiting = out[-2]
        late = lax.psum_scatter(out[-2], "batch", scatter_dimension=0)
        square_sum = sum_everywhere(square_sum, ("batch", "seq"))
    loss = jnp.sum(square_sum) / (total_valid * width)[0, 0]
    in_out = jnp.concatenate([late[:lines], early[:lines]], axis=1).astype(bf16)
    if False:
        row = (waiting[0, :1] * 0).astype(bf16)
        d_normed = list(d_normed)
        d_normed[-1] = d_normed[-1] + jnp.tile(row, (1, width // chans))
    row = in_out[:1].astype(f32) * 0.0
    d_normed = added([jnp.tile(row, (1, width // (2 * chans)))] + scatter_parts(d_normed, "seq"))
    in_out = lax.all_to_all(in_out.reshape(seqs, depth, 2 * chans), "seq", 0, 0)
    in_out, gain_out, xproj_out, dt_out, alog_out, conv_out, convb_out, dtb_out, skip_out = join_columns(
        in_out, late[lines:], in_weight, norm_gain.reshape(1, depth), batches, own
    )
    out_out = early[lines:].reshape(-1, own, chans).transpose(1, 0, 2).reshape(own, width)
    tok_f = tok.astype(f32)
    mean_sq = jnp.mean(tok_f * tok_f, axis=-1, keepdims=True)
    root_inv = lax.rsqrt(mean_sq + 1e-05)
    own_unit = tok_f * root_inv
    scaled = d_normed * gain
    input_grad = d_result + root_inv * (scaled - own_unit * jnp.mean(scaled * own_unit, axis=-1, keepdims=True))
    return (
        output[None],
        loss,
        input_grad[None],
        gain_out[0],
        in_out,
        conv_out,
        convb_out[0],
        xproj_out,
        dt_out,
        dtb_out[0],
        alog_out,
        skip_out[0],
        out_out,
    )


def solution(mesh):
    return jax.shard_map(
        body,
        mesh=mesh,
        in_specs=(
            P("batch", "seq", None),
            P("batch", "seq", None),
            P("batch", "seq"),
            P("batch", "seq"),
            P(("batch", "seq")),
            P(("batch", "seq"), None),
            P(None, ("batch", "seq")),
            P(("batch", "seq")),
            P(("batch", "seq"), None),
            P(None, ("batch", "seq")),
            P(("batch", "seq")),
            P(("batch", "seq"), None),
            P(("batch", "seq")),
            P(("batch", "seq"), None),
        ),
        out_specs=(
            P("batch", "seq", None),
            P(),
            P("batch", "seq", None),
            P(("batch", "seq")),
            P(("batch", "seq"), None),
            P(None, ("batch", "seq")),
            P(("batch", "seq")),
            P(("batch", "seq"), None),
            P(None, ("batch", "seq")),
            P(("batch", "seq")),
            P(("batch", "seq"), None),
            P(("batch", "seq")),
            P(("batch", "seq"), None),
        ),
        check_vma=False,
    )
```

```python
import jax
import jax.numpy as jnp
from jax import lax
from jax.experimental import pallas as pl
from jax.experimental.pallas import tpu as pltpu
from jax.sharding import PartitionSpec as P

PIECE = 256
BLOCK = 16
UNROLL = 4
ROWS = 256
HALF = 128
LOG2E = 1.4426950408889634
LN2 = 0.6931471805599453
NEVER = 1e9
LANES = 128
f32 = jnp.float32
bf16 = jnp.bfloat16

ALOG, CONV, CONVB, DTB, SKIP = 64, 80, 84, 85, 86
INTO, OUT, CARRY = 64, 80, 96


def dot(a, b):
    return jnp.dot(a, b, preferred_element_type=f32)


def dot_t(a, b):
    return lax.dot_general(a, b, (((1,), (1,)), ((), ())), preferred_element_type=f32)


def t_dot(a, b):
    return lax.dot_general(a, b, (((0,), (0,)), ((), ())), preferred_element_type=f32)


def sigmoid(v):
    return 1.0 / (1.0 + jnp.exp(-v))


def row_of(ref, t, n):
    return jnp.broadcast_to(ref[pl.ds(t, 1), :], (n, ref.shape[1]))


def col_of(block, tt, c):
    return jnp.broadcast_to(block[:, tt : tt + 1], (block.shape[0], c))


def rates_of(vec_ref, n):
    return -jnp.exp(vec_ref[ALOG : ALOG + n, :]) * LOG2E


def dt_of(proj, vec_ref, rank):
    low = proj[:, :rank].astype(bf16)
    return low, dot(low, vec_ref[:rank, :].astype(bf16)) + vec_ref[DTB : DTB + 1, :]


def softplus(v):
    return jnp.maximum(v, 0.0) + jnp.log1p(jnp.exp(-jnp.abs(v)))


def slope_of(step):
    small = step * (1.0 - step * (0.5 - step * (1.0 / 6.0 - step * (1.0 / 24.0))))
    return jnp.where(step < 0.02, small, 1.0 - jnp.exp(-step))


def columns(proj_t, first, n, into_ref):
    for j in range(into_ref.shape[0]):
        into_ref[j] = proj_t[first : first + n, j * BLOCK : (j + 1) * BLOCK]


def block_diag(values, n):
    rows, wide = values.shape[0], BLOCK * n
    spread = (
        lax.broadcasted_iota(jnp.int32, (n, wide), 1) % n == lax.broadcasted_iota(jnp.int32, (n, wide), 0)
    ).astype(f32).astype(bf16)
    keep = lax.broadcasted_iota(jnp.int32, (rows, wide), 1) // n == lax.broadcasted_iota(
        jnp.int32, (rows, wide), 0
    ) % BLOCK
    return jnp.where(keep, dot(values, spread), 0.0).astype(bf16)


def unit_of(x):
    return x * lax.rsqrt(jnp.mean(x * x, axis=-1, keepdims=True) + 1e-05)


def start_kernel(count, me_ref, x_ref, *refs):
    bottom, parts = refs[:count], refs[count:-14]
    (
        normed_ref, turned_ref, stream_ref, pre_ref, act_ref, proj_ref, w_ref, vec_ref, xproj_ref, gain_ref, marks_ref,
        wide_ref, ext_ref, cols_ref,
    ) = refs[-14:]
    rows, chans = stream_ref.shape
    taps = CONVB - CONV

    @pl.when(pl.program_id(0) == 0)
    def _():
        wide_ref[:8, :] = jnp.zeros((8, chans), f32)
        place = 1
        for part in parts:
            count, lines, _ = part.shape
            own = chans * lines // w_ref.shape[0]
            for k in range(count):
                block = me_ref[place]
                place += 1
                at = pl.ds(pl.multiple_of(block * lines, lines), lines)
                w_ref[at, :] = part[k, :, :chans]
                ext = part[k, :, chans:].astype(f32)
                ext_ref[at, :] = ext
                at = pl.ds(pl.multiple_of(block * own, own), own)
                cols_ref[at, :] = ext[:own]
                used = lax.broadcasted_iota(jnp.int32, (own, LANES), 1) < CARRY
                xproj_ref[at, :] = jnp.where(used, ext[own : 2 * own], 0.0).astype(bf16)
        for k in range(w_ref.shape[0] // LANES):
            at = slice(k * LANES, (k + 1) * LANES)
            gain_ref[:, at] = ext_ref[at, :].T[LANES - 3 : LANES - 2]
        for k in range(chans // LANES):
            at = slice(k * LANES, (k + 1) * LANES)
            vec_ref[:, at] = cols_ref[at, :].T
        marks_ref[...] = jnp.sum(ext_ref[...], axis=0, keepdims=True)

    x = x_ref[...]
    if count:
        x = jnp.concatenate([x, read_slot(bottom, pl.program_id(0) ^ me_ref[0])], axis=0)
    normed = (unit_of(x.astype(f32)) * gain_ref[...]).astype(bf16)
    normed_ref[...] = normed
    turned_ref[...] = normed.T
    stream = dot(normed, w_ref[...]).astype(bf16)
    stream_ref[...] = stream
    wide_ref[8:, :] = stream.astype(f32)
    pre = jnp.broadcast_to(vec_ref[CONVB : CONVB + 1, :], (rows, chans))
    for tap in range(taps):
        first = 8 - taps + 1 + tap
        pre = pre + vec_ref[CONV + tap : CONV + tap + 1, :] * wide_ref[first : first + rows, :]
    wide_ref[:8, :] = wide_ref[rows:, :]
    pre_ref[...] = pre
    act = (pre * sigmoid(pre)).astype(bf16)
    act_ref[...] = act
    proj_ref[...] = dot(act, xproj_ref[...]).T[:CARRY, :].astype(bf16)


def several(block):
    def blocks(i, carry):
        for k in range(UNROLL):
            carry = block(UNROLL * i + k, carry)
        return carry

    return blocks


def piece_kernel(me_ref, proj_ref, act_ref, vec_ref, g_ref, step_ref, carry_ref, u_ref, stepm_ref, col_ref):
    rows, c = act_ref.shape
    n = carry_ref.shape[0]

    @pl.when(pl.program_id(0) == 0)
    def _():
        carry_ref[...] = jnp.zeros_like(carry_ref)

    proj = proj_ref[...].T
    _, pre = dt_of(proj, vec_ref, INTO)
    step = softplus(pre)
    step_ref[...] = step
    u_ref[...] = step * act_ref[...].astype(f32)
    stepm_ref[...] = jnp.where(proj[:, CARRY : CARRY + 1] > 0.5, step, NEVER)
    columns(proj_ref[...], INTO, n, col_ref)
    r2 = rates_of(vec_ref, n)

    def block(i, carry):
        j = rows // BLOCK - 1 - i
        into = col_ref[j]
        for tt in reversed(range(BLOCK)):
            t = j * BLOCK + tt
            g = row_of(u_ref, t, n) * col_of(into, tt, c) + carry
            g_ref[pl.ds(pl.multiple_of(t * n, n), n), :] = g.astype(bf16)
            carry = jnp.exp2(row_of(stepm_ref, t, n) * r2) * g
        return carry

    carry_ref[...] = lax.fori_loop(0, rows // BLOCK // UNROLL, several(block), carry_ref[...])


def ahead_kernel(
    first, places, per, local, me_ref, *refs,
):
    proj_ref, act_ref, normed_ref, g_ref, step_ref, vec_ref = refs[:6]
    if first:
        enter_ref, wgate_ref, outw_ref = refs[6:9]
        hp_ref, mixed_ref, gate_ref, gated_ref, leave_ref = refs[-7 - places - 5 : -7 - places]
    else:
        second_ref = refs[6]
        hp_ref, mixed_ref, gate_ref, gated_ref, leave_ref, wgate_ref, outw_ref = refs[-7 - places - 7 : -7 - places]
    branch_refs = refs[-7 - places : -7]
    carry_ref, u_ref, col_ref, diag_ref, s_ref, y_ref, out_ref = refs[-7:]
    rows, c = act_ref.shape
    n = carry_ref.shape[0]

    @pl.when(pl.program_id(0) == 0)
    def _():
        if first:
            carry_ref[...] = enter_ref[...]
            return
        carry_ref[...] = jnp.zeros_like(carry_ref)
        blocks = second_ref.shape[0]
        lines, own = wgate_ref.shape[0] // blocks, outw_ref.shape[0] // blocks
        for b in range(blocks):
            wgate_ref[b * lines : (b + 1) * lines, :] = second_ref[b, :lines, :]
            for k in range(outw_ref.shape[1] // c):
                outw_ref[b * own : (b + 1) * own, k * c : (k + 1) * c] = second_ref[
                    b, lines + k * own : lines + (k + 1) * own, :
                ]

    act = act_ref[...].astype(f32)
    u_ref[...] = step_ref[...] * act
    columns(proj_ref[...], INTO, n, col_ref)
    read = proj_ref[OUT : OUT + n, :].T
    high = read.astype(bf16)
    diag_ref[0, BLOCK:] = block_diag(high, n)
    diag_ref[1, BLOCK:] = block_diag((read - high.astype(f32)).astype(bf16), n)
    r2 = rates_of(vec_ref, n)

    def read_out(j):
        r16 = pl.ds(pl.multiple_of(j * BLOCK, BLOCK), BLOCK)
        both = dot(jnp.concatenate([diag_ref[0, r16, :], diag_ref[1, r16, :]], axis=0), s_ref[...])
        y_ref[r16, :] = both[:BLOCK] + both[BLOCK:]

    def block(j, h):
        read_out(j)
        into = col_ref[j]
        for tt in range(BLOCK):
            t = j * BLOCK + tt
            at = pl.ds(pl.multiple_of(t * n, n), n)
            hp = jnp.exp2(row_of(step_ref, t, n) * r2) * h
            h = hp + row_of(u_ref, t, n) * col_of(into, tt, c)
            hp_ref[at, :] = hp.astype(bf16)
            s_ref[tt * n : (tt + 1) * n, :] = (hp + g_ref[at, :].astype(f32)).astype(bf16)
        return h

    carry_ref[...] = lax.fori_loop(0, rows // BLOCK // UNROLL, several(block), carry_ref[...])
    read_out(rows // BLOCK)
    mixed = y_ref[BLOCK:] + vec_ref[SKIP : SKIP + 1, :] * act
    mixed_ref[...] = mixed
    gate = dot(normed_ref[...], wgate_ref[...])
    gate_ref[...] = gate
    gated = (mixed * (gate * sigmoid(gate))).astype(bf16)
    gated_ref[...] = gated.T
    out_ref[...] = dot(gated, outw_ref[...]).astype(bf16)
    write_rows(branch_refs, me_ref, places, per, local, rows, out_ref)
    leave_ref[...] = carry_ref[...]


def piece_grad_kernel(
    first, places, per, local, me_ref, *refs,
):
    proj_ref, act_ref, mixed_ref, gate_ref, step_ref, vec_ref, outw_ref = refs[:7]
    db_refs = refs[7 : 7 + places]
    if first:
        enter_ref, before_ref = refs[7 + places : 9 + places]
    q_ref, dm_ref, dg_ref, db_ref, sgrad_ref, leave_ref = refs[-9:-3]
    carry_ref, stepm_ref, col_ref = refs[-3:]
    rows, c = act_ref.shape
    n = carry_ref.shape[0]

    @pl.when(pl.program_id(0) == 0)
    def _():
        if first:
            carry_ref[...] = enter_ref[...]
            sgrad_ref[...] = before_ref[...]
        else:
            carry_ref[...] = jnp.zeros_like(carry_ref)
            sgrad_ref[...] = jnp.zeros_like(sgrad_ref)

    stepm_ref[...] = jnp.where(proj_ref[CARRY : CARRY + 8, :].T[:, :1] > 0.5, step_ref[...], NEVER)
    columns(proj_ref[...], OUT, n, col_ref)
    db = read_rows(db_refs, me_ref, places, per, local, rows)
    db_ref[...] = db
    dgated = dot_t(db, outw_ref[...])
    gate = gate_ref[...]
    s = sigmoid(gate)
    dm = dgated * (gate * s)
    dm_ref[...] = dm
    dg = (dgated * mixed_ref[...] * (s * (1.0 + gate * (1.0 - s)))).astype(bf16)
    dg_ref[...] = dg
    sgrad_ref[...] += jnp.sum(dm * act_ref[...].astype(f32), axis=0, keepdims=True)
    r2 = rates_of(vec_ref, n)

    chunk = first + pl.program_id(0)

    size = UNROLL * BLOCK

    def scan(i, w):
        for k in range(UNROLL):
            j = UNROLL * i + k
            read = col_ref[j]
            for tt in range(BLOCK):
                t = j * BLOCK + tt
                q = jnp.exp2(row_of(stepm_ref, t, n) * r2) * w
                q_ref[pl.ds(pl.multiple_of(t * n, n), n), :] = q.astype(bf16)
                w = q + row_of(dm_ref, t, n) * col_of(read, tt, c)
        return w

    def fill(i, w):
        for k in range(UNROLL):
            at = pl.ds(pl.multiple_of((UNROLL * i + k) * BLOCK * n, BLOCK * n), BLOCK * n)
            q_ref[at, :] = jnp.zeros((BLOCK * n, c), bf16)
        return row_of(dm_ref, (i + 1) * size - 1, n) * col_of(col_ref[(i + 1) * UNROLL - 1], BLOCK - 1, c)

    def group(i, w):
        return lax.cond(me_ref[1 + chunk * (rows // size) + i] > 0, scan, fill, i, w)

    carry_ref[...] = lax.fori_loop(0, rows // size, group, carry_ref[...])
    leave_ref[...] = carry_ref[...]


def state_grad_kernel(
    me_ref, proj_ref, act_ref, dm_ref, g_ref, hp_ref, q_ref, step_ref, vec_ref, sgrad_ref, pieces_ref,
    dact_ref, dproj_ref, table_ref,
    carry_ref, u_ref, col_ref, diag_ref, ig_ref, rr_ref, pair_ref, own_ref, x_ref, y_ref, dp_ref,
):
    rows, c = act_ref.shape
    n = carry_ref.shape[0]
    wide = BLOCK * n

    @pl.when(pl.program_id(0) == 0)
    def _():
        carry_ref[...] = jnp.zeros_like(carry_ref)
        table_ref[...] = jnp.zeros_like(table_ref)
        table_ref[SKIP : SKIP + 1, :] = sgrad_ref[...]

    act = act_ref[...].astype(f32)
    u_ref[...] = step_ref[...] * act
    columns(proj_ref[...], OUT, n, col_ref)
    diag_ref[:rows] = block_diag(proj_ref[INTO : INTO + n, :].T.astype(bf16), n)
    r2 = rates_of(vec_ref, n)
    iota = lambda shape, axis: lax.broadcasted_iota(jnp.int32, shape, axis)
    mask = lambda v: v.astype(f32).astype(bf16)
    by_row = mask(iota((BLOCK, wide), 1) // n == iota((BLOCK, wide), 0))
    part = min(c, 2 * LANES)
    which = mask(iota((2 * part, LANES), 0) // part == iota((2 * part, LANES), 1) // n % 2)
    own_lane = iota((wide, LANES), 1) % n == iota((wide, LANES), 0) % n

    def sums(j):
        r16 = pl.ds(pl.multiple_of(j * BLOCK, BLOCK), BLOCK)
        x_ref[r16, :] = dot(diag_ref[r16, :], ig_ref[...])
        y_ref[r16, :] = dot(by_row, rr_ref[...])
        dp_ref[pl.ds(pl.multiple_of((j + 1) * BLOCK, BLOCK), BLOCK), :] = dot(by_row, own_ref[...])
        own_ref[...] = jnp.where(own_lane, dot(pair_ref[...], which), 0.0).astype(bf16)

    def block(i, both):
        m, al = both
        j = rows // BLOCK - 1 - i
        sums(j + 1)
        read = col_ref[j]
        for tt in reversed(range(BLOCK)):
            t = j * BLOCK + tt
            at = pl.ds(pl.multiple_of(t * n, n), n)
            loc = slice(tt * n, (tt + 1) * n)
            drow = row_of(dm_ref, t, n)
            mu = m + drow * col_of(read, tt, c)
            srow = row_of(step_ref, t, n)
            m = jnp.exp2(srow * r2) * mu
            low_mu = mu.astype(bf16)
            q = q_ref[at, :]
            g = g_ref[at, :]
            hp = hp_ref[at, :]
            rg = low_mu * hp + q * g
            ig = low_mu + q
            ig_ref[loc, :] = ig
            rg = rg.astype(f32)
            al = al + rg * srow
            rr_ref[loc, :] = (rg * r2).astype(bf16)
            pb = ig * row_of(u_ref, t, n).astype(bf16)
            pc = (hp + g) * drow.astype(bf16)
            sb, sc = pb[:, :part], pc[:, :part]
            for k in range(1, c // part):
                sb = sb + pb[:, k * part : (k + 1) * part]
                sc = sc + pc[:, k * part : (k + 1) * part]
            pair_ref[loc, :part] = sb
            pair_ref[loc, part:] = sc
        return m, al

    m, al = lax.fori_loop(0, rows // BLOCK, block, (carry_ref[...], table_ref[ALOG : ALOG + n, :]))
    carry_ref[...] = m
    table_ref[ALOG : ALOG + n, :] = al
    sums(0)
    dp_ref[:BLOCK, :] = dot(by_row, own_ref[...])
    xs = x_ref[:rows]
    dact_ref[...] = step_ref[...] * xs + vec_ref[SKIP : SKIP + 1, :] * dm_ref[...]
    dpre = (y_ref[:rows] * LN2 + act * xs) * slope_of(step_ref[...])
    table_ref[DTB : DTB + 1, :] += jnp.sum(dpre, axis=0, keepdims=True)
    dpre_low = dpre.astype(bf16)
    table_ref[:INTO, :] += dot(proj_ref[:INTO, :].astype(bf16), dpre_low)
    dproj_ref[...] = dp_ref[:rows].astype(bf16)
    dproj_ref[:, :INTO] = dot_t(dpre_low, vec_ref[:INTO, :].astype(bf16)).astype(bf16)

    @pl.when(pl.program_id(0) == pl.num_programs(0) - 1)
    def _():
        dproj_ref[:BLOCK, CARRY:] = pieces_ref[:, CARRY:]
        table_ref[ALOG : ALOG + n, :] *= -jnp.exp(vec_ref[ALOG : ALOG + n, :])


def end_kernel(own, local, count, paired, me_ref, *refs):
    sent = 2 if paired else 1
    dn_refs, refs = refs[-count - sent - 6 : -sent - 6], refs[: -count - sent - 6] + refs[-sent - 6 :]
    late_refs, refs = refs[-sent - 6 : -6], refs[: -sent - 6] + refs[-6:]
    parts = refs[:-17]
    (
        dact_ref, pre_ref, stream_ref, act_ref, dg_ref, vec_ref, xproj_ref, ws_ref, wg_ref, table_ref, normed_ref,
        sum_ref,
        wide_ref, xgrad_ref, cgrad_ref, turned_ref, grad_ref,
    ) = refs[-17:]
    rows, c = act_ref.shape
    taps = CONVB - CONV

    @pl.when(pl.program_id(0) == 0)
    def _():
        wide_ref[rows:, :] = jnp.zeros((8, c), f32)
        xgrad_ref[...] = jnp.zeros_like(xgrad_ref)
        cgrad_ref[...] = table_ref[...]
        grad_ref[...] = jnp.zeros_like(grad_ref)

    dproj = parts[0][...].astype(f32)
    for part in parts[1:]:
        dproj = dproj + part[...].astype(f32)
    used = lax.broadcasted_iota(jnp.int32, dproj.shape, 1) < CARRY
    dproj = jnp.where(used, dproj, 0.0).astype(bf16)
    pre = pre_ref[...]
    s = sigmoid(pre)
    dconv = (dact_ref[...] + dot_t(dproj, xproj_ref[...])) * (s * (1.0 + pre * (1.0 - s)))
    wide_ref[:rows, :] = dconv
    xgrad_ref[...] += t_dot(act_ref[...], dproj)
    cgrad_ref[CONVB : CONVB + 1, :] += jnp.sum(dconv, axis=0, keepdims=True)
    stream = stream_ref[...].astype(f32)
    dstream = jnp.zeros((rows, c), f32)
    for tap in range(taps):
        back = taps - 1 - tap
        moved = wide_ref[back : back + rows, :]
        cgrad_ref[CONV + tap : CONV + tap + 1, :] += jnp.sum(stream * moved, axis=0, keepdims=True)
        dstream = dstream + vec_ref[CONV + tap : CONV + tap + 1, :] * moved
    wide_ref[rows:, :] = dconv[:8, :]
    dstream_low = dstream.astype(bf16)
    dn = (dot_t(dstream_low, ws_ref[...]) + dot_t(dg_ref[...], wg_ref[...])).astype(bf16)
    write_slot(dn_refs, slot_of(me_ref, local, True), dn)
    grad_ref[...] += dot(normed_ref[...], dstream_low)

    @pl.when(pl.program_id(0) == pl.num_programs(0) - 1)
    def _():
        for k in range(c // LANES):
            at = slice(k * LANES, (k + 1) * LANES)
            turned_ref[at, :] = cgrad_ref[:, at].T
        sums = tree([row_sum(part[:BLOCK, :]) for part in parts])
        sums = jnp.where(lax.broadcasted_iota(jnp.int32, sums.shape, 1) < CARRY, 0.0, sums)
        sum_ref[...] = sums
        pieces = [jnp.zeros((BLOCK, LANES), f32)]
        row = lax.broadcasted_iota(jnp.int32, (BLOCK, LANES), 0)
        for k in range(3):
            term = sums.astype(bf16).astype(f32)
            pieces = [jnp.where(row == k, term, pieces[0])]
            sums = sums - term
        pieces = jnp.concatenate([pieces[0].astype(bf16)] * (c // LANES), axis=1)
        packed, lines = 2 * own * LANES // c, grad_ref.shape[0] * own // c

        def block(b):
            at = slice(b * own, (b + 1) * own)
            both = jnp.concatenate([xgrad_ref[at, :], turned_ref[at, :]], axis=0)
            small = [both[k * packed : (k + 1) * packed] for k in range(c // LANES)]
            return grad_ref[b * lines : (b + 1) * lines, :], jnp.concatenate(small, axis=1)

        if not paired:
            for b in range(c // own):
                late_refs[0][b, :lines, :], late_refs[0][b, lines:, :] = block(b)
            return
        mine_ref, theirs_ref = late_refs
        first = me_ref[me_ref.shape[0] - 1] == 0
        for z in range(c // own // 2):
            for part, at, end in zip(zip(block(2 * z), block(2 * z + 1)), (0, lines), (lines, lines + packed)):
                mine_ref[z, at:end, :] = jnp.where(first, part[0], part[1])
                theirs_ref[z, at:end, :] = jnp.where(first, part[1], part[0]).astype(bf16)
            theirs_ref[z, lines + packed :, :] = pieces


def slot_of(me_ref, local, reverse=False):
    step = pl.program_id(0)
    if reverse:
        step = pl.num_programs(0) - 1 - step
    return (step // (local // ROWS)) ^ me_ref[0]


def read_rows(refs, me_ref, places, per, local, size):
    step = pl.program_id(0)
    each = size // per
    at = pl.ds(pl.multiple_of(step // (local // size) * per, per), per)
    pieces = []
    for p in range(each):
        j = step % (local // size) * each + p
        if len(refs) == 1:
            pieces.append(refs[0][j, at, :])
            continue
        value = refs[0][at, :]
        for k in range(1, places):
            value = jnp.where(j ^ me_ref[0] == k, refs[k][at, :], value)
        pieces.append(value)
    return jnp.concatenate(pieces, axis=0)


def read_slot(refs, slot):
    value = refs[0][...]
    for k in range(1, len(refs)):
        value = jnp.where(slot == k, refs[k][...], value)
    return value


def write_rows(refs, me_ref, places, per, local, size, from_ref):
    step = pl.program_id(0)
    each = size // per
    at = pl.ds(pl.multiple_of(step // (local // size) * per, per), per)
    sub = step % (local // size)
    if len(refs) == 1:
        for p in range(each):
            refs[0][sub * each + p, at, :] = from_ref[p * per : (p + 1) * per, :]
        return
    for k, ref in enumerate(refs):
        j = k ^ me_ref[0]

        @pl.when(j // each == sub)
        def _(ref=ref, j=j):
            ref[at, :] = from_ref[pl.ds(pl.multiple_of(j % each * per, per), per), :]


def write_slot(refs, slot, value):
    if len(refs) == 1:
        refs[0][...] = value
        return
    for k, ref in enumerate(refs):

        @pl.when(slot == k)
        def _(ref=ref):
            ref[...] = value


def call(kernel, me, ins, outs, scratch, total, local, reverse=False, first=0, count=None, size=ROWS):
    steps = total // size
    per = local // size
    turn = (lambda i: steps - 1 - i) if reverse else (lambda i: i + first)
    aliases = {}
    for index, (_, kind) in enumerate(ins):
        if kind == "o":
            aliases[index + 1] = len(aliases)

    def slot_map(k):
        def index(i, me_ref):
            group = k ^ me_ref[0]
            if reverse:
                group = steps // per - 1 - group
            first, last = (per - 1, 0) if reverse else (0, per - 1)
            now = i // per
            return (jnp.where(now < group, first, jnp.where(now > group, last, turn(i) % per)), 0)

        return index

    def spec(shape, kind):
        if isinstance(kind, int):
            return pl.BlockSpec((size, shape[1]), slot_map(kind))
        if kind == "f":
            return pl.BlockSpec(shape, lambda i, me_ref: (0,) * len(shape))
        if kind == "o":
            return pl.BlockSpec(memory_space=pl.ANY)
        if kind == "c":
            return pl.BlockSpec(
                (shape[0], size), lambda i, me_ref: (0, turn(i))
            )
        if isinstance(kind, tuple):
            return pl.BlockSpec(
                (None, min(size, kind[1]), shape[2]), lambda i, me_ref: (turn(i) // per, turn(i) % per, 0)
            )
        if kind == "x":
            return pl.BlockSpec(
                (None, size, shape[2]), lambda i, me_ref: ((turn(i) // per) ^ me_ref[0], turn(i) % per, 0)
            )
        return pl.BlockSpec((shape[0] // steps, shape[1]), lambda i, me_ref: (turn(i), 0))

    return pl.pallas_call(
        kernel,
        out_shape=[jax.ShapeDtypeStruct(s, d) for s, d, _ in outs],
        grid_spec=pltpu.PrefetchScalarGridSpec(
            num_scalar_prefetch=1,
            grid=(count or steps,),
            in_specs=[spec(a.shape, k) for a, k in ins],
            out_specs=[spec(s, k) for s, _, k in outs],
            scratch_shapes=scratch,
        ),
        input_output_aliases=aliases,
        compiler_params=pltpu.CompilerParams(dimension_semantics=("arbitrary",), vmem_limit_bytes=60 << 20),
    )(me, *[a for a, _ in ins])


def slots_in(parts):
    if len(parts) == 1:
        return [(parts[0], "x")]
    return [(part, k) for k, part in enumerate(parts)]


def slots_out(seqs, rows, width):
    if seqs > 4:
        return [((seqs, rows, width), bf16, "x")]
    return [((rows, width), bf16, k) for k in range(seqs)]


def early_grad_kernel(normed_ref, gated_ref, dg_ref, *refs):
    parts, out_ref = refs[:-1], refs[-1]
    group, _, c = out_ref.shape
    lines, own = normed_ref.shape[0] // group, gated_ref.shape[0] // group
    gate = dot(normed_ref[...], dg_ref[...])
    out, first = 0.0, 0
    for part in parts:
        last = first + part.shape[0]
        out = out + dot(gated_ref[:, first:last], part[...])
        first = last
    for b in range(group):
        out_ref[b, :lines, :] = gate[b * lines : (b + 1) * lines]
        for k in range(out.shape[1] // c):
            out_ref[b, lines + k * own : lines + (k + 1) * own, :] = out[
                b * own : (b + 1) * own, k * c : (k + 1) * c
            ]


def by_blocks(kernel, batches, own, columns, whole, rows, chans):
    group = min(2 * LANES // own, batches)
    steps = batches // group

    def spec(array, cut):
        if cut:
            return pl.BlockSpec((array.shape[0] // steps, array.shape[1]), lambda i: (i, 0))
        return pl.BlockSpec(array.shape, lambda i: (0,) * array.ndim)

    return pl.pallas_call(
        kernel,
        out_shape=jax.ShapeDtypeStruct((batches, rows, chans), f32),
        grid=(steps,),
        in_specs=[spec(a, True) for a in columns] + [spec(a, False) for a in whole],
        out_specs=pl.BlockSpec((group, rows, chans), lambda i: (i, 0, 0)),
        compiler_params=pltpu.CompilerParams(dimension_semantics=("arbitrary",), vmem_limit_bytes=60 << 20),
    )(*columns, *whole)


def split_kernel(seqs, batches, own, w_ref, gain_ref, valid_ref, out_ref):
    depth, half, chans = w_ref.shape[0], w_ref.shape[1] // 2, batches * own
    count = jnp.sum(valid_ref[...].astype(f32), keepdims=True)
    high = jnp.floor(count * (1.0 / 128.0))
    iota = lambda shape, axis: lax.broadcasted_iota(jnp.int32, shape, axis)
    gain = jnp.broadcast_to(gain_ref[...].astype(f32), (depth, depth))
    gain = jnp.where(iota((depth, depth), 0) == iota((depth, depth), 1), gain, 0.0)
    gain = jnp.sum(gain, axis=1, keepdims=True)
    lane = iota((depth, LANES), 1)
    extra = jnp.where(lane == LANES - 3, gain, 0.0)
    extra = jnp.where(lane == LANES - 2, high, extra)
    extra = jnp.where(lane == LANES - 1, count - high * 128.0, extra).astype(bf16)
    for s in range(seqs):
        for k in range(2):
            pieces = [
                w_ref[:, k * half + (b * seqs + s) * own : k * half + (b * seqs + s + 1) * own].astype(f32)
                for b in range(batches)
            ]
            first = k * (chans + LANES)
            out_ref[s, :, first : first + chans] = jnp.concatenate(pieces, axis=1).astype(bf16)
        out_ref[s, :, chans : chans + LANES] = extra


def split_columns(weight, gain, valid, seqs, batches, own):
    shape = jax.ShapeDtypeStruct((seqs, weight.shape[0], 2 * batches * own + LANES), bf16)
    return pl.pallas_call(lambda *refs: split_kernel(seqs, batches, own, *refs), out_shape=shape)(weight, gain, valid)


def join_kernel(
    batches, both_ref, small_ref, w_ref, gain_ref,
    out_ref, gain_out_ref, xproj_ref, dt_ref, alog_ref, conv_ref, convb_ref, dtb_ref, skip_ref,
):
    seqs, half = both_ref.shape[0], w_ref.shape[1] // 2
    chans = half // seqs
    own = chans // batches
    for k in range(2):
        whole = [both_ref[s, :, k * chans : (k + 1) * chans].astype(f32) for s in range(seqs)]
        pieces = [whole[s][:, b * own : (b + 1) * own] for b in range(batches) for s in range(seqs)]
        out_ref[:, k * half : (k + 1) * half] = jnp.concatenate(pieces, axis=1)
    products = out_ref[...] * w_ref[...].astype(f32)
    depth = products.shape[0]
    sums = jnp.broadcast_to(jnp.sum(products, axis=1, keepdims=True), (depth, depth))
    eye = lax.broadcasted_iota(jnp.int32, (depth, depth), 0) == lax.broadcasted_iota(jnp.int32, (depth, depth), 1)
    gain_out_ref[...] = jnp.sum(jnp.where(eye, sums, 0.0), axis=0, keepdims=True) / gain_ref[...].astype(f32)
    small = small_ref[...]
    both = jnp.concatenate([small[:, k : k + LANES] for k in range(0, chans, LANES)], axis=0)
    xproj_ref[...] = both[:own, :CARRY]
    table = both[own:]
    alog_ref[...] = table[:, ALOG:CONV]
    table = jnp.concatenate([table, jnp.zeros((LANES - own, LANES), f32)], axis=0).T[:, :own]
    dt_ref[...] = table[:INTO]
    conv_ref[...] = table[CONV:CONVB]
    convb_ref[...] = table[CONVB : CONVB + 1]
    dtb_ref[...] = table[DTB : DTB + 1]
    skip_ref[...] = table[SKIP : SKIP + 1]


def join_columns(both, small, weight, gain, batches, own):
    depth = weight.shape[0]
    shapes = [weight.shape, (1, depth), (own, CARRY), (INTO, own), (own, CONV - ALOG), (CONVB - CONV, own)]
    shapes += [(1, own)] * 3
    return pl.pallas_call(
        lambda *refs: join_kernel(batches, *refs), out_shape=[jax.ShapeDtypeStruct(s, f32) for s in shapes]
    )(both, small, weight, gain)


def partner(value, axis, k):
    return lax.ppermute(value, axis, [(i, i ^ k) for i in range(lax.axis_size(axis))])


def gather_parts(value, axis):
    n = lax.axis_size(axis)
    if n > 4:
        return [lax.all_gather(value, axis)]
    return [value] + [partner(value, axis, k) for k in range(1, n)]


def gather_batch(value, after):
    n = lax.axis_size("batch")
    if n > 8:
        return [lax.all_gather(value, "batch")], [jnp.int32(k) for k in range(n)], after
    me = lax.axis_index("batch")
    chips = jnp.stack([value] + [partner(value, "batch", 2 * k) for k in range(1, n // 2)])
    other = partner(chips, "batch", 1)
    places = [me ^ (2 * k) for k in range(n // 2)] + [me ^ (2 * k + 1) for k in range(n // 2)]
    return [chips, other], places, after


def exact(total, rows):
    terms = []
    for _ in range(3):
        term = lax.reduce_precision(total, 8, 7)
        terms.append(term)
        total = total - term
    return jnp.concatenate(terms + [jnp.zeros((rows - 3, total.shape[1]), f32)], axis=0).astype(bf16)


def row_sum(rows):
    a = rows[:3].astype(f32)
    return (a[:1] + a[1:2]) + a[2:]


def tree(values):
    while len(values) > 1:
        values = [a + b for a, b in zip(values[::2], values[1::2])]
    return values[0]


def scatter_batch(mine, theirs, total):
    n = lax.axis_size("batch")
    me = lax.axis_index("batch")
    rows, c = mine.shape[1:]
    got = partner(theirs, "batch", 1)
    mine = mine + got[:, :rows].astype(f32)
    total = row_sum(exact(total, BLOCK)) + row_sum(got[0, rows:, :LANES])
    pieces = exact(jnp.tile(total, (1, c // LANES)), BLOCK)
    low = jnp.concatenate([mine.astype(bf16), jnp.broadcast_to(pieces[None], (n // 2, BLOCK, c))], axis=1)
    got = [
        partner(lax.dynamic_index_in_dim(low, (me // 2) ^ k, 0, False), "batch", 2 * k) for k in range(1, n // 2)
    ]
    result = lax.dynamic_index_in_dim(mine, me // 2, 0, False)
    for part in got:
        result = result + part[:rows].astype(f32)
    return result, tree([row_sum(exact(total, BLOCK))] + [row_sum(part[rows:, :LANES]) for part in got]), low


def scatter_parts(values, axis):
    n = lax.axis_size(axis)
    if n > 4:
        return [lax.psum_scatter(values[0].astype(f32), axis, scatter_dimension=0)]
    return [values[0]] + [partner(values[k], axis, k) for k in range(1, n)]


def share_parts(value, axis):
    n = lax.axis_size(axis)
    if n > 4:
        return [lax.psum(value.astype(f32), axis)]
    return [value] + [partner(value, axis, k) for k in range(1, n)]


def added(parts):
    total = parts[0].astype(f32)
    for part in parts[1:]:
        total = total + part.astype(f32)
    return total


def sum_everywhere(value, axes):
    for axis in axes:
        k = 1
        while k < lax.axis_size(axis):
            value = value + partner(value, axis, k)
            k *= 2
    return value


def body(
    tokens,
    teacher,
    piece_starts,
    valid_rows,
    norm_gain,
    in_weight,
    conv_weight,
    conv_bias,
    xproj_weight,
    dtproj_weight,
    dt_bias,
    a_log,
    skip_weight,
    out_weight,
):
    seqs = lax.axis_size("seq")
    batches = lax.axis_size("batch")
    _, rows, width = tokens.shape
    total = rows * seqs
    taps, own = conv_weight.shape
    chans = own * batches
    depth = in_weight.shape[0]
    rank = dtproj_weight.shape[0]
    states = a_log.shape[1]
    lines = depth * seqs
    packed = 2 * LANES * own // chans
    place = lax.axis_index("seq") if seqs <= 4 else jnp.int32(0)
    me = place.astype(jnp.int32).reshape(1)
    tok = tokens.reshape(rows, width)

    flags = jnp.concatenate([piece_starts, valid_rows], axis=0).astype(bf16)
    flags = jnp.pad(flags, ((0, 14), (0, width - rows)))
    top = rows // 2 if seqs <= 4 else rows
    bottom = gather_parts(tok[top:], "seq") if top < rows else []
    everything = lax.all_gather(jnp.concatenate([tok[:top], flags], axis=0), "seq")
    split = split_columns(in_weight, norm_gain.reshape(1, depth), valid_rows, seqs, batches, own)
    split = lax.all_to_all(split, "seq", 0, 0).reshape(lines, 2 * chans + LANES)
    vectors = jnp.concatenate(
        [
            dtproj_weight.T,
            a_log,
            conv_weight.T,
            conv_bias[:, None],
            dt_bias[:, None],
            skip_weight[:, None],
        ],
        axis=1,
    )
    vectors = jnp.pad(vectors, ((0, 0), (0, LANES - vectors.shape[1])))
    columns_x = jnp.pad(xproj_weight, ((0, 0), (0, LANES - xproj_weight.shape[1])))
    local = jnp.pad(jnp.concatenate([vectors, columns_x], axis=0), ((0, lines - 2 * own), (chans, 0)))
    second = jnp.concatenate(
        [split[:, chans + LANES :]] + [out_weight[:, k : k + chans] for k in range(0, width, chans)], axis=0
    )
    blocks, places, second = gather_batch(split[:, : chans + LANES] + local, second)
    second = lax.all_gather(second, "batch")


    tile = ((total, chans), f32, "t")
    low_tile = ((total, chans), bf16, "t")
    state = ((total * states, chans), bf16, "t")
    normed, normed_t, stream, conv_pre, act, proj, w_stream, vec, xproj, gain, marks = call(
        lambda *refs: start_kernel(len(bottom), *refs),
        jnp.concatenate([me] + [p.astype(jnp.int32).reshape(1) for p in places]),
        [(everything, ("y", top))] + [(part, "f") for part in bottom] + [(block, "f") for block in blocks],
        [
            ((total, width), bf16, "t"),
            ((width, total), bf16, "c"),
            low_tile,
            tile,
            low_tile,
            ((CARRY, total), bf16, "c"),
            ((width, chans), bf16, "f"),
            ((LANES, chans), f32, "f"),
            ((chans, LANES), bf16, "f"),
            ((1, width), f32, "f"),
            ((1, LANES), f32, "f"),
        ],
        [pltpu.VMEM((ROWS + 8, chans), f32), pltpu.VMEM((width, LANES), f32), pltpu.VMEM((chans, LANES), f32)],
        total,
        rows,
    )
    starts = everything[:, top, :rows].astype(f32).reshape(total)
    running = jnp.cumsum(starts)
    lagged = jnp.concatenate([jnp.zeros((PIECE,), f32), running[: total - PIECE]])
    carry_on = jnp.where(running - lagged > 0.5, 1.0 - starts, 0.0)
    flags = jnp.max(carry_on.reshape(-1, UNROLL * BLOCK), axis=1).astype(jnp.int32)
    teacher, proj = lax.optimization_barrier((teacher, proj))
    per = rows // seqs
    teach_v = lax.all_to_all(teacher.reshape(seqs, per, width), "seq", 0, 0).astype(f32)
    proj = added(share_parts(proj, "seq"))
    me = jnp.concatenate([me, flags])
    proj = jnp.concatenate([proj, jnp.broadcast_to(carry_on[None], (8, total))], axis=0)
    groups = (ROWS // BLOCK, states, BLOCK)
    g, step = call(
        piece_kernel,
        me,
        [(proj, "c"), (act, "t"), (vec, "f")],
        [state, tile],
        [
            pltpu.VMEM((states, chans), f32),
            pltpu.VMEM((ROWS, chans), f32),
            pltpu.VMEM((ROWS, chans), f32),
            pltpu.VMEM(groups, f32),
        ],
        total,
        rows,
        reverse=True,
    )
    halves = 2
    held = seqs // halves * per
    count = total // ROWS // halves
    places = seqs if seqs <= 4 else 1
    if seqs <= 4:
        messages = [((held, width), bf16, "f")] * seqs
    else:
        messages = [((seqs, held, width), bf16, "f")]
    by_time = [state, tile, tile, ((chans, total), bf16, "c")]
    weights = [((width, chans), bf16, "f"), ((chans, width), bf16, "f")]
    mine = lambda v: lax.dynamic_slice_in_dim(v, lax.axis_index("seq") * per, per, axis=1)
    if bottom:
        above = top // per
        tok_v = jnp.stack([lax.dynamic_slice_in_dim(b, jnp.maximum(place - above, 0) * per, per, axis=0) for b in bottom])
        tok_v = jnp.take(tok_v, jnp.arange(seqs) ^ place, axis=0)
        tops = lax.dynamic_slice_in_dim(everything, jnp.minimum(place, above - 1) * per, per, axis=1)
        tok_v = jnp.where(place < above, tops, tok_v).astype(f32)
    else:
        tok_v = mine(everything[:, :rows]).astype(f32)
    valid_v = mine(everything[:, top + 1, :rows].reshape(seqs, rows, 1)).astype(f32)
    marks, step = lax.optimization_barrier((marks, step))
    total_valid = (marks[:, LANES - 2 : LANES - 1] * 128.0 + marks[:, LANES - 1 :]) / depth
    kept = []
    branches = []
    for half in range(halves):
        out = call(
            lambda *refs, half=half: ahead_kernel(half, places, per, rows, *refs),
            me,
            [(proj, "c"), (act, "t"), (normed, "t"), (g, "t"), (step, "t"), (vec, "f")]
            + ([(enter, "f"), (w_gate, "f"), (out_w, "f")] if half else [(second, "f")])
            + [(array, "o") for array in kept],
            by_time + [((states, chans), f32, "f")] + ([] if half else weights) + messages,
            [
                pltpu.VMEM((states, chans), f32),
                pltpu.VMEM((HALF, chans), f32),
                pltpu.VMEM((HALF // BLOCK, states, BLOCK), f32),
                pltpu.VMEM((2, HALF + BLOCK, BLOCK * states), bf16),
                pltpu.VMEM((BLOCK * states, chans), bf16),
                pltpu.VMEM((HALF + BLOCK, chans), f32),
                pltpu.VMEM((HALF, width), bf16),
            ],
            total,
            rows,
            first=half * count * ROWS // HALF,
            count=count * ROWS // HALF,
            size=HALF,
        )
        kept, enter = out[:4], out[4]
        if not half:
            w_gate, out_w = out[5:7]
        branches.append(out[-places:])
    hp, mixed, gate, gated_t = kept

    factor = 2.0 * (total * batches) / total_valid
    squares = jnp.zeros((1, width), f32)
    results, d_branches = [], []
    for half in range(halves):
        at = slice(half * (seqs // halves), (half + 1) * (seqs // halves))
        flat_half = lambda v: v[at].reshape(held, v.shape[2])
        result = flat_half(tok_v) + added(scatter_parts(branches[half], "seq"))
        results.append(result.astype(bf16).reshape(seqs // halves, per, width))
        misfit = result - flat_half(teach_v)
        valid_f = flat_half(valid_v)
        squares = squares + jnp.sum(valid_f * misfit * misfit, axis=0, keepdims=True)
        d_branches.append(gather_parts((factor * valid_f * misfit).astype(bf16), "seq"))
    part = LANES - CARRY
    square_sum = squares[:, :LANES]
    for k in range(LANES, width, LANES):
        square_sum = square_sum + squares[:, k : k + LANES]
    square_sum = sum(square_sum[:, k : k + part] for k in range(0, LANES, part))
    square_sum = jnp.pad(square_sum, ((0, 0), (CARRY, 0)))

    kept = []
    for half in range(halves):
        *kept, skip_grad, enter = call(
            lambda *refs, half=half: piece_grad_kernel(half * count, places, per, rows, *refs),
            me,
            [
                (proj, "c"),
                (act, "t"),
                (mixed, "t"),
                (gate, "t"),
                (step, "t"),
                (vec, "f"),
                (out_w, "f"),
            ]
            + [(part, "f") for part in d_branches[half]]
            + ([(enter, "f"), (skip_grad, "f")] if half else [])
            + [(array, "o") for array in kept],
            [
                state,
                tile,
                low_tile,
                ((total, width), bf16, "t"),
                ((1, chans), f32, "f"),
                ((states, chans), f32, "f"),
            ],
            [pltpu.VMEM((states, chans), f32), pltpu.VMEM((ROWS, chans), f32), pltpu.VMEM(groups, f32)],
            total,
            rows,
            first=half * count,
            count=count,
        )
    q, d_mixed, d_gate, d_branch = kept
    output = lax.all_to_all(jnp.concatenate(results, axis=0), "seq", 0, 0).reshape(rows, width)
    d_result = lax.dynamic_slice_in_dim(d_branch, lax.axis_index("seq") * rows, rows, axis=0).astype(f32)
    early_sum = by_blocks(
        early_grad_kernel,
        batches,
        own,
        [normed_t, gated_t],
        [d_gate, d_branch],
        lines + own * width // chans,
        chans,
    )
    early = lax.psum_scatter(early_sum, "batch", scatter_dimension=0)
    pieces = exact(square_sum, BLOCK)
    d_act, d_proj, table = call(
        state_grad_kernel,
        me,
        [(proj, "c"), (act, "t"), (d_mixed, "t"), (g, "t"), (hp, "t"), (q, "t"), (step, "t"), (vec, "f"), (skip_grad, "f"), (pieces, "f")],
        [tile, ((total, LANES), bf16, "t"), ((LANES, chans), f32, "f")],
        [
            pltpu.VMEM((states, chans), f32),
            pltpu.VMEM((HALF, chans), f32),
            pltpu.VMEM((HALF // BLOCK, states, BLOCK), f32),
            pltpu.VMEM((HALF + BLOCK, BLOCK * states), bf16),
        ]
        + [pltpu.VMEM((BLOCK * states, chans), bf16)] * 2
        + [
            pltpu.VMEM((BLOCK * states, 2 * min(chans, 2 * LANES)), bf16),
            pltpu.VMEM((BLOCK * states, LANES), bf16),
        ]
        + [pltpu.VMEM((HALF + 2 * BLOCK, chans), f32)] * 2
        + [pltpu.VMEM((HALF + 2 * BLOCK, LANES), f32)],
        total,
        rows,
        size=HALF,
        reverse=True,
    )
    d_proj = share_parts(d_proj, "seq")
    slots = slots_out(seqs, rows, width)
    paired = batches <= 8
    size = lines + packed
    if paired:
        lates = [((batches // 2, size, chans), f32, "f"), ((batches // 2, size + BLOCK, chans), bf16, "f")]
    else:
        lates = [((batches, size, chans), f32, "f")]
    core = (lax.axis_index("batch") % 2).astype(jnp.int32).reshape(1)
    out = call(
        lambda *refs: end_kernel(own, rows, len(slots), paired, *refs),
        jnp.concatenate([me, core]),
        [(part, "t") for part in d_proj]
        + [
            (d_act, "t"),
            (conv_pre, "t"),
            (stream, "t"),
            (act, "t"),
            (d_gate, "t"),
            (vec, "f"),
            (xproj, "f"),
            (w_stream, "f"),
            (w_gate, "f"),
            (table, "f"),
            (normed_t, "c"),
        ],
        slots + lates + [((1, LANES), f32, "f")],
        [
            pltpu.VMEM((ROWS + 8, chans), f32),
            pltpu.VMEM((chans, LANES), f32),
            pltpu.VMEM((LANES, chans), f32),
            pltpu.VMEM((chans, LANES), f32),
            pltpu.VMEM((width, chans), f32),
        ],
        total,
        rows,
        reverse=True,
    )
    d_normed, seq_sum = out[: len(slots)], out[-1]
    if paired:
        late, square_sum, waiting = scatter_batch(out[-3], out[-2], seq_sum)
    else:
        waiting = out[-2]
        late = lax.psum_scatter(out[-2], "batch", scatter_dimension=0)
        square_sum = sum_everywhere(square_sum, ("batch", "seq"))
    loss = jnp.sum(square_sum) / (total_valid * width)[0, 0]
    in_out = jnp.concatenate([late[:lines], early[:lines]], axis=1).astype(bf16)
    if False:
        row = (waiting[0, :1] * 0).astype(bf16)
        d_normed = list(d_normed)
        d_normed[-1] = d_normed[-1] + jnp.tile(row, (1, width // chans))
    row = in_out[:1].astype(f32) * 0.0
    d_normed = added([jnp.tile(row, (1, width // (2 * chans)))] + scatter_parts(d_normed, "seq"))
    in_out = lax.all_to_all(in_out.reshape(seqs, depth, 2 * chans), "seq", 0, 0)
    in_out, gain_out, xproj_out, dt_out, alog_out, conv_out, convb_out, dtb_out, skip_out = join_columns(
        in_out, late[lines:], in_weight, norm_gain.reshape(1, depth), batches, own
    )
    out_out = early[lines:].reshape(-1, own, chans).transpose(1, 0, 2).reshape(own, width)
    tok_f = tok.astype(f32)
    mean_sq = jnp.mean(tok_f * tok_f, axis=-1, keepdims=True)
    root_inv = lax.rsqrt(mean_sq + 1e-05)
    own_unit = tok_f * root_inv
    scaled = d_normed * gain
    input_grad = d_result + root_inv * (scaled - own_unit * jnp.mean(scaled * own_unit, axis=-1, keepdims=True))
    return (
        output[None],
        loss,
        input_grad[None],
        gain_out[0],
        in_out,
        conv_out,
        convb_out[0],
        xproj_out,
        dt_out,
        dtb_out[0],
        alog_out,
        skip_out[0],
        out_out,
    )


def solution(mesh):
    return jax.shard_map(
        body,
        mesh=mesh,
        in_specs=(
            P("batch", "seq", None),
            P("batch", "seq", None),
            P("batch", "seq"),
            P("batch", "seq"),
            P(("batch", "seq")),
            P(("batch", "seq"), None),
            P(None, ("batch", "seq")),
            P(("batch", "seq")),
            P(("batch", "seq"), None),
            P(None, ("batch", "seq")),
            P(("batch", "seq")),
            P(("batch", "seq"), None),
            P(("batch", "seq")),
            P(("batch", "seq"), None),
        ),
        out_specs=(
            P("batch", "seq", None),
            P(),
            P("batch", "seq", None),
            P(("batch", "seq")),
            P(("batch", "seq"), None),
            P(None, ("batch", "seq")),
            P(("batch", "seq")),
            P(("batch", "seq"), None),
            P(None, ("batch", "seq")),
            P(("batch", "seq")),
            P(("batch", "seq"), None),
            P(("batch", "seq")),
            P(("batch", "seq"), None),
        ),
        check_vma=False,
    )
```

```python
import jax
import jax.numpy as jnp
from jax import lax
from jax.experimental import pallas as pl
from jax.experimental.pallas import tpu as pltpu
from jax.sharding import PartitionSpec as P

PIECE = 256
BLOCK = 16
UNROLL = 4
STEPS = 8
ROWS = 256
HALF = 128
LOG2E = 1.4426950408889634
LN2 = 0.6931471805599453
NEVER = 1e9
LANES = 128
f32 = jnp.float32
bf16 = jnp.bfloat16

ALOG, CONV, CONVB, DTB, SKIP = 64, 80, 84, 85, 86
INTO, OUT, CARRY = 64, 80, 96


def dot(a, b):
    return jnp.dot(a, b, preferred_element_type=f32)


def dot_t(a, b):
    return lax.dot_general(a, b, (((1,), (1,)), ((), ())), preferred_element_type=f32)


def t_dot(a, b):
    return lax.dot_general(a, b, (((0,), (0,)), ((), ())), preferred_element_type=f32)


def sigmoid(v):
    return 1.0 / (1.0 + jnp.exp(-v))


def row_of(ref, t, n):
    return jnp.broadcast_to(ref[pl.ds(t, 1), :], (n, ref.shape[1]))


def col_of(block, tt, c):
    return jnp.broadcast_to(block[:, tt : tt + 1], (block.shape[0], c))


def rates_of(vec_ref, n):
    return -jnp.exp(vec_ref[ALOG : ALOG + n, :]) * LOG2E


def dt_of(proj, vec_ref, rank):
    low = proj[:, :rank].astype(bf16)
    return low, dot(low, vec_ref[:rank, :].astype(bf16)) + vec_ref[DTB : DTB + 1, :]


def softplus(v):
    return jnp.maximum(v, 0.0) + jnp.log1p(jnp.exp(-jnp.abs(v)))


def slope_of(step):
    small = step * (1.0 - step * (0.5 - step * (1.0 / 6.0 - step * (1.0 / 24.0))))
    return jnp.where(step < 0.02, small, 1.0 - jnp.exp(-step))


def columns(proj_t, first, n, into_ref):
    for j in range(into_ref.shape[0]):
        into_ref[j] = proj_t[first : first + n, j * BLOCK : (j + 1) * BLOCK]


def block_diag(values, n):
    rows, wide = values.shape[0], BLOCK * n
    spread = (
        lax.broadcasted_iota(jnp.int32, (n, wide), 1) % n == lax.broadcasted_iota(jnp.int32, (n, wide), 0)
    ).astype(f32).astype(bf16)
    keep = lax.broadcasted_iota(jnp.int32, (rows, wide), 1) // n == lax.broadcasted_iota(
        jnp.int32, (rows, wide), 0
    ) % BLOCK
    return jnp.where(keep, dot(values, spread), 0.0).astype(bf16)


def unit_of(x):
    return x * lax.rsqrt(jnp.mean(x * x, axis=-1, keepdims=True) + 1e-05)


def start_kernel(count, me_ref, x_ref, *refs):
    bottom, parts = refs[:count], refs[count:-14]
    (
        normed_ref, turned_ref, stream_ref, pre_ref, act_ref, proj_ref, w_ref, vec_ref, xproj_ref, gain_ref, marks_ref,
        wide_ref, ext_ref, cols_ref,
    ) = refs[-14:]
    rows, chans = stream_ref.shape
    taps = CONVB - CONV

    @pl.when(pl.program_id(0) == 0)
    def _():
        wide_ref[:8, :] = jnp.zeros((8, chans), f32)
        place = 1
        for part in parts:
            count, lines, _ = part.shape
            own = chans * lines // w_ref.shape[0]
            for k in range(count):
                block = me_ref[place]
                place += 1
                at = pl.ds(pl.multiple_of(block * lines, lines), lines)
                w_ref[at, :] = part[k, :, :chans]
                ext = part[k, :, chans:].astype(f32)
                ext_ref[at, :] = ext
                at = pl.ds(pl.multiple_of(block * own, own), own)
                cols_ref[at, :] = ext[:own]
                used = lax.broadcasted_iota(jnp.int32, (own, LANES), 1) < CARRY
                xproj_ref[at, :] = jnp.where(used, ext[own : 2 * own], 0.0).astype(bf16)
        for k in range(w_ref.shape[0] // LANES):
            at = slice(k * LANES, (k + 1) * LANES)
            gain_ref[:, at] = ext_ref[at, :].T[LANES - 3 : LANES - 2]
        for k in range(chans // LANES):
            at = slice(k * LANES, (k + 1) * LANES)
            vec_ref[:, at] = cols_ref[at, :].T
        marks_ref[...] = jnp.sum(ext_ref[...], axis=0, keepdims=True)

    x = x_ref[...]
    if count:
        x = jnp.concatenate([x, read_slot(bottom, pl.program_id(0) ^ me_ref[0])], axis=0)
    normed = (unit_of(x.astype(f32)) * gain_ref[...]).astype(bf16)
    normed_ref[...] = normed
    turned_ref[...] = normed.T
    stream = dot(normed, w_ref[...]).astype(bf16)
    stream_ref[...] = stream
    wide_ref[8:, :] = stream.astype(f32)
    pre = jnp.broadcast_to(vec_ref[CONVB : CONVB + 1, :], (rows, chans))
    for tap in range(taps):
        first = 8 - taps + 1 + tap
        pre = pre + vec_ref[CONV + tap : CONV + tap + 1, :] * wide_ref[first : first + rows, :]
    wide_ref[:8, :] = wide_ref[rows:, :]
    pre_ref[...] = pre
    act = (pre * sigmoid(pre)).astype(bf16)
    act_ref[...] = act
    proj_ref[...] = dot(act, xproj_ref[...]).T[:CARRY, :].astype(bf16)


def several(block):
    def blocks(i, carry):
        for k in range(STEPS):
            carry = block(STEPS * i + k, carry)
        return carry

    return blocks


def piece_kernel(me_ref, proj_ref, act_ref, vec_ref, g_ref, step_ref, carry_ref, u_ref, stepm_ref, col_ref):
    rows, c = act_ref.shape
    n = carry_ref.shape[0]

    @pl.when(pl.program_id(0) == 0)
    def _():
        carry_ref[...] = jnp.zeros_like(carry_ref)

    proj = proj_ref[...].T
    _, pre = dt_of(proj, vec_ref, INTO)
    step = softplus(pre)
    step_ref[...] = step
    u_ref[...] = step * act_ref[...].astype(f32)
    stepm_ref[...] = jnp.where(proj[:, CARRY : CARRY + 1] > 0.5, step, NEVER)
    columns(proj_ref[...], INTO, n, col_ref)
    r2 = rates_of(vec_ref, n)

    def block(i, carry):
        j = rows // BLOCK - 1 - i
        into = col_ref[j]
        for tt in reversed(range(BLOCK)):
            t = j * BLOCK + tt
            g = row_of(u_ref, t, n) * col_of(into, tt, c) + carry
            g_ref[pl.ds(pl.multiple_of(t * n, n), n), :] = g.astype(bf16)
            carry = jnp.exp2(row_of(stepm_ref, t, n) * r2) * g
        return carry

    carry_ref[...] = lax.fori_loop(0, rows // BLOCK // STEPS, several(block), carry_ref[...])


def ahead_kernel(
    first, places, per, local, me_ref, *refs,
):
    proj_ref, act_ref, normed_ref, g_ref, step_ref, vec_ref = refs[:6]
    if first:
        enter_ref, wgate_ref, outw_ref = refs[6:9]
        hp_ref, mixed_ref, gate_ref, gated_ref, leave_ref = refs[-7 - places - 5 : -7 - places]
    else:
        second_ref = refs[6]
        hp_ref, mixed_ref, gate_ref, gated_ref, leave_ref, wgate_ref, outw_ref = refs[-7 - places - 7 : -7 - places]
    branch_refs = refs[-7 - places : -7]
    carry_ref, u_ref, col_ref, diag_ref, s_ref, y_ref, out_ref = refs[-7:]
    rows, c = act_ref.shape
    n = carry_ref.shape[0]

    @pl.when(pl.program_id(0) == 0)
    def _():
        if first:
            carry_ref[...] = enter_ref[...]
            return
        carry_ref[...] = jnp.zeros_like(carry_ref)
        blocks = second_ref.shape[0]
        lines, own = wgate_ref.shape[0] // blocks, outw_ref.shape[0] // blocks
        for b in range(blocks):
            wgate_ref[b * lines : (b + 1) * lines, :] = second_ref[b, :lines, :]
            for k in range(outw_ref.shape[1] // c):
                outw_ref[b * own : (b + 1) * own, k * c : (k + 1) * c] = second_ref[
                    b, lines + k * own : lines + (k + 1) * own, :
                ]

    act = act_ref[...].astype(f32)
    u_ref[...] = step_ref[...] * act
    columns(proj_ref[...], INTO, n, col_ref)
    read = proj_ref[OUT : OUT + n, :].T
    high = read.astype(bf16)
    diag_ref[0, BLOCK:] = block_diag(high, n)
    diag_ref[1, BLOCK:] = block_diag((read - high.astype(f32)).astype(bf16), n)
    r2 = rates_of(vec_ref, n)

    def read_out(j):
        r16 = pl.ds(pl.multiple_of(j * BLOCK, BLOCK), BLOCK)
        both = dot(jnp.concatenate([diag_ref[0, r16, :], diag_ref[1, r16, :]], axis=0), s_ref[...])
        y_ref[r16, :] = both[:BLOCK] + both[BLOCK:]

    def block(j, h):
        read_out(j)
        into = col_ref[j]
        for tt in range(BLOCK):
            t = j * BLOCK + tt
            at = pl.ds(pl.multiple_of(t * n, n), n)
            hp = jnp.exp2(row_of(step_ref, t, n) * r2) * h
            h = hp + row_of(u_ref, t, n) * col_of(into, tt, c)
            hp_ref[at, :] = hp.astype(bf16)
            s_ref[tt * n : (tt + 1) * n, :] = (hp + g_ref[at, :].astype(f32)).astype(bf16)
        return h

    carry_ref[...] = lax.fori_loop(0, rows // BLOCK // STEPS, several(block), carry_ref[...])
    read_out(rows // BLOCK)
    mixed = y_ref[BLOCK:] + vec_ref[SKIP : SKIP + 1, :] * act
    mixed_ref[...] = mixed
    gate = dot(normed_ref[...], wgate_ref[...])
    gate_ref[...] = gate
    gated = (mixed * (gate * sigmoid(gate))).astype(bf16)
    gated_ref[...] = gated.T
    out_ref[...] = dot(gated, outw_ref[...]).astype(bf16)
    write_rows(branch_refs, me_ref, places, per, local, rows, out_ref)
    leave_ref[...] = carry_ref[...]


def piece_grad_kernel(
    first, places, per, local, me_ref, *refs,
):
    proj_ref, act_ref, mixed_ref, gate_ref, step_ref, vec_ref, outw_ref = refs[:7]
    db_refs = refs[7 : 7 + places]
    if first:
        enter_ref, before_ref = refs[7 + places : 9 + places]
    q_ref, dm_ref, dg_ref, db_ref, sgrad_ref, leave_ref = refs[-9:-3]
    carry_ref, stepm_ref, col_ref = refs[-3:]
    rows, c = act_ref.shape
    n = carry_ref.shape[0]

    @pl.when(pl.program_id(0) == 0)
    def _():
        if first:
            carry_ref[...] = enter_ref[...]
            sgrad_ref[...] = before_ref[...]
        else:
            carry_ref[...] = jnp.zeros_like(carry_ref)
            sgrad_ref[...] = jnp.zeros_like(sgrad_ref)

    stepm_ref[...] = jnp.where(proj_ref[CARRY : CARRY + 8, :].T[:, :1] > 0.5, step_ref[...], NEVER)
    columns(proj_ref[...], OUT, n, col_ref)
    db = read_rows(db_refs, me_ref, places, per, local, rows)
    db_ref[...] = db
    dgated = dot_t(db, outw_ref[...])
    gate = gate_ref[...]
    s = sigmoid(gate)
    dm = dgated * (gate * s)
    dm_ref[...] = dm
    dg = (dgated * mixed_ref[...] * (s * (1.0 + gate * (1.0 - s)))).astype(bf16)
    dg_ref[...] = dg
    sgrad_ref[...] += jnp.sum(dm * act_ref[...].astype(f32), axis=0, keepdims=True)
    r2 = rates_of(vec_ref, n)

    chunk = first + pl.program_id(0)

    size = UNROLL * BLOCK

    def scan(i, w):
        for k in range(UNROLL):
            j = UNROLL * i + k
            read = col_ref[j]
            for tt in range(BLOCK):
                t = j * BLOCK + tt
                q = jnp.exp2(row_of(stepm_ref, t, n) * r2) * w
                q_ref[pl.ds(pl.multiple_of(t * n, n), n), :] = q.astype(bf16)
                w = q + row_of(dm_ref, t, n) * col_of(read, tt, c)
        return w

    def fill(i, w):
        for k in range(UNROLL):
            at = pl.ds(pl.multiple_of((UNROLL * i + k) * BLOCK * n, BLOCK * n), BLOCK * n)
            q_ref[at, :] = jnp.zeros((BLOCK * n, c), bf16)
        return row_of(dm_ref, (i + 1) * size - 1, n) * col_of(col_ref[(i + 1) * UNROLL - 1], BLOCK - 1, c)

    def group(i, w):
        return lax.cond(me_ref[1 + chunk * (rows // size) + i] > 0, scan, fill, i, w)

    carry_ref[...] = lax.fori_loop(0, rows // size, group, carry_ref[...])
    leave_ref[...] = carry_ref[...]


def state_grad_kernel(
    me_ref, proj_ref, act_ref, dm_ref, g_ref, hp_ref, q_ref, step_ref, vec_ref, sgrad_ref, pieces_ref,
    dact_ref, dproj_ref, table_ref,
    carry_ref, u_ref, col_ref, diag_ref, ig_ref, rr_ref, pair_ref, own_ref, x_ref, y_ref, dp_ref,
):
    rows, c = act_ref.shape
    n = carry_ref.shape[0]
    wide = BLOCK * n

    @pl.when(pl.program_id(0) == 0)
    def _():
        carry_ref[...] = jnp.zeros_like(carry_ref)
        table_ref[...] = jnp.zeros_like(table_ref)
        table_ref[SKIP : SKIP + 1, :] = sgrad_ref[...]

    act = act_ref[...].astype(f32)
    u_ref[...] = step_ref[...] * act
    columns(proj_ref[...], OUT, n, col_ref)
    diag_ref[:rows] = block_diag(proj_ref[INTO : INTO + n, :].T.astype(bf16), n)
    r2 = rates_of(vec_ref, n)
    iota = lambda shape, axis: lax.broadcasted_iota(jnp.int32, shape, axis)
    mask = lambda v: v.astype(f32).astype(bf16)
    by_row = mask(iota((BLOCK, wide), 1) // n == iota((BLOCK, wide), 0))
    part = min(c, 2 * LANES)
    which = mask(iota((2 * part, LANES), 0) // part == iota((2 * part, LANES), 1) // n % 2)
    own_lane = iota((wide, LANES), 1) % n == iota((wide, LANES), 0) % n

    def sums(j):
        r16 = pl.ds(pl.multiple_of(j * BLOCK, BLOCK), BLOCK)
        x_ref[r16, :] = dot(diag_ref[r16, :], ig_ref[...])
        y_ref[r16, :] = dot(by_row, rr_ref[...])
        dp_ref[pl.ds(pl.multiple_of((j + 1) * BLOCK, BLOCK), BLOCK), :] = dot(by_row, own_ref[...])
        own_ref[...] = jnp.where(own_lane, dot(pair_ref[...], which), 0.0).astype(bf16)

    def block(i, both):
        m, al = both
        j = rows // BLOCK - 1 - i
        sums(j + 1)
        read = col_ref[j]
        for tt in reversed(range(BLOCK)):
            t = j * BLOCK + tt
            at = pl.ds(pl.multiple_of(t * n, n), n)
            loc = slice(tt * n, (tt + 1) * n)
            drow = row_of(dm_ref, t, n)
            mu = m + drow * col_of(read, tt, c)
            srow = row_of(step_ref, t, n)
            m = jnp.exp2(srow * r2) * mu
            low_mu = mu.astype(bf16)
            q = q_ref[at, :]
            g = g_ref[at, :]
            hp = hp_ref[at, :]
            rg = low_mu * hp + q * g
            ig = low_mu + q
            ig_ref[loc, :] = ig
            rg = rg.astype(f32)
            al = al + rg * srow
            rr_ref[loc, :] = (rg * r2).astype(bf16)
            pb = ig * row_of(u_ref, t, n).astype(bf16)
            pc = (hp + g) * drow.astype(bf16)
            sb, sc = pb[:, :part], pc[:, :part]
            for k in range(1, c // part):
                sb = sb + pb[:, k * part : (k + 1) * part]
                sc = sc + pc[:, k * part : (k + 1) * part]
            pair_ref[loc, :part] = sb
            pair_ref[loc, part:] = sc
        return m, al

    m, al = lax.fori_loop(0, rows // BLOCK, block, (carry_ref[...], table_ref[ALOG : ALOG + n, :]))
    carry_ref[...] = m
    table_ref[ALOG : ALOG + n, :] = al
    sums(0)
    dp_ref[:BLOCK, :] = dot(by_row, own_ref[...])
    xs = x_ref[:rows]
    dact_ref[...] = step_ref[...] * xs + vec_ref[SKIP : SKIP + 1, :] * dm_ref[...]
    dpre = (y_ref[:rows] * LN2 + act * xs) * slope_of(step_ref[...])
    table_ref[DTB : DTB + 1, :] += jnp.sum(dpre, axis=0, keepdims=True)
    dpre_low = dpre.astype(bf16)
    table_ref[:INTO, :] += dot(proj_ref[:INTO, :].astype(bf16), dpre_low)
    dproj_ref[...] = dp_ref[:rows].astype(bf16)
    dproj_ref[:, :INTO] = dot_t(dpre_low, vec_ref[:INTO, :].astype(bf16)).astype(bf16)

    @pl.when(pl.program_id(0) == pl.num_programs(0) - 1)
    def _():
        dproj_ref[:BLOCK, CARRY:] = pieces_ref[:, CARRY:]
        table_ref[ALOG : ALOG + n, :] *= -jnp.exp(vec_ref[ALOG : ALOG + n, :])


def end_kernel(own, local, count, paired, me_ref, *refs):
    sent = 2 if paired else 1
    dn_refs, refs = refs[-count - sent - 6 : -sent - 6], refs[: -count - sent - 6] + refs[-sent - 6 :]
    late_refs, refs = refs[-sent - 6 : -6], refs[: -sent - 6] + refs[-6:]
    parts = refs[:-17]
    (
        dact_ref, pre_ref, stream_ref, act_ref, dg_ref, vec_ref, xproj_ref, ws_ref, wg_ref, table_ref, normed_ref,
        sum_ref,
        wide_ref, xgrad_ref, cgrad_ref, turned_ref, grad_ref,
    ) = refs[-17:]
    rows, c = act_ref.shape
    taps = CONVB - CONV

    @pl.when(pl.program_id(0) == 0)
    def _():
        wide_ref[rows:, :] = jnp.zeros((8, c), f32)
        xgrad_ref[...] = jnp.zeros_like(xgrad_ref)
        cgrad_ref[...] = table_ref[...]
        grad_ref[...] = jnp.zeros_like(grad_ref)

    dproj = parts[0][...].astype(f32)
    for part in parts[1:]:
        dproj = dproj + part[...].astype(f32)
    used = lax.broadcasted_iota(jnp.int32, dproj.shape, 1) < CARRY
    dproj = jnp.where(used, dproj, 0.0).astype(bf16)
    pre = pre_ref[...]
    s = sigmoid(pre)
    dconv = (dact_ref[...] + dot_t(dproj, xproj_ref[...])) * (s * (1.0 + pre * (1.0 - s)))
    wide_ref[:rows, :] = dconv
    xgrad_ref[...] += t_dot(act_ref[...], dproj)
    cgrad_ref[CONVB : CONVB + 1, :] += jnp.sum(dconv, axis=0, keepdims=True)
    stream = stream_ref[...].astype(f32)
    dstream = jnp.zeros((rows, c), f32)
    for tap in range(taps):
        back = taps - 1 - tap
        moved = wide_ref[back : back + rows, :]
        cgrad_ref[CONV + tap : CONV + tap + 1, :] += jnp.sum(stream * moved, axis=0, keepdims=True)
        dstream = dstream + vec_ref[CONV + tap : CONV + tap + 1, :] * moved
    wide_ref[rows:, :] = dconv[:8, :]
    dstream_low = dstream.astype(bf16)
    dn = (dot_t(dstream_low, ws_ref[...]) + dot_t(dg_ref[...], wg_ref[...])).astype(bf16)
    write_slot(dn_refs, slot_of(me_ref, local, True), dn)
    grad_ref[...] += dot(normed_ref[...], dstream_low)

    @pl.when(pl.program_id(0) == pl.num_programs(0) - 1)
    def _():
        for k in range(c // LANES):
            at = slice(k * LANES, (k + 1) * LANES)
            turned_ref[at, :] = cgrad_ref[:, at].T
        sums = tree([row_sum(part[:BLOCK, :]) for part in parts])
        sums = jnp.where(lax.broadcasted_iota(jnp.int32, sums.shape, 1) < CARRY, 0.0, sums)
        sum_ref[...] = sums
        pieces = [jnp.zeros((BLOCK, LANES), f32)]
        row = lax.broadcasted_iota(jnp.int32, (BLOCK, LANES), 0)
        for k in range(3):
            term = sums.astype(bf16).astype(f32)
            pieces = [jnp.where(row == k, term, pieces[0])]
            sums = sums - term
        pieces = jnp.concatenate([pieces[0].astype(bf16)] * (c // LANES), axis=1)
        packed, lines = 2 * own * LANES // c, grad_ref.shape[0] * own // c

        def block(b):
            at = slice(b * own, (b + 1) * own)
            both = jnp.concatenate([xgrad_ref[at, :], turned_ref[at, :]], axis=0)
            small = [both[k * packed : (k + 1) * packed] for k in range(c // LANES)]
            return grad_ref[b * lines : (b + 1) * lines, :], jnp.concatenate(small, axis=1)

        if not paired:
            for b in range(c // own):
                late_refs[0][b, :lines, :], late_refs[0][b, lines:, :] = block(b)
            return
        mine_ref, theirs_ref = late_refs
        first = me_ref[me_ref.shape[0] - 1] == 0
        for z in range(c // own // 2):
            for part, at, end in zip(zip(block(2 * z), block(2 * z + 1)), (0, lines), (lines, lines + packed)):
                mine_ref[z, at:end, :] = jnp.where(first, part[0], part[1])
                theirs_ref[z, at:end, :] = jnp.where(first, part[1], part[0]).astype(bf16)
            theirs_ref[z, lines + packed :, :] = pieces


def slot_of(me_ref, local, reverse=False):
    step = pl.program_id(0)
    if reverse:
        step = pl.num_programs(0) - 1 - step
    return (step // (local // ROWS)) ^ me_ref[0]


def read_rows(refs, me_ref, places, per, local, size):
    step = pl.program_id(0)
    each = size // per
    at = pl.ds(pl.multiple_of(step // (local // size) * per, per), per)
    pieces = []
    for p in range(each):
        j = step % (local // size) * each + p
        if len(refs) == 1:
            pieces.append(refs[0][j, at, :])
            continue
        value = refs[0][at, :]
        for k in range(1, places):
            value = jnp.where(j ^ me_ref[0] == k, refs[k][at, :], value)
        pieces.append(value)
    return jnp.concatenate(pieces, axis=0)


def read_slot(refs, slot):
    value = refs[0][...]
    for k in range(1, len(refs)):
        value = jnp.where(slot == k, refs[k][...], value)
    return value


def write_rows(refs, me_ref, places, per, local, size, from_ref):
    step = pl.program_id(0)
    each = size // per
    at = pl.ds(pl.multiple_of(step // (local // size) * per, per), per)
    sub = step % (local // size)
    if len(refs) == 1:
        for p in range(each):
            refs[0][sub * each + p, at, :] = from_ref[p * per : (p + 1) * per, :]
        return
    for k, ref in enumerate(refs):
        j = k ^ me_ref[0]

        @pl.when(j // each == sub)
        def _(ref=ref, j=j):
            ref[at, :] = from_ref[pl.ds(pl.multiple_of(j % each * per, per), per), :]


def write_slot(refs, slot, value):
    if len(refs) == 1:
        refs[0][...] = value
        return
    for k, ref in enumerate(refs):

        @pl.when(slot == k)
        def _(ref=ref):
            ref[...] = value


def call(kernel, me, ins, outs, scratch, total, local, reverse=False, first=0, count=None, size=ROWS):
    steps = total // size
    per = local // size
    turn = (lambda i: steps - 1 - i) if reverse else (lambda i: i + first)
    aliases = {}
    for index, (_, kind) in enumerate(ins):
        if kind == "o":
            aliases[index + 1] = len(aliases)

    def slot_map(k):
        def index(i, me_ref):
            group = k ^ me_ref[0]
            if reverse:
                group = steps // per - 1 - group
            first, last = (per - 1, 0) if reverse else (0, per - 1)
            now = i // per
            return (jnp.where(now < group, first, jnp.where(now > group, last, turn(i) % per)), 0)

        return index

    def spec(shape, kind):
        if isinstance(kind, int):
            return pl.BlockSpec((size, shape[1]), slot_map(kind))
        if kind == "f":
            return pl.BlockSpec(shape, lambda i, me_ref: (0,) * len(shape))
        if kind == "o":
            return pl.BlockSpec(memory_space=pl.ANY)
        if kind == "c":
            return pl.BlockSpec(
                (shape[0], size), lambda i, me_ref: (0, turn(i))
            )
        if isinstance(kind, tuple):
            return pl.BlockSpec(
                (None, min(size, kind[1]), shape[2]), lambda i, me_ref: (turn(i) // per, turn(i) % per, 0)
            )
        if kind == "x":
            return pl.BlockSpec(
                (None, size, shape[2]), lambda i, me_ref: ((turn(i) // per) ^ me_ref[0], turn(i) % per, 0)
            )
        return pl.BlockSpec((shape[0] // steps, shape[1]), lambda i, me_ref: (turn(i), 0))

    return pl.pallas_call(
        kernel,
        out_shape=[jax.ShapeDtypeStruct(s, d) for s, d, _ in outs],
        grid_spec=pltpu.PrefetchScalarGridSpec(
            num_scalar_prefetch=1,
            grid=(count or steps,),
            in_specs=[spec(a.shape, k) for a, k in ins],
            out_specs=[spec(s, k) for s, _, k in outs],
            scratch_shapes=scratch,
        ),
        input_output_aliases=aliases,
        compiler_params=pltpu.CompilerParams(dimension_semantics=("arbitrary",), vmem_limit_bytes=60 << 20),
    )(me, *[a for a, _ in ins])


def slots_in(parts):
    if len(parts) == 1:
        return [(parts[0], "x")]
    return [(part, k) for k, part in enumerate(parts)]


def slots_out(seqs, rows, width):
    if seqs > 4:
        return [((seqs, rows, width), bf16, "x")]
    return [((rows, width), bf16, k) for k in range(seqs)]


def early_grad_kernel(normed_ref, gated_ref, dg_ref, *refs):
    parts, out_ref = refs[:-1], refs[-1]
    group, _, c = out_ref.shape
    lines, own = normed_ref.shape[0] // group, gated_ref.shape[0] // group
    gate = dot(normed_ref[...], dg_ref[...])
    out, first = 0.0, 0
    for part in parts:
        last = first + part.shape[0]
        out = out + dot(gated_ref[:, first:last], part[...])
        first = last
    for b in range(group):
        out_ref[b, :lines, :] = gate[b * lines : (b + 1) * lines]
        for k in range(out.shape[1] // c):
            out_ref[b, lines + k * own : lines + (k + 1) * own, :] = out[
                b * own : (b + 1) * own, k * c : (k + 1) * c
            ]


def by_blocks(kernel, batches, own, columns, whole, rows, chans):
    group = min(2 * LANES // own, batches)
    steps = batches // group

    def spec(array, cut):
        if cut:
            return pl.BlockSpec((array.shape[0] // steps, array.shape[1]), lambda i: (i, 0))
        return pl.BlockSpec(array.shape, lambda i: (0,) * array.ndim)

    return pl.pallas_call(
        kernel,
        out_shape=jax.ShapeDtypeStruct((batches, rows, chans), f32),
        grid=(steps,),
        in_specs=[spec(a, True) for a in columns] + [spec(a, False) for a in whole],
        out_specs=pl.BlockSpec((group, rows, chans), lambda i: (i, 0, 0)),
        compiler_params=pltpu.CompilerParams(dimension_semantics=("arbitrary",), vmem_limit_bytes=60 << 20),
    )(*columns, *whole)


def split_kernel(seqs, batches, own, w_ref, gain_ref, valid_ref, out_ref):
    depth, half, chans = w_ref.shape[0], w_ref.shape[1] // 2, batches * own
    count = jnp.sum(valid_ref[...].astype(f32), keepdims=True)
    high = jnp.floor(count * (1.0 / 128.0))
    iota = lambda shape, axis: lax.broadcasted_iota(jnp.int32, shape, axis)
    gain = jnp.broadcast_to(gain_ref[...].astype(f32), (depth, depth))
    gain = jnp.where(iota((depth, depth), 0) == iota((depth, depth), 1), gain, 0.0)
    gain = jnp.sum(gain, axis=1, keepdims=True)
    lane = iota((depth, LANES), 1)
    extra = jnp.where(lane == LANES - 3, gain, 0.0)
    extra = jnp.where(lane == LANES - 2, high, extra)
    extra = jnp.where(lane == LANES - 1, count - high * 128.0, extra).astype(bf16)
    for s in range(seqs):
        for k in range(2):
            pieces = [
                w_ref[:, k * half + (b * seqs + s) * own : k * half + (b * seqs + s + 1) * own].astype(f32)
                for b in range(batches)
            ]
            first = k * (chans + LANES)
            out_ref[s, :, first : first + chans] = jnp.concatenate(pieces, axis=1).astype(bf16)
        out_ref[s, :, chans : chans + LANES] = extra


def split_columns(weight, gain, valid, seqs, batches, own):
    shape = jax.ShapeDtypeStruct((seqs, weight.shape[0], 2 * batches * own + LANES), bf16)
    return pl.pallas_call(lambda *refs: split_kernel(seqs, batches, own, *refs), out_shape=shape)(weight, gain, valid)


def join_kernel(
    batches, both_ref, small_ref, w_ref, gain_ref,
    out_ref, gain_out_ref, xproj_ref, dt_ref, alog_ref, conv_ref, convb_ref, dtb_ref, skip_ref,
):
    seqs, half = both_ref.shape[0], w_ref.shape[1] // 2
    chans = half // seqs
    own = chans // batches
    for k in range(2):
        whole = [both_ref[s, :, k * chans : (k + 1) * chans].astype(f32) for s in range(seqs)]
        pieces = [whole[s][:, b * own : (b + 1) * own] for b in range(batches) for s in range(seqs)]
        out_ref[:, k * half : (k + 1) * half] = jnp.concatenate(pieces, axis=1)
    products = out_ref[...] * w_ref[...].astype(f32)
    depth = products.shape[0]
    sums = jnp.broadcast_to(jnp.sum(products, axis=1, keepdims=True), (depth, depth))
    eye = lax.broadcasted_iota(jnp.int32, (depth, depth), 0) == lax.broadcasted_iota(jnp.int32, (depth, depth), 1)
    gain_out_ref[...] = jnp.sum(jnp.where(eye, sums, 0.0), axis=0, keepdims=True) / gain_ref[...].astype(f32)
    small = small_ref[...]
    both = jnp.concatenate([small[:, k : k + LANES] for k in range(0, chans, LANES)], axis=0)
    xproj_ref[...] = both[:own, :CARRY]
    table = both[own:]
    alog_ref[...] = table[:, ALOG:CONV]
    table = jnp.concatenate([table, jnp.zeros((LANES - own, LANES), f32)], axis=0).T[:, :own]
    dt_ref[...] = table[:INTO]
    conv_ref[...] = table[CONV:CONVB]
    convb_ref[...] = table[CONVB : CONVB + 1]
    dtb_ref[...] = table[DTB : DTB + 1]
    skip_ref[...] = table[SKIP : SKIP + 1]


def join_columns(both, small, weight, gain, batches, own):
    depth = weight.shape[0]
    shapes = [weight.shape, (1, depth), (own, CARRY), (INTO, own), (own, CONV - ALOG), (CONVB - CONV, own)]
    shapes += [(1, own)] * 3
    return pl.pallas_call(
        lambda *refs: join_kernel(batches, *refs), out_shape=[jax.ShapeDtypeStruct(s, f32) for s in shapes]
    )(both, small, weight, gain)


def partner(value, axis, k):
    return lax.ppermute(value, axis, [(i, i ^ k) for i in range(lax.axis_size(axis))])


def gather_parts(value, axis):
    n = lax.axis_size(axis)
    if n > 4:
        return [lax.all_gather(value, axis)]
    return [value] + [partner(value, axis, k) for k in range(1, n)]


def gather_batch(value, after):
    n = lax.axis_size("batch")
    if n > 8:
        return [lax.all_gather(value, "batch")], [jnp.int32(k) for k in range(n)], after
    me = lax.axis_index("batch")
    chips = jnp.stack([value] + [partner(value, "batch", 2 * k) for k in range(1, n // 2)])
    other = partner(chips, "batch", 1)
    places = [me ^ (2 * k) for k in range(n // 2)] + [me ^ (2 * k + 1) for k in range(n // 2)]
    return [chips, other], places, after


def exact(total, rows):
    terms = []
    for _ in range(3):
        term = lax.reduce_precision(total, 8, 7)
        terms.append(term)
        total = total - term
    return jnp.concatenate(terms + [jnp.zeros((rows - 3, total.shape[1]), f32)], axis=0).astype(bf16)


def row_sum(rows):
    a = rows[:3].astype(f32)
    return (a[:1] + a[1:2]) + a[2:]


def tree(values):
    while len(values) > 1:
        values = [a + b for a, b in zip(values[::2], values[1::2])]
    return values[0]


def scatter_batch(mine, theirs, total):
    n = lax.axis_size("batch")
    me = lax.axis_index("batch")
    rows, c = mine.shape[1:]
    got = partner(theirs, "batch", 1)
    mine = mine + got[:, :rows].astype(f32)
    total = row_sum(exact(total, BLOCK)) + row_sum(got[0, rows:, :LANES])
    pieces = exact(jnp.tile(total, (1, c // LANES)), BLOCK)
    low = jnp.concatenate([mine.astype(bf16), jnp.broadcast_to(pieces[None], (n // 2, BLOCK, c))], axis=1)
    got = [
        partner(lax.dynamic_index_in_dim(low, (me // 2) ^ k, 0, False), "batch", 2 * k) for k in range(1, n // 2)
    ]
    result = lax.dynamic_index_in_dim(mine, me // 2, 0, False)
    for part in got:
        result = result + part[:rows].astype(f32)
    return result, tree([row_sum(exact(total, BLOCK))] + [row_sum(part[rows:, :LANES]) for part in got]), low


def scatter_parts(values, axis):
    n = lax.axis_size(axis)
    if n > 4:
        return [lax.psum_scatter(values[0].astype(f32), axis, scatter_dimension=0)]
    return [values[0]] + [partner(values[k], axis, k) for k in range(1, n)]


def share_parts(value, axis):
    n = lax.axis_size(axis)
    if n > 4:
        return [lax.psum(value.astype(f32), axis)]
    return [value] + [partner(value, axis, k) for k in range(1, n)]


def added(parts):
    total = parts[0].astype(f32)
    for part in parts[1:]:
        total = total + part.astype(f32)
    return total


def sum_everywhere(value, axes):
    for axis in axes:
        k = 1
        while k < lax.axis_size(axis):
            value = value + partner(value, axis, k)
            k *= 2
    return value


def body(
    tokens,
    teacher,
    piece_starts,
    valid_rows,
    norm_gain,
    in_weight,
    conv_weight,
    conv_bias,
    xproj_weight,
    dtproj_weight,
    dt_bias,
    a_log,
    skip_weight,
    out_weight,
):
    seqs = lax.axis_size("seq")
    batches = lax.axis_size("batch")
    _, rows, width = tokens.shape
    total = rows * seqs
    taps, own = conv_weight.shape
    chans = own * batches
    depth = in_weight.shape[0]
    rank = dtproj_weight.shape[0]
    states = a_log.shape[1]
    lines = depth * seqs
    packed = 2 * LANES * own // chans
    place = lax.axis_index("seq") if seqs <= 4 else jnp.int32(0)
    me = place.astype(jnp.int32).reshape(1)
    tok = tokens.reshape(rows, width)

    flags = jnp.concatenate([piece_starts, valid_rows], axis=0).astype(bf16)
    flags = jnp.pad(flags, ((0, 14), (0, width - rows)))
    top = rows // 2 if seqs <= 4 else rows
    bottom = gather_parts(tok[top:], "seq") if top < rows else []
    everything = lax.all_gather(jnp.concatenate([tok[:top], flags], axis=0), "seq")
    split = split_columns(in_weight, norm_gain.reshape(1, depth), valid_rows, seqs, batches, own)
    split = lax.all_to_all(split, "seq", 0, 0).reshape(lines, 2 * chans + LANES)
    vectors = jnp.concatenate(
        [
            dtproj_weight.T,
            a_log,
            conv_weight.T,
            conv_bias[:, None],
            dt_bias[:, None],
            skip_weight[:, None],
        ],
        axis=1,
    )
    vectors = jnp.pad(vectors, ((0, 0), (0, LANES - vectors.shape[1])))
    columns_x = jnp.pad(xproj_weight, ((0, 0), (0, LANES - xproj_weight.shape[1])))
    local = jnp.pad(jnp.concatenate([vectors, columns_x], axis=0), ((0, lines - 2 * own), (chans, 0)))
    second = jnp.concatenate(
        [split[:, chans + LANES :]] + [out_weight[:, k : k + chans] for k in range(0, width, chans)], axis=0
    )
    blocks, places, second = gather_batch(split[:, : chans + LANES] + local, second)
    second = lax.all_gather(second, "batch")


    tile = ((total, chans), f32, "t")
    low_tile = ((total, chans), bf16, "t")
    state = ((total * states, chans), bf16, "t")
    normed, normed_t, stream, conv_pre, act, proj, w_stream, vec, xproj, gain, marks = call(
        lambda *refs: start_kernel(len(bottom), *refs),
        jnp.concatenate([me] + [p.astype(jnp.int32).reshape(1) for p in places]),
        [(everything, ("y", top))] + [(part, "f") for part in bottom] + [(block, "f") for block in blocks],
        [
            ((total, width), bf16, "t"),
            ((width, total), bf16, "c"),
            low_tile,
            tile,
            low_tile,
            ((CARRY, total), bf16, "c"),
            ((width, chans), bf16, "f"),
            ((LANES, chans), f32, "f"),
            ((chans, LANES), bf16, "f"),
            ((1, width), f32, "f"),
            ((1, LANES), f32, "f"),
        ],
        [pltpu.VMEM((ROWS + 8, chans), f32), pltpu.VMEM((width, LANES), f32), pltpu.VMEM((chans, LANES), f32)],
        total,
        rows,
    )
    starts = everything[:, top, :rows].astype(f32).reshape(total)
    running = jnp.cumsum(starts)
    lagged = jnp.concatenate([jnp.zeros((PIECE,), f32), running[: total - PIECE]])
    carry_on = jnp.where(running - lagged > 0.5, 1.0 - starts, 0.0)
    flags = jnp.max(carry_on.reshape(-1, UNROLL * BLOCK), axis=1).astype(jnp.int32)
    teacher, proj = lax.optimization_barrier((teacher, proj))
    per = rows // seqs
    teach_v = lax.all_to_all(teacher.reshape(seqs, per, width), "seq", 0, 0).astype(f32)
    proj = added(share_parts(proj, "seq"))
    me = jnp.concatenate([me, flags])
    proj = jnp.concatenate([proj, jnp.broadcast_to(carry_on[None], (8, total))], axis=0)
    groups = (ROWS // BLOCK, states, BLOCK)
    g, step = call(
        piece_kernel,
        me,
        [(proj, "c"), (act, "t"), (vec, "f")],
        [state, tile],
        [
            pltpu.VMEM((states, chans), f32),
            pltpu.VMEM((ROWS, chans), f32),
            pltpu.VMEM((ROWS, chans), f32),
            pltpu.VMEM(groups, f32),
        ],
        total,
        rows,
        reverse=True,
    )
    halves = 2
    held = seqs // halves * per
    count = total // ROWS // halves
    places = seqs if seqs <= 4 else 1
    if seqs <= 4:
        messages = [((held, width), bf16, "f")] * seqs
    else:
        messages = [((seqs, held, width), bf16, "f")]
    by_time = [state, tile, tile, ((chans, total), bf16, "c")]
    weights = [((width, chans), bf16, "f"), ((chans, width), bf16, "f")]
    mine = lambda v: lax.dynamic_slice_in_dim(v, lax.axis_index("seq") * per, per, axis=1)
    if bottom:
        above = top // per
        tok_v = jnp.stack([lax.dynamic_slice_in_dim(b, jnp.maximum(place - above, 0) * per, per, axis=0) for b in bottom])
        tok_v = jnp.take(tok_v, jnp.arange(seqs) ^ place, axis=0)
        tops = lax.dynamic_slice_in_dim(everything, jnp.minimum(place, above - 1) * per, per, axis=1)
        tok_v = jnp.where(place < above, tops, tok_v).astype(f32)
    else:
        tok_v = mine(everything[:, :rows]).astype(f32)
    valid_v = mine(everything[:, top + 1, :rows].reshape(seqs, rows, 1)).astype(f32)
    marks, step = lax.optimization_barrier((marks, step))
    total_valid = (marks[:, LANES - 2 : LANES - 1] * 128.0 + marks[:, LANES - 1 :]) / depth
    kept = []
    branches = []
    for half in range(halves):
        out = call(
            lambda *refs, half=half: ahead_kernel(half, places, per, rows, *refs),
            me,
            [(proj, "c"), (act, "t"), (normed, "t"), (g, "t"), (step, "t"), (vec, "f")]
            + ([(enter, "f"), (w_gate, "f"), (out_w, "f")] if half else [(second, "f")])
            + [(array, "o") for array in kept],
            by_time + [((states, chans), f32, "f")] + ([] if half else weights) + messages,
            [
                pltpu.VMEM((states, chans), f32),
                pltpu.VMEM((HALF, chans), f32),
                pltpu.VMEM((HALF // BLOCK, states, BLOCK), f32),
                pltpu.VMEM((2, HALF + BLOCK, BLOCK * states), bf16),
                pltpu.VMEM((BLOCK * states, chans), bf16),
                pltpu.VMEM((HALF + BLOCK, chans), f32),
                pltpu.VMEM((HALF, width), bf16),
            ],
            total,
            rows,
            first=half * count * ROWS // HALF,
            count=count * ROWS // HALF,
            size=HALF,
        )
        kept, enter = out[:4], out[4]
        if not half:
            w_gate, out_w = out[5:7]
        branches.append(out[-places:])
    hp, mixed, gate, gated_t = kept

    factor = 2.0 * (total * batches) / total_valid
    squares = jnp.zeros((1, width), f32)
    results, d_branches = [], []
    for half in range(halves):
        at = slice(half * (seqs // halves), (half + 1) * (seqs // halves))
        flat_half = lambda v: v[at].reshape(held, v.shape[2])
        result = flat_half(tok_v) + added(scatter_parts(branches[half], "seq"))
        results.append(result.astype(bf16).reshape(seqs // halves, per, width))
        misfit = result - flat_half(teach_v)
        valid_f = flat_half(valid_v)
        squares = squares + jnp.sum(valid_f * misfit * misfit, axis=0, keepdims=True)
        d_branches.append(gather_parts((factor * valid_f * misfit).astype(bf16), "seq"))
    part = LANES - CARRY
    square_sum = squares[:, :LANES]
    for k in range(LANES, width, LANES):
        square_sum = square_sum + squares[:, k : k + LANES]
    square_sum = sum(square_sum[:, k : k + part] for k in range(0, LANES, part))
    square_sum = jnp.pad(square_sum, ((0, 0), (CARRY, 0)))

    kept = []
    for half in range(halves):
        *kept, skip_grad, enter = call(
            lambda *refs, half=half: piece_grad_kernel(half * count, places, per, rows, *refs),
            me,
            [
                (proj, "c"),
                (act, "t"),
                (mixed, "t"),
                (gate, "t"),
                (step, "t"),
                (vec, "f"),
                (out_w, "f"),
            ]
            + [(part, "f") for part in d_branches[half]]
            + ([(enter, "f"), (skip_grad, "f")] if half else [])
            + [(array, "o") for array in kept],
            [
                state,
                tile,
                low_tile,
                ((total, width), bf16, "t"),
                ((1, chans), f32, "f"),
                ((states, chans), f32, "f"),
            ],
            [pltpu.VMEM((states, chans), f32), pltpu.VMEM((ROWS, chans), f32), pltpu.VMEM(groups, f32)],
            total,
            rows,
            first=half * count,
            count=count,
        )
    q, d_mixed, d_gate, d_branch = kept
    output = lax.all_to_all(jnp.concatenate(results, axis=0), "seq", 0, 0).reshape(rows, width)
    d_result = lax.dynamic_slice_in_dim(d_branch, lax.axis_index("seq") * rows, rows, axis=0).astype(f32)
    early_sum = by_blocks(
        early_grad_kernel,
        batches,
        own,
        [normed_t, gated_t],
        [d_gate, d_branch],
        lines + own * width // chans,
        chans,
    )
    early = lax.psum_scatter(early_sum, "batch", scatter_dimension=0)
    pieces = exact(square_sum, BLOCK)
    d_act, d_proj, table = call(
        state_grad_kernel,
        me,
        [(proj, "c"), (act, "t"), (d_mixed, "t"), (g, "t"), (hp, "t"), (q, "t"), (step, "t"), (vec, "f"), (skip_grad, "f"), (pieces, "f")],
        [tile, ((total, LANES), bf16, "t"), ((LANES, chans), f32, "f")],
        [
            pltpu.VMEM((states, chans), f32),
            pltpu.VMEM((HALF, chans), f32),
            pltpu.VMEM((HALF // BLOCK, states, BLOCK), f32),
            pltpu.VMEM((HALF + BLOCK, BLOCK * states), bf16),
        ]
        + [pltpu.VMEM((BLOCK * states, chans), bf16)] * 2
        + [
            pltpu.VMEM((BLOCK * states, 2 * min(chans, 2 * LANES)), bf16),
            pltpu.VMEM((BLOCK * states, LANES), bf16),
        ]
        + [pltpu.VMEM((HALF + 2 * BLOCK, chans), f32)] * 2
        + [pltpu.VMEM((HALF + 2 * BLOCK, LANES), f32)],
        total,
        rows,
        size=HALF,
        reverse=True,
    )
    d_proj = share_parts(d_proj, "seq")
    slots = slots_out(seqs, rows, width)
    paired = batches <= 8
    size = lines + packed
    if paired:
        lates = [((batches // 2, size, chans), f32, "f"), ((batches // 2, size + BLOCK, chans), bf16, "f")]
    else:
        lates = [((batches, size, chans), f32, "f")]
    core = (lax.axis_index("batch") % 2).astype(jnp.int32).reshape(1)
    out = call(
        lambda *refs: end_kernel(own, rows, len(slots), paired, *refs),
        jnp.concatenate([me, core]),
        [(part, "t") for part in d_proj]
        + [
            (d_act, "t"),
            (conv_pre, "t"),
            (stream, "t"),
            (act, "t"),
            (d_gate, "t"),
            (vec, "f"),
            (xproj, "f"),
            (w_stream, "f"),
            (w_gate, "f"),
            (table, "f"),
            (normed_t, "c"),
        ],
        slots + lates + [((1, LANES), f32, "f")],
        [
            pltpu.VMEM((ROWS + 8, chans), f32),
            pltpu.VMEM((chans, LANES), f32),
            pltpu.VMEM((LANES, chans), f32),
            pltpu.VMEM((chans, LANES), f32),
            pltpu.VMEM((width, chans), f32),
        ],
        total,
        rows,
        reverse=True,
    )
    d_normed, seq_sum = out[: len(slots)], out[-1]
    if paired:
        late, square_sum, waiting = scatter_batch(out[-3], out[-2], seq_sum)
    else:
        waiting = out[-2]
        late = lax.psum_scatter(out[-2], "batch", scatter_dimension=0)
        square_sum = sum_everywhere(square_sum, ("batch", "seq"))
    loss = jnp.sum(square_sum) / (total_valid * width)[0, 0]
    in_out = jnp.concatenate([late[:lines], early[:lines]], axis=1).astype(bf16)
    if False:
        row = (waiting[0, :1] * 0).astype(bf16)
        d_normed = list(d_normed)
        d_normed[-1] = d_normed[-1] + jnp.tile(row, (1, width // chans))
    row = in_out[:1].astype(f32) * 0.0
    d_normed = added([jnp.tile(row, (1, width // (2 * chans)))] + scatter_parts(d_normed, "seq"))
    in_out = lax.all_to_all(in_out.reshape(seqs, depth, 2 * chans), "seq", 0, 0)
    in_out, gain_out, xproj_out, dt_out, alog_out, conv_out, convb_out, dtb_out, skip_out = join_columns(
        in_out, late[lines:], in_weight, norm_gain.reshape(1, depth), batches, own
    )
    out_out = early[lines:].reshape(-1, own, chans).transpose(1, 0, 2).reshape(own, width)
    tok_f = tok.astype(f32)
    mean_sq = jnp.mean(tok_f * tok_f, axis=-1, keepdims=True)
    root_inv = lax.rsqrt(mean_sq + 1e-05)
    own_unit = tok_f * root_inv
    scaled = d_normed * gain
    input_grad = d_result + root_inv * (scaled - own_unit * jnp.mean(scaled * own_unit, axis=-1, keepdims=True))
    return (
        output[None],
        loss,
        input_grad[None],
        gain_out[0],
        in_out,
        conv_out,
        convb_out[0],
        xproj_out,
        dt_out,
        dtb_out[0],
        alog_out,
        skip_out[0],
        out_out,
    )


def solution(mesh):
    return jax.shard_map(
        body,
        mesh=mesh,
        in_specs=(
            P("batch", "seq", None),
            P("batch", "seq", None),
            P("batch", "seq"),
            P("batch", "seq"),
            P(("batch", "seq")),
            P(("batch", "seq"), None),
            P(None, ("batch", "seq")),
            P(("batch", "seq")),
            P(("batch", "seq"), None),
            P(None, ("batch", "seq")),
            P(("batch", "seq")),
            P(("batch", "seq"), None),
            P(("batch", "seq")),
            P(("batch", "seq"), None),
        ),
        out_specs=(
            P("batch", "seq", None),
            P(),
            P("batch", "seq", None),
            P(("batch", "seq")),
            P(("batch", "seq"), None),
            P(None, ("batch", "seq")),
            P(("batch", "seq")),
            P(("batch", "seq"), None),
            P(None, ("batch", "seq")),
            P(("batch", "seq")),
            P(("batch", "seq"), None),
            P(("batch", "seq")),
            P(("batch", "seq"), None),
        ),
        check_vma=False,
    )
```
